256 devices in a mesh: gy: 32 (over y, x, core), gz: 8 (over z).
Axes of the slice: x: 4, y: 4, z: 8, core: 2. Of those that a mesh axis runs over, the one named last changes fastest.
Arguments:
- dual_flow_speeds: float32 [3, 256, 128, 1024], P(None, 'gy', 'gz'), may hold values from -6 to 6
- dual_thermal_state: float32 [256, 128, 1024], P('gy', 'gz'), may hold values from -6 to 6
- forward_flow_speeds: bfloat16 [3, 256, 128, 1024], P(None, 'gy', 'gz'), may hold values from -4 to 4
- forward_thermal_state: bfloat16 [256, 128, 1024], P('gy', 'gz'), may hold values from -6 to 6
Outputs:
- advanced_dual_motion: float32 [3, 256, 128, 1024], P(None, 'gy', 'gz')
- advanced_dual_thermal: float32 [256, 128, 1024], P('gy', 'gz')
The draws below stay inside these ranges and needn't reach their ends.
All inputs are finite; a program needn't handle non-finite values.
Results may differ from the reference program's by a relative error of at most 0.0003.
Values sent between devices are 32-bit elements; how exact they have to be, the bound alone decides.
No kernel may reach another device: no remote copies, remote signals or barrier semaphores. Data moves between devices by JAX's collectives and lax.ppermute only.
A program may use at most 128 MiB of HBM per device.

```python
import math
import jax
import jax.numpy as jnp
from jax import lax

LENGTHWISE_SIZE = 1024
SPANWISE_SIZE = 256
VERTICAL_SIZE = 128


def shard_levels(rng, shape, split, low, top_value):
    loudness = 1.0
    for dim, shards_of in split:
        draws = jax.random.uniform(jax.random.fold_in(jax.random.fold_in(rng, 6), dim), (shards_of,), jnp.float32, low / len(split), top_value / len(split))
        loudness = loudness * jnp.repeat(jnp.exp(draws), shape[dim] // shards_of).reshape((-1,) + (1,) * (len(shape) - 1 - dim))
    return loudness


def scatter_about(key, extent, deviation, most, split=(), kind=jnp.bfloat16):
    loudness = shard_levels(key, extent, split, -0.22, 0.18) if split else 1.0
    drawn = jax.random.normal(key, extent, jnp.float32) * deviation * loudness
    return jnp.minimum(jnp.maximum(drawn, -most), most).astype(kind)


def setup_inputs(seed: int = 0) -> dict:
    splits = jax.random.split(jax.random.key(seed), 5)
    return {
        "dual_flow_speeds": scatter_about(splits[0], (3, SPANWISE_SIZE, VERTICAL_SIZE, LENGTHWISE_SIZE), 1.0, 6.0, ((1, 32), (2, 8)), jnp.float32),
        "dual_thermal_state": scatter_about(splits[1], (SPANWISE_SIZE, VERTICAL_SIZE, LENGTHWISE_SIZE), 1.0, 6.0, ((0, 32), (1, 8)), jnp.float32),
        "forward_flow_speeds": scatter_about(splits[2], (3, SPANWISE_SIZE, VERTICAL_SIZE, LENGTHWISE_SIZE), 1.0, 4.0, ((1, 32), (2, 8))),
        "forward_thermal_state": scatter_about(splits[3], (SPANWISE_SIZE, VERTICAL_SIZE, LENGTHWISE_SIZE), 1.0, 6.0, ((0, 32), (1, 8))),
    }


time_step = 0.2
viscosity = 0.1
diffusivity = 0.1
buoyancy = 1.0


def tendency_contributions(haloed_quantities, motion_pieces):
    centre = haloed_quantities[:, 1:-1, 1:-1]
    slope_x = 0.5 * (jnp.roll(centre, -1, axis=3) - jnp.roll(centre, 1, axis=3))
    slope_y = 0.5 * (haloed_quantities[:, 2:, 1:-1] - haloed_quantities[:, :-2, 1:-1])
    slope_z = 0.5 * (haloed_quantities[:, 1:-1, 2:] - haloed_quantities[:, 1:-1, :-2])
    laplace = (jnp.roll(centre[:4], -1, axis=3) + jnp.roll(centre[:4], 1, axis=3)) + (haloed_quantities[:4, 2:, 1:-1] + haloed_quantities[:4, :-2, 1:-1]) + (haloed_quantities[:4, 1:-1, 2:] + haloed_quantities[:4, 1:-1, :-2]) - 6.0 * centre[:4]
    advect = motion_pieces[0] * slope_x[:4] + motion_pieces[1] * slope_y[:4] + motion_pieces[2] * slope_z[:4]
    heat_slope = jnp.stack([slope_x[4], slope_y[4], slope_z[4]])
    unprojected_motion = centre[:3] + time_step * (advect[:3] + viscosity * laplace[:3] + centre[3] * heat_slope)
    thermal_following = centre[3] + time_step * (advect[3] + diffusivity * laplace[3] + buoyancy * centre[2])
    return unprojected_motion, thermal_following


def hartley(field, axis):
    transformed = jnp.fft.fft(field, axis=axis)
    return transformed.real - transformed.imag


def cosine_table(length):
    indices = jnp.arange(length, dtype=jnp.int32)
    phases = (indices[None, :] * (2 * indices[:, None] + 1)) % (4 * length)
    return jnp.cos(phases.astype(jnp.float32) * (math.pi / (2 * length)))


def cosine_inverse(length):
    indices = jnp.arange(length, dtype=jnp.int32)
    weights = jnp.where(indices == 0, 1.0, 2.0).astype(jnp.float32)
    return cosine_table(length).T * weights[:, None] / length


def eigen_periodic(waves, length):
    return 2.0 - 2.0 * jnp.cos(waves.astype(jnp.float32) * (2.0 * math.pi / length))


def eigen_wall(waves, length):
    return 2.0 - 2.0 * jnp.cos(waves.astype(jnp.float32) * (math.pi / length))


def reference(dual_flow_speeds, dual_thermal_state, forward_flow_speeds, forward_thermal_state):
    quantity_bundle = jnp.concatenate([dual_flow_speeds, dual_thermal_state[None], forward_thermal_state[None].astype(jnp.float32)], 0)
    haloed_quantities = jnp.concatenate([quantity_bundle[:, -1:], quantity_bundle, quantity_bundle[:, :1]], axis=1)
    haloed_quantities = jnp.pad(haloed_quantities, ((0, 0), (0, 0), (1, 1), (0, 0)))
    motion_pieces = forward_flow_speeds.astype(jnp.float32)
    block_rows = math.gcd(SPANWISE_SIZE, 64)
    parts_pre = []
    thermal_pieces = []
    for start in range(0, SPANWISE_SIZE, block_rows):
        unprojected_motion, thermal_following = tendency_contributions(haloed_quantities[:, start:start + block_rows + 2], motion_pieces[:, start:start + block_rows])
        parts_pre.append(unprojected_motion)
        thermal_pieces.append(thermal_following)
    unprojected_motion = jnp.concatenate(parts_pre, 1)
    advanced_dual_thermal = jnp.concatenate(thermal_pieces, 0)
    next_z = jnp.concatenate([unprojected_motion[2][:, 1:], jnp.zeros((SPANWISE_SIZE, 1, LENGTHWISE_SIZE), jnp.float32)], 1)
    source = (jnp.roll(unprojected_motion[0], -1, axis=2) - unprojected_motion[0]) + (jnp.roll(unprojected_motion[1], -1, axis=0) - unprojected_motion[1]) + (next_z - unprojected_motion[2])
    spectral = hartley(hartley(source, 2), 0)
    spectral = jnp.einsum('yzx,zk->ykx', spectral, cosine_table(VERTICAL_SIZE), precision=lax.Precision.HIGHEST)
    eigen_sum = eigen_periodic(jnp.arange(LENGTHWISE_SIZE, dtype=jnp.int32), LENGTHWISE_SIZE)[None, None, :] + eigen_periodic(jnp.arange(SPANWISE_SIZE, dtype=jnp.int32), SPANWISE_SIZE)[:, None, None] + eigen_wall(jnp.arange(VERTICAL_SIZE, dtype=jnp.int32), VERTICAL_SIZE)[None, :, None]
    positive = eigen_sum > 0
    solved = jnp.where(positive, -spectral / jnp.where(positive, eigen_sum, 1.0), 0.0)
    pressure = jnp.einsum('ykx,kz->yzx', solved, cosine_inverse(VERTICAL_SIZE), precision=lax.Precision.HIGHEST)
    pressure = hartley(pressure, 0) / SPANWISE_SIZE
    pressure = hartley(pressure, 2) / LENGTHWISE_SIZE
    grad_x = pressure - jnp.roll(pressure, 1, axis=2)
    grad_y = pressure - jnp.roll(pressure, 1, axis=0)
    below = jnp.concatenate([jnp.zeros((SPANWISE_SIZE, 1, LENGTHWISE_SIZE), jnp.float32), pressure[:, :-1]], 1)
    layer_index = jnp.arange(VERTICAL_SIZE, dtype=jnp.int32)
    grad_z = jnp.where((layer_index == 0)[None, :, None], 0.0, pressure - below)
    advanced_dual_motion = unprojected_motion - jnp.stack([grad_x, grad_y, grad_z])
    return advanced_dual_motion, advanced_dual_thermal
```

```python
import functools

import jax
import jax.numpy as jnp
import ml_dtypes
import numpy as np
from jax import lax
from jax.experimental import pallas as pl
from jax.experimental.pallas import tpu as pltpu
from jax.sharding import PartitionSpec as P

F32 = jnp.float32
BF16 = jnp.bfloat16
ROWS = 8
LAYERS = 16
WAVES = 32
QUADS = LAYERS // 4
PIECE = 8 * (QUADS + 1)
VMEM = pl.BlockSpec(memory_space=pltpu.VMEM)
SMEM = pl.BlockSpec(memory_space=pltpu.SMEM)


def two_parts(table):
    head = table.astype(ml_dtypes.bfloat16)
    return head, (table - head.astype(np.float64)).astype(ml_dtypes.bfloat16)


def cas(phases, length):
    angles = (phases % length) * (2.0 * np.pi / length)
    return np.cos(angles) + np.sin(angles)


@functools.lru_cache(None)
def tables(size_x, size_y):
    half = np.arange(size_x // 2)
    even = two_parts(cas(half[:, None] * half[None, :], size_x // 2))
    odd = two_parts(cas(half[:, None] * (2 * half[None, :] + 1), size_x))
    full = np.arange(size_y)
    span = two_parts(cas(full[:, None] * full[None, :], size_y))
    waves = np.concatenate([2 * half, 2 * half + 1])
    line_x = 4.0 * np.sin(np.pi * waves / size_x) ** 2
    line_x = np.tile(line_x.reshape(-1, WAVES), (1, 128 // WAVES)).astype(np.float32)
    row = np.arange(size_y // 4)[:, None]
    lane = np.arange(128)[None, :]
    wave_y = 32 * (row // 8) + 8 * (lane // WAVES) + row % 8
    line_y = (4.0 * np.sin(np.pi * wave_y / size_y) ** 2).astype(np.float32)
    return even, odd, span, line_x, line_y


def split(values):
    head = values.astype(BF16)
    return head, (values - head.astype(F32)).astype(BF16)


def lane_group(shape):
    return lax.broadcasted_iota(jnp.int32, shape, len(shape) - 1) // WAVES


def swap_groups(a):
    axis = a[0].ndim - 1
    group = lane_group(a[0].shape)
    low = group < 2
    even = group % 2 == 0
    b0 = jnp.where(low, a[0], pltpu.roll(a[2], 64, axis))
    b2 = jnp.where(low, pltpu.roll(a[0], 64, axis), a[2])
    b1 = jnp.where(low, a[1], pltpu.roll(a[3], 64, axis))
    b3 = jnp.where(low, pltpu.roll(a[1], 64, axis), a[3])
    return (
        jnp.where(even, b0, pltpu.roll(b1, 32, axis)),
        jnp.where(even, pltpu.roll(b0, 96, axis), b1),
        jnp.where(even, b2, pltpu.roll(b3, 32, axis)),
        jnp.where(even, pltpu.roll(b2, 96, axis), b3),
    )


def dot(a, b):
    return jnp.dot(a, b, preferred_element_type=F32)


def dot_nt(a, b):
    return lax.dot_general(a, b, (((1,), (1,)), ((), ())), preferred_element_type=F32)


def product(values, head, tail, how):
    a, b = split(values)
    return how(a, head) + (how(b, head) + how(a, tail))


def keep(ref, start, values):
    for b in range(ref.shape[0]):
        ref[b, pl.ds(start, values.shape[0]), :] = values[:, b * 128:(b + 1) * 128]


def kept(ref, start, count):
    return jnp.concatenate([ref[b, pl.ds(start, count), :] for b in range(ref.shape[0])], 1)


def stencil_kernel(
    motion, thermal, flow, base, y_low, y_high, z_low, z_high, even_h, even_t, odd_h, odd_t,
    provisional, thermal_out, message, source, lines, row_p, layer_p,
):
    size_x = motion.shape[-1]
    row = lax.broadcasted_iota(jnp.int32, (LAYERS, size_x), 0)
    top = row == LAYERS - 1
    bottom = row == 0

    def field(c, y):
        if c < 3:
            return motion[c, y]
        if c == 3:
            return thermal[y]
        return base[y].astype(F32)

    def neighbours(c, y):
        centre = field(c, y)
        y_plus = field(c, y + 1) if y < ROWS - 1 else y_high[c]
        y_minus = field(c, y - 1) if y > 0 else y_low[c]
        z_plus = jnp.where(top, z_high[c, y:y + 1, :], pltpu.roll(centre, LAYERS - 1, 0))
        z_minus = jnp.where(bottom, z_low[c, y:y + 1, :], pltpu.roll(centre, 1, 0))
        x_plus = pltpu.roll(centre, size_x - 1, 1)
        x_minus = pltpu.roll(centre, 1, 1)
        return centre, x_plus, x_minus, y_plus, y_minus, z_plus, z_minus

    carried = None
    for y in range(ROWS):
        weights = []
        for c in range(3):
            speed = flow[c, y].astype(F32) * 0.1
            weights += [0.02 + speed, 0.02 - speed]
        _, hx, gx, hy, gy, hz, gz = neighbours(4, y)
        slopes = (hx - gx, hy - gy, hz - gz)
        heat = thermal[y] * 0.1
        moved = []
        for c in range(4):
            parts = neighbours(c, y)
            value = parts[0] * 0.88
            for weight, part in zip(weights, parts[1:]):
                value = value + weight * part
            if c < 3:
                value = value + heat * slopes[c]
                provisional[c, y] = value
            else:
                thermal_out[y] = value + 0.2 * motion[2, y]
            moved.append(value)
        p0, p1, p2 = moved[:3]
        if y == 0:
            keep(row_p, 0, p1)
        else:
            keep(source, (y - 1) * LAYERS, carried + p1)
        keep(layer_p, y, p2[0:1, :])
        above = jnp.where(top, 0.0, pltpu.roll(p2, LAYERS - 1, 0))
        carried = (pltpu.roll(p0, size_x - 1, 1) - p0) - p1 + (above - p2)
    keep(source, (ROWS - 1) * LAYERS, carried)

    for b in range(size_x // 128):
        lanes = pl.ds(b * 128, 128)
        for j in range(4):
            for q in range(QUADS):
                lines[pl.ds(j * PIECE + q * 8, 8), lanes] = source[b, pl.ds(4 * q + j, ROWS, stride=LAYERS), :]
            lines[pl.ds(j * PIECE + 32, 4), lanes] = row_p[b, pl.ds(j, 4, stride=4), :]
            lines[pl.ds(j * PIECE + 36, 2), lanes] = layer_p[b, pl.ds(j, 2, stride=4), :]
            lines[pl.ds(j * PIECE + 38, 2), lanes] = jnp.zeros((2, 128), F32)
    near = lines[:, : size_x // 2]
    far = lines[:, size_x // 2:]
    evens = product(near + far, even_h[...], even_t[...], dot)
    odds = product(near - far, odd_h[...], odd_t[...], dot)
    for block in range(size_x // 128):
        part, at = (evens, block) if block < size_x // 256 else (odds, block - size_x // 256)
        a = [part[j * PIECE:(j + 1) * PIECE, at * 128:(at + 1) * 128] for j in range(4)]
        for i, piece in enumerate(swap_groups(a)):
            message[4 * block + i] = piece


def mode_constants(place, line_x, line_y):
    a = line_x[pl.ds(place[0], 1), :] + line_y[...]
    sinh = jnp.sqrt(a * (1.0 + 0.25 * a))
    lam = 1.0 / (1.0 + 0.5 * a + sinh)
    return a, sinh, lam


def wall_factors(lam, slab, slabs):
    square = lam * lam
    powers = [jnp.ones_like(lam), square]
    for m in range(2, LAYERS + 1):
        powers.append(powers[m // 2] * powers[m - m // 2])
    step = powers[LAYERS]

    def raised(count):
        value = lam
        factor = step
        for bit in range((slabs - 1).bit_length()):
            value = jnp.where((count // (1 << bit)) % 2 == 1, value * factor, value)
            factor = factor * factor
        return value

    low = raised(slab)
    high = raised(slabs - 1 - slab)
    below = low * (1.0 / square)
    floor = [1.0 + jnp.where(slab == 0, lam, below)] + [1.0 + low * powers[l] for l in range(LAYERS)]
    ceiling = [1.0 + high * powers[LAYERS - 1 - l] for l in range(-1, LAYERS)]
    return floor, ceiling, powers


def down_kernel(place, received, span_h, span_t, line_x, line_y, spectral, handed):
    sources = received.shape[0]
    size_y = sources * ROWS
    slabs = handed.shape[0]
    slab = place[1]
    row = lax.broadcasted_iota(jnp.int32, (sources, 8, 128), 1)
    group = lane_group((sources, 8, 128))
    extra = received[:, 8 * QUADS:, :]
    onward = jnp.concatenate([extra[1:], extra[:1]], 0)
    columns = []
    for q in range(QUADS):
        more = jnp.broadcast_to(onward[:, q:q + 1, :], (sources, 8, 128))
        values = received[:, 8 * q:8 * q + 8, :] + jnp.where(row == ROWS - 1, more, 0.0)
        columns.append(values.reshape(size_y, 128))
    first = jnp.broadcast_to(extra[:, 4:5, :], (sources, 8, 128))
    second = jnp.broadcast_to(extra[:, 5:6, :], (sources, 8, 128))
    layer = jnp.where(row < 4, first, second)
    layer = jnp.where((row % 4 == group) & (slab > 0), layer, 0.0)
    columns.append(layer.reshape(size_y, 128))
    stacked = jnp.concatenate(columns, 1)
    head, tail = split(stacked)
    waves = dot(span_h[...], head) + (dot(span_h[...], tail) + dot(span_t[...], head))

    last = waves[:, 128 * QUADS:]
    last = last + pltpu.roll(last, 64, 1)
    last = (last + pltpu.roll(last, 32, 1)).reshape(size_y // 32, 4, 8, 128)
    modes = size_y // 4
    mode_group = lane_group((modes, 128))
    pick = [last[:, i].reshape(modes, 128) for i in range(4)]
    layers = [
        jnp.where(
            mode_group < 2,
            jnp.where(mode_group == 0, pick[0], pick[1]),
            jnp.where(mode_group == 2, pick[2], pick[3]),
        )
    ]
    for q in range(QUADS):
        block = waves[:, 128 * q:128 * (q + 1)].reshape(size_y // 32, 4, 8, 128)
        layers += swap_groups([block[:, i].reshape(modes, 128) for i in range(4)])
    _, _, lam = mode_constants(place, line_x, line_y)
    floor, ceiling, _ = wall_factors(lam, slab, slabs)
    upward = jnp.zeros_like(lam)
    downward = jnp.zeros_like(lam)
    for l in range(LAYERS + 1):
        spectral[l] = layers[l]
        upward = lam * upward + floor[l] * layers[l]
        m = LAYERS - l
        downward = lam * downward + ceiling[m] * layers[m]
    for d in range(slabs):
        handed[d] = jnp.where(d > slab, upward, downward)


def up_kernel(place, spectral, handed, span_h, span_t, line_x, line_y, message):
    size_y = span_h.shape[0]
    sources = size_y // ROWS
    slabs = handed.shape[0]
    size_x = line_x.shape[0] * WAVES
    size_z = slabs * LAYERS
    slab = place[1]
    a, sinh, lam = mode_constants(place, line_x, line_y)
    floor, ceiling, powers = wall_factors(lam, slab, slabs)
    scale = 1.0 / (size_x * size_y)
    whole = powers[LAYERS]
    reach = powers[LAYERS // 2]
    for _ in range((slabs - 1).bit_length()):
        whole = whole * whole
    zero = a == 0.0
    weight = (-scale) / jnp.where(zero, 1.0, 2.0 * sinh * (1.0 - whole))
    weight = jnp.where(zero, 0.0, weight)
    upward = jnp.zeros_like(lam)
    downward = jnp.zeros_like(lam)
    for d in range(slabs - 1):
        upward = jnp.where(d < slab, reach * upward + handed[d], upward)
        e = slabs - 1 - d
        downward = jnp.where(e > slab, reach * downward + handed[e], downward)
    below = []
    for l in range(LAYERS + 1):
        upward = (lam * upward if l else upward) + floor[l] * spectral[l]
        below.append(upward)
    pressure = [None] * (LAYERS + 1)
    for l in reversed(range(LAYERS + 1)):
        pressure[l] = weight * (ceiling[l] * below[l] + floor[l] * downward)
        if l == LAYERS:
            mean = (0.5 / size_z) * (below[l][:8] + downward[:8])
        downward = lam * (downward + ceiling[l] * spectral[l])
    modes = size_y // 4
    flat = jnp.zeros((8, 128), F32)
    first_zero = zero[:8]
    for l in range(LAYERS + 1):
        if l:
            count = (slab * LAYERS + (l - 1)).astype(F32)
            flat = flat + (0.5 * below[l - 1][:8] - count * mean)
        pressure[l] = jnp.concatenate(
            [jnp.where(first_zero, flat * scale, pressure[l][:8]), pressure[l][8:]], 0
        )

    columns = []
    tall = (size_y // 32, 1, 8, 128)
    for q in range(QUADS):
        block = swap_groups(pressure[1 + 4 * q:5 + 4 * q])
        columns.append(jnp.concatenate([b.reshape(tall) for b in block], 1).reshape(size_y, 128))
    mode_group = lane_group((modes, 128))
    spread = []
    for i in range(4):
        part = jnp.where(mode_group == i, pressure[0], 0.0)
        part = part + pltpu.roll(part, 64, 1)
        spread.append((part + pltpu.roll(part, 32, 1)).reshape(tall))
    columns.append(jnp.concatenate(spread, 1).reshape(size_y, 128))
    stacked = jnp.concatenate(columns, 1)
    head, tail = split(stacked)
    values = dot(span_h[...], head) + (dot(span_h[...], tail) + dot(span_t[...], head))

    row = lax.broadcasted_iota(jnp.int32, (sources, 8, 128), 1)
    group = lane_group((sources, 8, 128))
    extra = jnp.zeros((sources, 8, 128), F32)
    for q in range(QUADS):
        block = values[:, 128 * q:128 * (q + 1)].reshape(sources, 8, 128)
        message[:, 8 * q:8 * q + 8, :] = block
        edge = jnp.concatenate([block[-1:], block[:-1]], 0)[:, ROWS - 1:ROWS, :]
        extra = jnp.where(row == q, jnp.broadcast_to(edge, extra.shape), extra)
    layer = values[:, 128 * QUADS:].reshape(sources, 8, 128)
    layer = jnp.where(row % 4 == group, layer, 0.0)
    layer = layer + pltpu.roll(layer, 7, 1)
    layer = layer + pltpu.roll(layer, 6, 1)
    extra = jnp.where(row == 4, jnp.broadcast_to(layer[:, 0:1, :], extra.shape), extra)
    extra = jnp.where(row == 5, jnp.broadcast_to(layer[:, 4:5, :], extra.shape), extra)
    message[:, 8 * QUADS:, :] = extra


def gradient_kernel(
    place, received, even_h, even_t, odd_h, odd_t, provisional, motion, lines, pressure, row_p, layer_p
):
    size_x = provisional.shape[-1]
    for block in range(size_x // 128):
        for j, piece in enumerate(swap_groups([received[4 * block + i] for i in range(4)])):
            lines[j * PIECE:(j + 1) * PIECE, block * 128:(block + 1) * 128] = piece
    evens = product(lines[:, : size_x // 2], even_h[...], even_t[...], dot)
    odds = product(lines[:, size_x // 2:], odd_h[...], odd_t[...], dot_nt)
    lines[:, : size_x // 2] = evens + odds
    lines[:, size_x // 2:] = evens - odds
    for b in range(size_x // 128):
        lanes = pl.ds(b * 128, 128)
        for j in range(4):
            for q in range(QUADS):
                pressure[b, pl.ds(4 * q + j, ROWS, stride=LAYERS), :] = lines[pl.ds(j * PIECE + q * 8, 8), lanes]
            row_p[b, pl.ds(j, 4, stride=4), :] = lines[pl.ds(j * PIECE + 32, 4), lanes]
            layer_p[b, pl.ds(j, 2, stride=4), :] = lines[pl.ds(j * PIECE + 36, 2), lanes]
    bottom = lax.broadcasted_iota(jnp.int32, (LAYERS, size_x), 0) == 0
    for y in range(ROWS):
        p = kept(pressure, y * LAYERS, LAYERS)
        before = kept(row_p, 0, LAYERS) if y == 0 else kept(pressure, (y - 1) * LAYERS, LAYERS)
        below = jnp.where(bottom, kept(layer_p, y, 1), pltpu.roll(p, 1, 0))
        slope_z = jnp.where(bottom & (place[1] == 0), 0.0, p - below)
        motion[0, y] = provisional[0, y] - (p - pltpu.roll(p, 1, 1))
        motion[1, y] = provisional[1, y] - (p - before)
        motion[2, y] = provisional[2, y] - slope_z


def shifted(value, axis, by, periodic):
    size = lax.axis_size(axis)
    pairs = [(i, (i + by) % size) for i in range(size) if periodic or 0 <= i + by < size]
    return lax.ppermute(value, axis, pairs)


def exchanged(pieces, axis):
    return lax.all_to_all(pieces, axis, split_axis=0, concat_axis=0, tiled=True)


def shape_of(*shape):
    return jax.ShapeDtypeStruct(shape, F32)


def on_device(dual_motion, dual_thermal, flow, base):
    size_x = dual_thermal.shape[-1]
    groups_y = lax.axis_size("gy")
    groups_z = lax.axis_size("gz")
    even, odd, span, line_x, line_y = tables(size_x, ROWS * groups_y)
    even_h, even_t = map(jnp.asarray, even)
    odd_h, odd_t = map(jnp.asarray, odd)
    span_h, span_t = map(jnp.asarray, span)
    line_x, line_y = jnp.asarray(line_x), jnp.asarray(line_y)
    modes = line_y.shape[0]
    place = jnp.stack([lax.axis_index("gy"), lax.axis_index("gz")]).astype(jnp.int32)
    params = pltpu.CompilerParams(vmem_limit_bytes=48 << 20)

    def side(index, dim):
        def cut(a, at):
            return lax.index_in_dim(a, index, at, keepdims=False)

        return jnp.concatenate(
            [
                cut(dual_motion, dim + 1),
                cut(dual_thermal, dim)[None],
                cut(base, dim)[None].astype(F32),
            ],
            0,
        )

    y_low = shifted(side(ROWS - 1, 0), "gy", 1, True)
    y_high = shifted(side(0, 0), "gy", -1, True)
    z_low = shifted(side(LAYERS - 1, 1), "gz", 1, False)
    z_high = shifted(side(0, 1), "gz", -1, False)

    provisional, thermal_out, message = pl.pallas_call(
        stencil_kernel,
        out_shape=(
            shape_of(3, ROWS, LAYERS, size_x),
            shape_of(ROWS, LAYERS, size_x),
            shape_of(groups_y, PIECE, 128),
        ),
        in_specs=[VMEM] * 12,
        out_specs=(VMEM,) * 3,
        scratch_shapes=[
            pltpu.VMEM((size_x // 128, ROWS * LAYERS, 128), F32),
            pltpu.VMEM((4 * PIECE, size_x), F32),
            pltpu.VMEM((size_x // 128, LAYERS, 128), F32),
            pltpu.VMEM((size_x // 128, ROWS, 128), F32),
        ],
        compiler_params=params,
        name="stencil",
    )(
        dual_motion, dual_thermal, flow, base, y_low, y_high, z_low, z_high,
        even_h, even_t, odd_h, odd_t,
    )
    received = exchanged(message, "gy")
    spectral, handed = pl.pallas_call(
        down_kernel,
        out_shape=(shape_of(LAYERS + 1, modes, 128), shape_of(groups_z, modes, 128)),
        in_specs=[SMEM] + [VMEM] * 5,
        out_specs=(VMEM,) * 2,
        compiler_params=params,
        name="down",
    )(place, received, span_h, span_t, line_x, line_y)
    handed = exchanged(handed, "gz")
    message = pl.pallas_call(
        up_kernel,
        out_shape=shape_of(groups_y, PIECE, 128),
        in_specs=[SMEM] + [VMEM] * 6,
        out_specs=VMEM,
        compiler_params=params,
        name="up",
    )(place, spectral, handed, span_h, span_t, line_x, line_y)
    received = exchanged(message, "gy")
    motion = pl.pallas_call(
        gradient_kernel,
        out_shape=shape_of(3, ROWS, LAYERS, size_x),
        in_specs=[SMEM] + [VMEM] * 6,
        out_specs=VMEM,
        scratch_shapes=[
            pltpu.VMEM((4 * PIECE, size_x), F32),
            pltpu.VMEM((size_x // 128, ROWS * LAYERS, 128), F32),
            pltpu.VMEM((size_x // 128, LAYERS, 128), F32),
            pltpu.VMEM((size_x // 128, ROWS, 128), F32),
        ],
        compiler_params=params,
        name="gradient",
    )(place, received, even_h, even_t, odd_h, odd_t, provisional)
    return motion, thermal_out


def solution(mesh):
    split_y = P(None, "gy", "gz", None)
    split_flat = P("gy", "gz", None)
    return jax.shard_map(
        on_device,
        mesh=mesh,
        in_specs=(split_y, split_flat, split_y, split_flat),
        out_specs=(split_y, split_flat),
        check_vma=False,
    )
```

```python
import functools

import jax
import jax.numpy as jnp
import ml_dtypes
import numpy as np
from jax import lax
from jax.experimental import pallas as pl
from jax.experimental.pallas import tpu as pltpu
from jax.sharding import PartitionSpec as P

F32 = jnp.float32
BF16 = jnp.bfloat16
ROWS = 8
LAYERS = 16
WAVES = 32
QUADS = LAYERS // 4
PIECE = 8 * (QUADS + 1)
VMEM = pl.BlockSpec(memory_space=pltpu.VMEM)
SMEM = pl.BlockSpec(memory_space=pltpu.SMEM)


def two_parts(table):
    head = table.astype(ml_dtypes.bfloat16)
    return head, (table - head.astype(np.float64)).astype(ml_dtypes.bfloat16)


def cas(phases, length):
    angles = (phases % length) * (2.0 * np.pi / length)
    return np.cos(angles) + np.sin(angles)


@functools.lru_cache(None)
def tables(size_x, size_y):
    half = np.arange(size_x // 2)
    even = two_parts(cas(half[:, None] * half[None, :], size_x // 2))
    odd = two_parts(cas(half[:, None] * (2 * half[None, :] + 1), size_x))
    full = np.arange(size_y)
    span = two_parts(cas(full[:, None] * full[None, :], size_y))
    waves = np.concatenate([2 * half, 2 * half + 1])
    line_x = 4.0 * np.sin(np.pi * waves / size_x) ** 2
    line_x = np.tile(line_x.reshape(-1, WAVES), (1, 128 // WAVES)).astype(np.float32)
    row = np.arange(size_y // 4)[:, None]
    lane = np.arange(128)[None, :]
    wave_y = 32 * (row // 8) + 8 * (lane // WAVES) + row % 8
    line_y = (4.0 * np.sin(np.pi * wave_y / size_y) ** 2).astype(np.float32)
    return even, odd, span, line_x, line_y


def split(values):
    head = values.astype(BF16)
    return head, (values - head.astype(F32)).astype(BF16)


def lane_group(shape):
    return lax.broadcasted_iota(jnp.int32, shape, len(shape) - 1) // WAVES


def swap_groups(a):
    axis = a[0].ndim - 1
    group = lane_group(a[0].shape)
    low = group < 2
    even = group % 2 == 0
    b0 = jnp.where(low, a[0], pltpu.roll(a[2], 64, axis))
    b2 = jnp.where(low, pltpu.roll(a[0], 64, axis), a[2])
    b1 = jnp.where(low, a[1], pltpu.roll(a[3], 64, axis))
    b3 = jnp.where(low, pltpu.roll(a[1], 64, axis), a[3])
    return (
        jnp.where(even, b0, pltpu.roll(b1, 32, axis)),
        jnp.where(even, pltpu.roll(b0, 96, axis), b1),
        jnp.where(even, b2, pltpu.roll(b3, 32, axis)),
        jnp.where(even, pltpu.roll(b2, 96, axis), b3),
    )


def dot(a, b):
    return jnp.dot(a, b, preferred_element_type=F32)


def dot_nt(a, b):
    return lax.dot_general(a, b, (((1,), (1,)), ((), ())), preferred_element_type=F32)


def product(values, head, tail, how):
    a, b = split(values)
    return how(a, head) + (how(b, head) + how(a, tail))


def keep(ref, start, values):
    for b in range(ref.shape[0]):
        ref[b, pl.ds(start, values.shape[0]), :] = values[:, b * 128:(b + 1) * 128]


def kept(ref, start, count):
    return jnp.concatenate([ref[b, pl.ds(start, count), :] for b in range(ref.shape[0])], 1)


def sides_kernel(motion, thermal, base, y_first, y_last, z_first, z_last):
    for out, y in ((y_first, 0), (y_last, ROWS - 1)):
        for c in range(3):
            out[c] = motion[c, y]
        out[3] = thermal[y]
        out[4] = base[y].astype(F32)
    for y in range(ROWS):
        warm = base[y].astype(F32)
        for out, z in ((z_first, 0), (z_last, LAYERS - 1)):
            for c in range(3):
                out[c, y:y + 1, :] = motion[c, y, z:z + 1, :]
            out[3, y:y + 1, :] = thermal[y, z:z + 1, :]
            out[4, y:y + 1, :] = warm[z:z + 1, :]


def inner_kernel(motion, thermal, flow, base, moved, warmed):
    size_x = motion.shape[-1]
    row = lax.broadcasted_iota(jnp.int32, (LAYERS, size_x), 0)
    top = row == LAYERS - 1
    bottom = row == 0

    def field(c, y):
        if c < 3:
            return motion[c, y]
        if c == 3:
            return thermal[y]
        return base[y].astype(F32)

    def neighbours(c, y):
        centre = field(c, y)
        y_plus = field(c, y + 1) if y < ROWS - 1 else None
        y_minus = field(c, y - 1) if y > 0 else None
        z_plus = jnp.where(top, 0.0, pltpu.roll(centre, LAYERS - 1, 0))
        z_minus = jnp.where(bottom, 0.0, pltpu.roll(centre, 1, 0))
        x_plus = pltpu.roll(centre, size_x - 1, 1)
        x_minus = pltpu.roll(centre, 1, 1)
        return centre, x_plus, x_minus, y_plus, y_minus, z_plus, z_minus

    for y in range(ROWS):
        weights = []
        for c in range(3):
            speed = flow[c, y].astype(F32) * 0.1
            weights += [0.02 + speed, 0.02 - speed]
        _, hx, gx, hy, gy, hz, gz = neighbours(4, y)
        slope_y = -gy if hy is None else hy if gy is None else hy - gy
        slopes = (hx - gx, slope_y, hz - gz)
        heat = thermal[y] * 0.1
        for c in range(4):
            parts = neighbours(c, y)
            value = parts[0] * 0.88
            for weight, part in zip(weights, parts[1:]):
                if part is not None:
                    value = value + weight * part
            if c < 3:
                moved[c, y] = value + heat * slopes[c]
            else:
                warmed[y] = value + 0.2 * motion[2, y]


def edge_weights(flow, y):
    size_x = flow.shape[-1]
    row = lax.broadcasted_iota(jnp.int32, (8, size_x), 0)
    speed = flow[2, y].astype(F32) * 0.1
    first = jnp.where(row == 0, 0.02 - speed[:8], 0.0)
    last = jnp.where(row == 7, 0.02 + speed[LAYERS - 8:], 0.0)
    return row, first, last


def warm_kernel(warmed, flow, y_low, y_high, z_low, z_high, thermal_out):
    for y in range(ROWS):
        value = warmed[y]
        if y == 0:
            value = value + (0.02 - flow[1, y].astype(F32) * 0.1) * y_low[3]
        if y == ROWS - 1:
            value = value + (0.02 + flow[1, y].astype(F32) * 0.1) * y_high[3]
        _, first, last = edge_weights(flow, y)
        thermal_out[y, :8] = value[:8] + first * z_low[3, y:y + 1, :]
        thermal_out[y, 8:] = value[8:] + last * z_high[3, y:y + 1, :]


def source_kernel(
    moved, thermal, flow, y_low, y_high, z_low, z_high, even_h, even_t, odd_h, odd_t,
    provisional, message, source, lines, row_p, layer_p,
):
    size_x = moved.shape[-1]
    top = lax.broadcasted_iota(jnp.int32, (LAYERS, size_x), 0) == LAYERS - 1
    carried = None
    for y in range(ROWS):
        row, first, last = edge_weights(flow, y)
        fields = []
        for c in range(3):
            value = moved[c, y]
            if y == 0:
                value = value + (0.02 - flow[1, y].astype(F32) * 0.1) * y_low[c]
                if c == 1:
                    value = value - thermal[y] * 0.1 * y_low[4]
            if y == ROWS - 1:
                value = value + (0.02 + flow[1, y].astype(F32) * 0.1) * y_high[c]
                if c == 1:
                    value = value + thermal[y] * 0.1 * y_high[4]
            low = value[:8] + first * z_low[c, y:y + 1, :]
            high = value[8:] + last * z_high[c, y:y + 1, :]
            if c == 2:
                low = low - jnp.where(row == 0, thermal[y, :8] * 0.1, 0.0) * z_low[4, y:y + 1, :]
                high = high + jnp.where(row == 7, thermal[y, 8:] * 0.1, 0.0) * z_high[4, y:y + 1, :]
            value = jnp.concatenate([low, high], 0)
            provisional[c, y] = value
            fields.append(value)
        p0, p1, p2 = fields
        if y == 0:
            keep(row_p, 0, p1)
        else:
            keep(source, (y - 1) * LAYERS, carried + p1)
        keep(layer_p, y, p2[0:1, :])
        above = jnp.where(top, 0.0, pltpu.roll(p2, LAYERS - 1, 0))
        carried = (pltpu.roll(p0, size_x - 1, 1) - p0) - p1 + (above - p2)
    keep(source, (ROWS - 1) * LAYERS, carried)

    for b in range(size_x // 128):
        lanes = pl.ds(b * 128, 128)
        for j in range(4):
            for q in range(QUADS):
                lines[pl.ds(j * PIECE + q * 8, 8), lanes] = source[b, pl.ds(4 * q + j, ROWS, stride=LAYERS), :]
            lines[pl.ds(j * PIECE + 32, 4), lanes] = row_p[b, pl.ds(j, 4, stride=4), :]
            lines[pl.ds(j * PIECE + 36, 2), lanes] = layer_p[b, pl.ds(j, 2, stride=4), :]
            lines[pl.ds(j * PIECE + 38, 2), lanes] = jnp.zeros((2, 128), F32)
    near = lines[:, : size_x // 2]
    far = lines[:, size_x // 2:]
    evens = product(near + far, even_h[...], even_t[...], dot)
    odds = product(near - far, odd_h[...], odd_t[...], dot)
    for block in range(size_x // 128):
        part, at = (evens, block) if block < size_x // 256 else (odds, block - size_x // 256)
        a = [part[j * PIECE:(j + 1) * PIECE, at * 128:(at + 1) * 128] for j in range(4)]
        for i, piece in enumerate(swap_groups(a)):
            message[4 * block + i] = piece


def mode_constants(place, line_x, line_y):
    a = line_x[pl.ds(place[0], 1), :] + line_y[...]
    sinh = jnp.sqrt(a * (1.0 + 0.25 * a))
    lam = 1.0 / (1.0 + 0.5 * a + sinh)
    return a, sinh, lam


def wall_factors(lam, slab, slabs):
    square = lam * lam
    powers = [jnp.ones_like(lam), square]
    for m in range(2, LAYERS + 1):
        powers.append(powers[m // 2] * powers[m - m // 2])
    step = powers[LAYERS]

    def raised(count):
        value = lam
        factor = step
        for bit in range((slabs - 1).bit_length()):
            value = jnp.where((count // (1 << bit)) % 2 == 1, value * factor, value)
            factor = factor * factor
        return value

    low = raised(slab)
    high = raised(slabs - 1 - slab)
    below = low * (1.0 / square)
    floor = [1.0 + jnp.where(slab == 0, lam, below)] + [1.0 + low * powers[l] for l in range(LAYERS)]
    ceiling = [1.0 + high * powers[LAYERS - 1 - l] for l in range(-1, LAYERS)]
    return floor, ceiling, powers


def down_kernel(place, received, span_h, span_t, line_x, line_y, spectral, handed):
    sources = received.shape[0]
    size_y = sources * ROWS
    slabs = handed.shape[0]
    slab = place[1]
    row = lax.broadcasted_iota(jnp.int32, (sources, 8, 128), 1)
    group = lane_group((sources, 8, 128))
    extra = received[:, 8 * QUADS:, :]
    onward = jnp.concatenate([extra[1:], extra[:1]], 0)
    columns = []
    for q in range(QUADS):
        more = jnp.broadcast_to(onward[:, q:q + 1, :], (sources, 8, 128))
        values = received[:, 8 * q:8 * q + 8, :] + jnp.where(row == ROWS - 1, more, 0.0)
        columns.append(values.reshape(size_y, 128))
    first = jnp.broadcast_to(extra[:, 4:5, :], (sources, 8, 128))
    second = jnp.broadcast_to(extra[:, 5:6, :], (sources, 8, 128))
    layer = jnp.where(row < 4, first, second)
    layer = jnp.where((row % 4 == group) & (slab > 0), layer, 0.0)
    columns.append(layer.reshape(size_y, 128))
    stacked = jnp.concatenate(columns, 1)
    head, tail = split(stacked)
    waves = dot(span_h[...], head) + (dot(span_h[...], tail) + dot(span_t[...], head))

    last = waves[:, 128 * QUADS:]
    last = last + pltpu.roll(last, 64, 1)
    last = (last + pltpu.roll(last, 32, 1)).reshape(size_y // 32, 4, 8, 128)
    modes = size_y // 4
    mode_group = lane_group((modes, 128))
    pick = [last[:, i].reshape(modes, 128) for i in range(4)]
    layers = [
        jnp.where(
            mode_group < 2,
            jnp.where(mode_group == 0, pick[0], pick[1]),
            jnp.where(mode_group == 2, pick[2], pick[3]),
        )
    ]
    for q in range(QUADS):
        block = waves[:, 128 * q:128 * (q + 1)].reshape(size_y // 32, 4, 8, 128)
        layers += swap_groups([block[:, i].reshape(modes, 128) for i in range(4)])
    _, _, lam = mode_constants(place, line_x, line_y)
    floor, ceiling, _ = wall_factors(lam, slab, slabs)
    upward = jnp.zeros_like(lam)
    downward = jnp.zeros_like(lam)
    for l in range(LAYERS + 1):
        spectral[l] = layers[l]
        upward = lam * upward + floor[l] * layers[l]
        m = LAYERS - l
        downward = lam * downward + ceiling[m] * layers[m]
    for d in range(slabs):
        handed[d] = jnp.where(d > slab, upward, downward)


def up_kernel(place, spectral, handed, span_h, span_t, line_x, line_y, message):
    size_y = span_h.shape[0]
    sources = size_y // ROWS
    slabs = handed.shape[0]
    size_x = line_x.shape[0] * WAVES
    size_z = slabs * LAYERS
    slab = place[1]
    a, sinh, lam = mode_constants(place, line_x, line_y)
    floor, ceiling, powers = wall_factors(lam, slab, slabs)
    scale = 1.0 / (size_x * size_y)
    whole = powers[LAYERS]
    reach = powers[LAYERS // 2]
    for _ in range((slabs - 1).bit_length()):
        whole = whole * whole
    zero = a == 0.0
    weight = (-scale) / jnp.where(zero, 1.0, 2.0 * sinh * (1.0 - whole))
    weight = jnp.where(zero, 0.0, weight)
    upward = jnp.zeros_like(lam)
    downward = jnp.zeros_like(lam)
    for d in range(slabs - 1):
        upward = jnp.where(d < slab, reach * upward + handed[d], upward)
        e = slabs - 1 - d
        downward = jnp.where(e > slab, reach * downward + handed[e], downward)
    below = []
    for l in range(LAYERS + 1):
        upward = (lam * upward if l else upward) + floor[l] * spectral[l]
        below.append(upward)
    pressure = [None] * (LAYERS + 1)
    for l in reversed(range(LAYERS + 1)):
        pressure[l] = weight * (ceiling[l] * below[l] + floor[l] * downward)
        if l == LAYERS:
            mean = (0.5 / size_z) * (below[l][:8] + downward[:8])
        downward = lam * (downward + ceiling[l] * spectral[l])
    modes = size_y // 4
    flat = jnp.zeros((8, 128), F32)
    first_zero = zero[:8]
    for l in range(LAYERS + 1):
        if l:
            count = (slab * LAYERS + (l - 1)).astype(F32)
            flat = flat + (0.5 * below[l - 1][:8] - count * mean)
        pressure[l] = jnp.concatenate(
            [jnp.where(first_zero, flat * scale, pressure[l][:8]), pressure[l][8:]], 0
        )

    columns = []
    tall = (size_y // 32, 1, 8, 128)
    for q in range(QUADS):
        block = swap_groups(pressure[1 + 4 * q:5 + 4 * q])
        columns.append(jnp.concatenate([b.reshape(tall) for b in block], 1).reshape(size_y, 128))
    mode_group = lane_group((modes, 128))
    spread = []
    for i in range(4):
        part = jnp.where(mode_group == i, pressure[0], 0.0)
        part = part + pltpu.roll(part, 64, 1)
        spread.append((part + pltpu.roll(part, 32, 1)).reshape(tall))
    columns.append(jnp.concatenate(spread, 1).reshape(size_y, 128))
    stacked = jnp.concatenate(columns, 1)
    head, tail = split(stacked)
    values = dot(span_h[...], head) + (dot(span_h[...], tail) + dot(span_t[...], head))

    row = lax.broadcasted_iota(jnp.int32, (sources, 8, 128), 1)
    group = lane_group((sources, 8, 128))
    extra = jnp.zeros((sources, 8, 128), F32)
    for q in range(QUADS):
        block = values[:, 128 * q:128 * (q + 1)].reshape(sources, 8, 128)
        message[:, 8 * q:8 * q + 8, :] = block
        edge = jnp.concatenate([block[-1:], block[:-1]], 0)[:, ROWS - 1:ROWS, :]
        extra = jnp.where(row == q, jnp.broadcast_to(edge, extra.shape), extra)
    layer = values[:, 128 * QUADS:].reshape(sources, 8, 128)
    layer = jnp.where(row % 4 == group, layer, 0.0)
    layer = layer + pltpu.roll(layer, 7, 1)
    layer = layer + pltpu.roll(layer, 6, 1)
    extra = jnp.where(row == 4, jnp.broadcast_to(layer[:, 0:1, :], extra.shape), extra)
    extra = jnp.where(row == 5, jnp.broadcast_to(layer[:, 4:5, :], extra.shape), extra)
    message[:, 8 * QUADS:, :] = extra


def gradient_kernel(
    place, received, even_h, even_t, odd_h, odd_t, provisional, motion, lines, pressure, row_p, layer_p
):
    size_x = provisional.shape[-1]
    for block in range(size_x // 128):
        for j, piece in enumerate(swap_groups([received[4 * block + i] for i in range(4)])):
            lines[j * PIECE:(j + 1) * PIECE, block * 128:(block + 1) * 128] = piece
    evens = product(lines[:, : size_x // 2], even_h[...], even_t[...], dot)
    odds = product(lines[:, size_x // 2:], odd_h[...], odd_t[...], dot_nt)
    lines[:, : size_x // 2] = evens + odds
    lines[:, size_x // 2:] = evens - odds
    for b in range(size_x // 128):
        lanes = pl.ds(b * 128, 128)
        for j in range(4):
            for q in range(QUADS):
                pressure[b, pl.ds(4 * q + j, ROWS, stride=LAYERS), :] = lines[pl.ds(j * PIECE + q * 8, 8), lanes]
            row_p[b, pl.ds(j, 4, stride=4), :] = lines[pl.ds(j * PIECE + 32, 4), lanes]
            layer_p[b, pl.ds(j, 2, stride=4), :] = lines[pl.ds(j * PIECE + 36, 2), lanes]
    bottom = lax.broadcasted_iota(jnp.int32, (LAYERS, size_x), 0) == 0
    for y in range(ROWS):
        p = kept(pressure, y * LAYERS, LAYERS)
        before = kept(row_p, 0, LAYERS) if y == 0 else kept(pressure, (y - 1) * LAYERS, LAYERS)
        below = jnp.where(bottom, kept(layer_p, y, 1), pltpu.roll(p, 1, 0))
        slope_z = jnp.where(bottom & (place[1] == 0), 0.0, p - below)
        motion[0, y] = provisional[0, y] - (p - pltpu.roll(p, 1, 1))
        motion[1, y] = provisional[1, y] - (p - before)
        motion[2, y] = provisional[2, y] - slope_z


def shifted(value, axis, by, periodic):
    size = lax.axis_size(axis)
    pairs = [(i, (i + by) % size) for i in range(size) if periodic or 0 <= i + by < size]
    return lax.ppermute(value, axis, pairs)


def exchanged(pieces, axis):
    return lax.all_to_all(pieces, axis, split_axis=0, concat_axis=0, tiled=True)


def shape_of(*shape):
    return jax.ShapeDtypeStruct(shape, F32)


def on_device(dual_motion, dual_thermal, flow, base):
    size_x = dual_thermal.shape[-1]
    groups_y = lax.axis_size("gy")
    groups_z = lax.axis_size("gz")
    even, odd, span, line_x, line_y = tables(size_x, ROWS * groups_y)
    even_h, even_t = map(jnp.asarray, even)
    odd_h, odd_t = map(jnp.asarray, odd)
    span_h, span_t = map(jnp.asarray, span)
    line_x, line_y = jnp.asarray(line_x), jnp.asarray(line_y)
    modes = line_y.shape[0]
    place = jnp.stack([lax.axis_index("gy"), lax.axis_index("gz")]).astype(jnp.int32)

    def params(mib):
        return pltpu.CompilerParams(vmem_limit_bytes=mib << 20)

    rows = shape_of(5, LAYERS, size_x)
    layers = shape_of(5, ROWS, size_x)
    y_first, y_last, z_first, z_last = pl.pallas_call(
        sides_kernel,
        out_shape=(rows, rows, layers, layers),
        in_specs=[VMEM] * 3,
        out_specs=(VMEM,) * 4,
        compiler_params=params(8),
        name="sides",
    )(dual_motion, dual_thermal, base)
    z_low = shifted(z_last, "gz", 1, False)
    z_high = shifted(z_first, "gz", -1, False)
    y_low = shifted(y_last, "gy", 1, True)
    y_high = shifted(y_first, "gy", -1, True)
    moved, warmed = pl.pallas_call(
        inner_kernel,
        out_shape=(shape_of(3, ROWS, LAYERS, size_x), shape_of(ROWS, LAYERS, size_x)),
        in_specs=[VMEM] * 4,
        out_specs=(VMEM,) * 2,
        compiler_params=params(16),
        cost_estimate=pl.CostEstimate(flops=80 * ROWS * LAYERS * size_x, transcendentals=0, bytes_accessed=10 << 20),
        name="inner",
    )(dual_motion, dual_thermal, flow, base)
    provisional, message = pl.pallas_call(
        source_kernel,
        out_shape=(shape_of(3, ROWS, LAYERS, size_x), shape_of(groups_y, PIECE, 128)),
        in_specs=[VMEM] * 11,
        out_specs=(VMEM,) * 2,
        scratch_shapes=[
            pltpu.VMEM((size_x // 128, ROWS * LAYERS, 128), F32),
            pltpu.VMEM((4 * PIECE, size_x), F32),
            pltpu.VMEM((size_x // 128, LAYERS, 128), F32),
            pltpu.VMEM((size_x // 128, ROWS, 128), F32),
        ],
        compiler_params=params(24),
        name="source",
    )(moved, dual_thermal, flow, y_low, y_high, z_low, z_high, even_h, even_t, odd_h, odd_t)
    thermal_out = pl.pallas_call(
        warm_kernel,
        out_shape=shape_of(ROWS, LAYERS, size_x),
        in_specs=[VMEM] * 6,
        out_specs=VMEM,
        compiler_params=params(8),
        cost_estimate=pl.CostEstimate(flops=10 * ROWS * LAYERS * size_x, transcendentals=0, bytes_accessed=3 << 20),
        name="warm",
    )(warmed, flow, y_low, y_high, z_low, z_high)
    received = exchanged(message, "gy")
    spectral, handed = pl.pallas_call(
        down_kernel,
        out_shape=(shape_of(LAYERS + 1, modes, 128), shape_of(groups_z, modes, 128)),
        in_specs=[SMEM] + [VMEM] * 5,
        out_specs=(VMEM,) * 2,
        compiler_params=params(16),
        name="down",
    )(place, received, span_h, span_t, line_x, line_y)
    handed = exchanged(handed, "gz")
    message = pl.pallas_call(
        up_kernel,
        out_shape=shape_of(groups_y, PIECE, 128),
        in_specs=[SMEM] + [VMEM] * 6,
        out_specs=VMEM,
        compiler_params=params(16),
        name="up",
    )(place, spectral, handed, span_h, span_t, line_x, line_y)
    received = exchanged(message, "gy")
    motion = pl.pallas_call(
        gradient_kernel,
        out_shape=shape_of(3, ROWS, LAYERS, size_x),
        in_specs=[SMEM] + [VMEM] * 6,
        out_specs=VMEM,
        scratch_shapes=[
            pltpu.VMEM((4 * PIECE, size_x), F32),
            pltpu.VMEM((size_x // 128, ROWS * LAYERS, 128), F32),
            pltpu.VMEM((size_x // 128, LAYERS, 128), F32),
            pltpu.VMEM((size_x // 128, ROWS, 128), F32),
        ],
        compiler_params=params(24),
        name="gradient",
    )(place, received, even_h, even_t, odd_h, odd_t, provisional)
    return motion, thermal_out


def solution(mesh):
    split_y = P(None, "gy", "gz", None)
    split_flat = P("gy", "gz", None)
    return jax.shard_map(
        on_device,
        mesh=mesh,
        in_specs=(split_y, split_flat, split_y, split_flat),
        out_specs=(split_y, split_flat),
        check_vma=False,
    )
```

```python
import functools

import jax
import jax.numpy as jnp
import ml_dtypes
import numpy as np
from jax import lax
from jax.experimental import pallas as pl
from jax.experimental.pallas import tpu as pltpu
from jax.sharding import PartitionSpec as P

F32 = jnp.float32
BF16 = jnp.bfloat16
ROWS = 8
LAYERS = 16
WAVES = 32
QUADS = LAYERS // 4
PIECE = 8 * (QUADS + 1)
VMEM = pl.BlockSpec(memory_space=pltpu.VMEM)
SMEM = pl.BlockSpec(memory_space=pltpu.SMEM)
HBM = pl.BlockSpec(memory_space=pltpu.HBM)


def two_parts(table):
    head = table.astype(ml_dtypes.bfloat16)
    return head, (table - head.astype(np.float64)).astype(ml_dtypes.bfloat16)


def cas(phases, length):
    angles = (phases % length) * (2.0 * np.pi / length)
    return np.cos(angles) + np.sin(angles)


@functools.lru_cache(None)
def tables(size_x, size_y):
    half = np.arange(size_x // 2)
    even = two_parts(cas(half[:, None] * half[None, :], size_x // 2))
    odd = two_parts(cas(half[:, None] * (2 * half[None, :] + 1), size_x))
    full = np.arange(size_y)
    span = cas(full[:, None] * full[None, :], size_y)
    waves = np.concatenate([2 * half, 2 * half + 1])
    line_x = 4.0 * np.sin(np.pi * waves / size_x) ** 2
    line_x = np.tile(line_x.reshape(-1, WAVES), (1, 128 // WAVES))
    row = np.arange(size_y // 4)[:, None]
    lane = np.arange(128)[None, :]
    wave_y = 32 * (row // 8) + 8 * (lane // WAVES) + row % 8
    line_y = 4.0 * np.sin(np.pi * wave_y / size_y) ** 2
    halves = [span[:, n * 128:(n + 1) * 128] for n in range(size_y // 128)]
    return even, odd, np.concatenate(halves + [line_y, line_x], 0).astype(np.float32)


def split(values):
    head = values.astype(BF16)
    return head, (values - head.astype(F32)).astype(BF16)


def lane_group(shape):
    return lax.broadcasted_iota(jnp.int32, shape, len(shape) - 1) // WAVES


def swap_groups(a):
    axis = a[0].ndim - 1
    group = lane_group(a[0].shape)
    low = group < 2
    even = group % 2 == 0
    b0 = jnp.where(low, a[0], pltpu.roll(a[2], 64, axis))
    b2 = jnp.where(low, pltpu.roll(a[0], 64, axis), a[2])
    b1 = jnp.where(low, a[1], pltpu.roll(a[3], 64, axis))
    b3 = jnp.where(low, pltpu.roll(a[1], 64, axis), a[3])
    return (
        jnp.where(even, b0, pltpu.roll(b1, 32, axis)),
        jnp.where(even, pltpu.roll(b0, 96, axis), b1),
        jnp.where(even, b2, pltpu.roll(b3, 32, axis)),
        jnp.where(even, pltpu.roll(b2, 96, axis), b3),
    )


def dot(a, b):
    return jnp.dot(a, b, preferred_element_type=F32)


def dot_nt(a, b):
    return lax.dot_general(a, b, (((1,), (1,)), ((), ())), preferred_element_type=F32)


def product(values, head, tail, how):
    a, b = split(values)
    return how(a, head) + (how(b, head) + how(a, tail))


def keep(ref, start, values):
    for b in range(ref.shape[0]):
        ref[b, pl.ds(start, values.shape[0]), :] = values[:, b * 128:(b + 1) * 128]


def kept(ref, start, count):
    return jnp.concatenate([ref[b, pl.ds(start, count), :] for b in range(ref.shape[0])], 1)


def start_copies(pairs, sems):
    copies = [pltpu.make_async_copy(a, b, sems.at[n]) for n, (a, b) in enumerate(pairs)]
    for copy in copies:
        copy.start()
    return copies


def sides_kernel(motion_hbm, thermal_hbm, base_hbm, y_first, y_last, z_first, z_last, motion, thermal, base, sems):
    fetched = start_copies(((base_hbm, base), (thermal_hbm, thermal), (motion_hbm, motion)), sems)
    fetched[0].wait()
    for y in range(ROWS):
        warm = base[y].astype(F32)
        z_first[4, y:y + 1, :] = warm[:1]
        z_last[4, y:y + 1, :] = warm[LAYERS - 1:]
        if y in (0, ROWS - 1):
            (y_last if y else y_first)[4] = warm
    fetched[1].wait()
    y_first[3] = thermal[0]
    y_last[3] = thermal[ROWS - 1]
    for y in range(ROWS):
        z_first[3, y:y + 1, :] = thermal[y, :1, :]
        z_last[3, y:y + 1, :] = thermal[y, LAYERS - 1:, :]
    fetched[2].wait()
    for c in range(3):
        y_first[c] = motion[c, 0]
        y_last[c] = motion[c, ROWS - 1]
        for y in range(ROWS):
            z_first[c, y:y + 1, :] = motion[c, y, :1, :]
            z_last[c, y:y + 1, :] = motion[c, y, LAYERS - 1:, :]


def inner_kernel(
    motion_hbm, thermal_hbm, flow_hbm, base_hbm, moved, row_factors, layer_factors,
    motion, thermal, flow, base, sems,
):
    pairs = ((thermal_hbm, thermal), (base_hbm, base), (flow_hbm, flow), (motion_hbm, motion))
    for copy in start_copies(pairs, sems):
        copy.wait()
    size_x = motion.shape[-1]
    row = lax.broadcasted_iota(jnp.int32, (LAYERS, size_x), 0)
    top = row == LAYERS - 1
    bottom = row == 0

    def field(c, y):
        if c < 3:
            return motion[c, y]
        if c == 3:
            return thermal[y]
        return base[y].astype(F32)

    def neighbours(c, y):
        centre = field(c, y)
        y_plus = field(c, y + 1) if y < ROWS - 1 else None
        y_minus = field(c, y - 1) if y > 0 else None
        z_plus = jnp.where(top, 0.0, pltpu.roll(centre, LAYERS - 1, 0))
        z_minus = jnp.where(bottom, 0.0, pltpu.roll(centre, 1, 0))
        x_plus = pltpu.roll(centre, size_x - 1, 1)
        x_minus = pltpu.roll(centre, 1, 1)
        return centre, x_plus, x_minus, y_plus, y_minus, z_plus, z_minus

    for y in range(ROWS):
        weights = []
        for c in range(3):
            speed = flow[c, y].astype(F32) * 0.1
            weights += [0.02 + speed, 0.02 - speed]
        _, hx, gx, hy, gy, hz, gz = neighbours(4, y)
        slope_y = -gy if hy is None else hy if gy is None else hy - gy
        slopes = (hx - gx, slope_y, hz - gz)
        heat = thermal[y] * 0.1
        if y == 0:
            row_factors[0] = weights[3]
            row_factors[1] = -heat
        if y == ROWS - 1:
            row_factors[2] = weights[2]
            row_factors[3] = heat
        layer_factors[0, y:y + 1, :] = weights[5][:1]
        layer_factors[1, y:y + 1, :] = -heat[:1]
        layer_factors[2, y:y + 1, :] = weights[4][LAYERS - 1:]
        layer_factors[3, y:y + 1, :] = heat[LAYERS - 1:]
        for c in range(4):
            parts = neighbours(c, y)
            value = parts[0] * 0.88
            for weight, part in zip(weights, parts[1:]):
                if part is not None:
                    value = value + weight * part
            moved[c, y] = value + (heat * slopes[c] if c < 3 else 0.2 * motion[2, y])


def source_kernel(
    moved, row_factors, layer_factors, y_low, y_high, z_low, z_high, even_h, even_t, odd_h, odd_t,
    provisional_hbm, thermal_hbm, message_hbm,
    provisional, message, source, lines, row_p, layer_p, sems,
):
    size_x = moved.shape[-1]
    row = lax.broadcasted_iota(jnp.int32, (8, size_x), 0)
    top = lax.broadcasted_iota(jnp.int32, (LAYERS, size_x), 0) == LAYERS - 1
    lows = [layer_factors[0] * z_low[c] for c in range(4)]
    highs = [layer_factors[2] * z_high[c] for c in range(4)]
    lows[2] = lows[2] + layer_factors[1] * z_low[4]
    highs[2] = highs[2] + layer_factors[3] * z_high[4]
    carried = None
    for y in range(ROWS):
        for c in range(4):
            value = moved[c, y]
            if y == 0:
                value = value + row_factors[0] * y_low[c]
                if c == 1:
                    value = value + row_factors[1] * y_low[4]
            if y == ROWS - 1:
                value = value + row_factors[2] * y_high[c]
                if c == 1:
                    value = value + row_factors[3] * y_high[4]
            provisional[c, y, :8] = value[:8] + jnp.where(row == 0, lows[c][y:y + 1], 0.0)
            provisional[c, y, 8:] = value[8:] + jnp.where(row == 7, highs[c][y:y + 1], 0.0)
        p0, p1, p2 = (provisional[c, y] for c in range(3))
        if y == 0:
            keep(row_p, 0, p1)
        else:
            keep(source, (y - 1) * LAYERS, carried + p1)
        keep(layer_p, y, p2[0:1, :])
        above = jnp.where(top, 0.0, pltpu.roll(p2, LAYERS - 1, 0))
        carried = (pltpu.roll(p0, size_x - 1, 1) - p0) - p1 + (above - p2)
    keep(source, (ROWS - 1) * LAYERS, carried)
    stored = start_copies(
        ((provisional.at[pl.ds(0, 3)], provisional_hbm), (provisional.at[3], thermal_hbm)), sems
    )

    for b in range(size_x // 128):
        lanes = pl.ds(b * 128, 128)
        for j in range(4):
            for q in range(QUADS):
                lines[pl.ds(j * PIECE + q * 8, 8), lanes] = source[b, pl.ds(4 * q + j, ROWS, stride=LAYERS), :]
            lines[pl.ds(j * PIECE + 32, 4), lanes] = row_p[b, pl.ds(j, 4, stride=4), :]
            lines[pl.ds(j * PIECE + 36, 2), lanes] = layer_p[b, pl.ds(j, 2, stride=4), :]
            lines[pl.ds(j * PIECE + 38, 2), lanes] = jnp.zeros((2, 128), F32)
    near = lines[:, : size_x // 2]
    far = lines[:, size_x // 2:]
    half = size_x // 256
    for turn in range(2):
        if turn == 0:
            waves = product(near + far, even_h[...], even_t[...], dot)
        else:
            waves = product(near - far, odd_h[...], odd_t[...], dot)
        for block in range(half):
            a = [waves[j * PIECE:(j + 1) * PIECE, block * 128:(block + 1) * 128] for j in range(4)]
            for i, piece in enumerate(swap_groups(a)):
                message[4 * (turn * half + block) + i] = piece
        part = pl.ds(turn * 4 * half, 4 * half)
        copy = pltpu.make_async_copy(message.at[part], message_hbm.at[part], sems.at[2 + turn])
        copy.start()
        stored.append(copy)
    for copy in stored:
        copy.wait()


def span_product(table, values):
    size_y = values.shape[0]
    wide = jnp.concatenate([table[pl.ds(n * size_y, size_y), :] for n in range(size_y // 128)], 1)
    left = split(wide)
    right = split(values)
    return dot(left[0], right[0]) + (dot(left[0], right[1]) + dot(left[1], right[0]))


def wall_factors(lam, slab, slabs):
    square = lam * lam
    powers = [jnp.ones_like(lam), square]
    for m in range(2, LAYERS + 1):
        powers.append(powers[m // 2] * powers[m - m // 2])
    step = powers[LAYERS]

    def raised(count):
        value = lam
        factor = step
        for bit in range((slabs - 1).bit_length()):
            value = jnp.where((count // (1 << bit)) % 2 == 1, value * factor, value)
            factor = factor * factor
        return value

    low = raised(slab)
    high = raised(slabs - 1 - slab)
    below = low * (1.0 / square)
    floor = [1.0 + jnp.where(slab == 0, lam, below)] + [1.0 + low * powers[l] for l in range(LAYERS)]
    ceiling = [1.0 + high * powers[LAYERS - 1 - l] for l in range(-1, LAYERS)]
    return floor, ceiling, powers


def down_kernel(place, received, table_hbm, spectral, handed, table, sems):
    fetched = start_copies(((table_hbm, table),), sems)
    sources = received.shape[0]
    size_y = sources * ROWS
    slabs = handed.shape[0]
    size_x = sources * WAVES
    slab = place[1]
    row = lax.broadcasted_iota(jnp.int32, (sources, 8, 128), 1)
    group = lane_group((sources, 8, 128))
    extra = received[:, 8 * QUADS:, :]
    onward = jnp.concatenate([extra[1:], extra[:1]], 0)
    columns = []
    for q in range(QUADS):
        more = jnp.broadcast_to(onward[:, q:q + 1, :], (sources, 8, 128))
        values = received[:, 8 * q:8 * q + 8, :] + jnp.where(row == ROWS - 1, more, 0.0)
        columns.append(values.reshape(size_y, 128))
    first = jnp.broadcast_to(extra[:, 4:5, :], (sources, 8, 128))
    second = jnp.broadcast_to(extra[:, 5:6, :], (sources, 8, 128))
    layer = jnp.where(row < 4, first, second)
    layer = jnp.where((row % 4 == group) & (slab > 0), layer, 0.0)
    columns.append(layer.reshape(size_y, 128))
    fetched[0].wait()
    waves = span_product(table, jnp.concatenate(columns, 1))

    last = waves[:, 128 * QUADS:]
    last = last + pltpu.roll(last, 64, 1)
    last = (last + pltpu.roll(last, 32, 1)).reshape(size_y // 32, 4, 8, 128)
    modes = size_y // 4
    mode_group = lane_group((modes, 128))
    pick = [last[:, i].reshape(modes, 128) for i in range(4)]
    layers = [
        jnp.where(
            mode_group < 2,
            jnp.where(mode_group == 0, pick[0], pick[1]),
            jnp.where(mode_group == 2, pick[2], pick[3]),
        )
    ]
    for q in range(QUADS):
        block = waves[:, 128 * q:128 * (q + 1)].reshape(size_y // 32, 4, 8, 128)
        layers += swap_groups([block[:, i].reshape(modes, 128) for i in range(4)])
    modes = size_y // 4
    line_y = table[pl.ds(2 * size_y, modes), :]
    a = table[pl.ds(2 * size_y + modes + place[0], 1), :] + line_y
    sinh = jnp.sqrt(a * (1.0 + 0.25 * a))
    lam = 1.0 / (1.0 + 0.5 * a + sinh)
    floor, ceiling, powers = wall_factors(lam, slab, slabs)
    spectral[LAYERS + 1] = lam
    whole = powers[LAYERS]
    for _ in range((slabs - 1).bit_length()):
        whole = whole * whole
    zero = a == 0.0
    weight = (-1.0 / (size_x * size_y)) / jnp.where(zero, 1.0, 2.0 * sinh * (1.0 - whole))
    spectral[LAYERS + 2] = jnp.where(zero, 0.0, weight)
    upward = jnp.zeros_like(lam)
    downward = jnp.zeros_like(lam)
    for l in range(LAYERS + 1):
        spectral[l] = layers[l]
        upward = lam * upward + floor[l] * layers[l]
        m = LAYERS - l
        downward = lam * downward + ceiling[m] * layers[m]
    for d in range(slabs):
        handed[d] = jnp.where(d > slab, upward, downward)


def up_kernel(place, spectral, handed, table_hbm, message_hbm, table, message, sems):
    fetched = start_copies(((table_hbm, table),), sems)
    sources = message.shape[0]
    size_y = sources * ROWS
    slabs = handed.shape[0]
    size_x = sources * WAVES
    size_z = slabs * LAYERS
    slab = place[1]
    lam = spectral[LAYERS + 1]
    weight = spectral[LAYERS + 2]
    floor, ceiling, powers = wall_factors(lam, slab, slabs)
    scale = 1.0 / (size_x * size_y)
    reach = powers[LAYERS // 2]
    upward = jnp.zeros_like(lam)
    downward = jnp.zeros_like(lam)
    for d in range(slabs - 1):
        upward = jnp.where(d < slab, reach * upward + handed[d], upward)
        e = slabs - 1 - d
        downward = jnp.where(e > slab, reach * downward + handed[e], downward)
    below = []
    for l in range(LAYERS + 1):
        upward = (lam * upward if l else upward) + floor[l] * spectral[l]
        below.append(upward)
    pressure = [None] * (LAYERS + 1)
    for l in reversed(range(LAYERS + 1)):
        pressure[l] = weight * (ceiling[l] * below[l] + floor[l] * downward)
        if l == LAYERS:
            mean = (0.5 / size_z) * (below[l][:8] + downward[:8])
        downward = lam * (downward + ceiling[l] * spectral[l])
    modes = size_y // 4
    flat = jnp.zeros((8, 128), F32)
    first_zero = weight[:8] == 0.0
    for l in range(LAYERS + 1):
        if l:
            count = (slab * LAYERS + (l - 1)).astype(F32)
            flat = flat + (0.5 * below[l - 1][:8] - count * mean)
        pressure[l] = jnp.concatenate(
            [jnp.where(first_zero, flat * scale, pressure[l][:8]), pressure[l][8:]], 0
        )

    columns = []
    tall = (size_y // 32, 1, 8, 128)
    for q in range(QUADS):
        block = swap_groups(pressure[1 + 4 * q:5 + 4 * q])
        columns.append(jnp.concatenate([b.reshape(tall) for b in block], 1).reshape(size_y, 128))
    mode_group = lane_group((modes, 128))
    spread = []
    for i in range(4):
        part = jnp.where(mode_group == i, pressure[0], 0.0)
        part = part + pltpu.roll(part, 64, 1)
        spread.append((part + pltpu.roll(part, 32, 1)).reshape(tall))
    columns.append(jnp.concatenate(spread, 1).reshape(size_y, 128))
    fetched[0].wait()
    values = span_product(table, jnp.concatenate(columns, 1))

    row = lax.broadcasted_iota(jnp.int32, (sources, 8, 128), 1)
    group = lane_group((sources, 8, 128))
    extra = jnp.zeros((sources, 8, 128), F32)
    for q in range(QUADS):
        block = values[:, 128 * q:128 * (q + 1)].reshape(sources, 8, 128)
        message[:, 8 * q:8 * q + 8, :] = block
        edge = jnp.concatenate([block[-1:], block[:-1]], 0)[:, ROWS - 1:ROWS, :]
        extra = jnp.where(row == q, jnp.broadcast_to(edge, extra.shape), extra)
    layer = values[:, 128 * QUADS:].reshape(sources, 8, 128)
    layer = jnp.where(row % 4 == group, layer, 0.0)
    layer = layer + pltpu.roll(layer, 7, 1)
    layer = layer + pltpu.roll(layer, 6, 1)
    extra = jnp.where(row == 4, jnp.broadcast_to(layer[:, 0:1, :], extra.shape), extra)
    extra = jnp.where(row == 5, jnp.broadcast_to(layer[:, 4:5, :], extra.shape), extra)
    message[:, 8 * QUADS:, :] = extra
    copy = pltpu.make_async_copy(message, message_hbm, sems.at[1])
    copy.start()
    copy.wait()


def gradient_kernel(
    place, received, even_h, even_t, odd_h, odd_t, provisional_hbm, motion_hbm,
    provisional, motion, lines, pressure, row_p, layer_p, sems,
):
    fetched = start_copies(((provisional_hbm, provisional),), sems)
    size_x = provisional.shape[-1]
    for block in range(size_x // 128):
        for j, piece in enumerate(swap_groups([received[4 * block + i] for i in range(4)])):
            lines[j * PIECE:(j + 1) * PIECE, block * 128:(block + 1) * 128] = piece
    evens = product(lines[:, : size_x // 2], even_h[...], even_t[...], dot)
    odds = product(lines[:, size_x // 2:], odd_h[...], odd_t[...], dot_nt)
    lines[:, : size_x // 2] = evens + odds
    lines[:, size_x // 2:] = evens - odds
    for b in range(size_x // 128):
        lanes = pl.ds(b * 128, 128)
        for j in range(4):
            for q in range(QUADS):
                pressure[b, pl.ds(4 * q + j, ROWS, stride=LAYERS), :] = lines[pl.ds(j * PIECE + q * 8, 8), lanes]
            row_p[b, pl.ds(j, 4, stride=4), :] = lines[pl.ds(j * PIECE + 32, 4), lanes]
            layer_p[b, pl.ds(j, 2, stride=4), :] = lines[pl.ds(j * PIECE + 36, 2), lanes]
    fetched[0].wait()
    stored = []
    bottom = lax.broadcasted_iota(jnp.int32, (LAYERS, size_x), 0) == 0
    for y in range(ROWS):
        p = kept(pressure, y * LAYERS, LAYERS)
        before = kept(row_p, 0, LAYERS) if y == 0 else kept(pressure, (y - 1) * LAYERS, LAYERS)
        below = jnp.where(bottom, kept(layer_p, y, 1), pltpu.roll(p, 1, 0))
        slope_z = jnp.where(bottom & (place[1] == 0), 0.0, p - below)
        motion[0, y] = provisional[0, y] - (p - pltpu.roll(p, 1, 1))
        motion[1, y] = provisional[1, y] - (p - before)
        motion[2, y] = provisional[2, y] - slope_z
        copy = pltpu.make_async_copy(motion.at[:, pl.ds(y, 1)], motion_hbm.at[:, pl.ds(y, 1)], sems.at[1 + y])
        copy.start()
        stored.append(copy)
    for copy in stored:
        copy.wait()


def shifted(value, axis, by, periodic):
    size = lax.axis_size(axis)
    pairs = [(i, (i + by) % size) for i in range(size) if periodic or 0 <= i + by < size]
    return lax.ppermute(value, axis, pairs)


def exchanged(pieces, axis):
    return lax.all_to_all(pieces, axis, split_axis=0, concat_axis=0, tiled=True)


def shape_of(*shape):
    return jax.ShapeDtypeStruct(shape, F32)


def on_device(dual_motion, dual_thermal, flow, base):
    size_x = dual_thermal.shape[-1]
    groups_y = lax.axis_size("gy")
    groups_z = lax.axis_size("gz")
    even, odd, table = tables(size_x, ROWS * groups_y)
    even_h, even_t = map(jnp.asarray, even)
    odd_h, odd_t = map(jnp.asarray, odd)
    size_t = table.shape[0]
    modes = ROWS * groups_y // 4
    blocks = size_x // 128
    place = jnp.stack([lax.axis_index("gy"), lax.axis_index("gz")]).astype(jnp.int32)

    def hbm(value):
        return pltpu.with_memory_space_constraint(value, pltpu.HBM)

    def params(mib):
        return pltpu.CompilerParams(vmem_limit_bytes=mib << 20)

    motion_in, thermal_in, flow_in, base_in = map(hbm, (dual_motion, dual_thermal, flow, base))
    table = hbm(jnp.asarray(table))
    rows = shape_of(5, LAYERS, size_x)
    layers = shape_of(5, ROWS, size_x)
    motion_shape = (3, ROWS, LAYERS, size_x)
    thermal_shape = motion_shape[1:]
    message_shape = (groups_y, PIECE, 128)
    y_first, y_last, z_first, z_last = pl.pallas_call(
        sides_kernel,
        out_shape=(rows, rows, layers, layers),
        in_specs=[HBM] * 3,
        out_specs=(VMEM,) * 4,
        scratch_shapes=[
            pltpu.VMEM(motion_shape, F32),
            pltpu.VMEM(thermal_shape, F32),
            pltpu.VMEM(thermal_shape, BF16),
            pltpu.SemaphoreType.DMA((3,)),
        ],
        compiler_params=params(16),
        name="sides",
    )(motion_in, thermal_in, base_in)
    z_low = shifted(z_last, "gz", 1, False)
    z_high = shifted(z_first, "gz", -1, False)
    y_low = shifted(y_last, "gy", 1, True)
    y_high = shifted(y_first, "gy", -1, True)
    moved, row_factors, layer_factors = pl.pallas_call(
        inner_kernel,
        out_shape=(
            shape_of(4, *thermal_shape),
            shape_of(4, LAYERS, size_x),
            shape_of(4, ROWS, size_x),
        ),
        in_specs=[HBM] * 4,
        out_specs=(VMEM,) * 3,
        scratch_shapes=[
            pltpu.VMEM(motion_shape, F32),
            pltpu.VMEM(thermal_shape, F32),
            pltpu.VMEM(motion_shape, BF16),
            pltpu.VMEM(thermal_shape, BF16),
            pltpu.SemaphoreType.DMA((4,)),
        ],
        compiler_params=params(16),
        cost_estimate=pl.CostEstimate(
            flops=80 * ROWS * LAYERS * size_x, transcendentals=0, bytes_accessed=10 << 20
        ),
        name="inner",
    )(motion_in, thermal_in, flow_in, base_in)
    provisional, thermal_out, message = pl.pallas_call(
        source_kernel,
        out_shape=(
            pltpu.HBM(motion_shape, F32),
            pltpu.HBM(thermal_shape, F32),
            pltpu.HBM(message_shape, F32),
        ),
        in_specs=[VMEM] * 11,
        out_specs=(HBM,) * 3,
        scratch_shapes=[
            pltpu.VMEM((4, *thermal_shape), F32),
            pltpu.VMEM(message_shape, F32),
            pltpu.VMEM((blocks, ROWS * LAYERS, 128), F32),
            pltpu.VMEM((4 * PIECE, size_x), F32),
            pltpu.VMEM((blocks, LAYERS, 128), F32),
            pltpu.VMEM((blocks, ROWS, 128), F32),
            pltpu.SemaphoreType.DMA((4,)),
        ],
        compiler_params=params(24),
        name="source",
    )(moved, row_factors, layer_factors, y_low, y_high, z_low, z_high, even_h, even_t, odd_h, odd_t)
    received = exchanged(message, "gy")
    spectral, handed = pl.pallas_call(
        down_kernel,
        out_shape=(shape_of(LAYERS + 3, modes, 128), shape_of(groups_z, modes, 128)),
        in_specs=[SMEM, VMEM, HBM],
        out_specs=(VMEM,) * 2,
        scratch_shapes=[pltpu.VMEM((size_t, 128), F32), pltpu.SemaphoreType.DMA((1,))],
        compiler_params=params(16),
        name="down",
    )(place, received, table)
    handed = exchanged(handed, "gz")
    message = pl.pallas_call(
        up_kernel,
        out_shape=pltpu.HBM(message_shape, F32),
        in_specs=[SMEM, VMEM, VMEM, HBM],
        out_specs=HBM,
        scratch_shapes=[
            pltpu.VMEM((size_t, 128), F32),
            pltpu.VMEM(message_shape, F32),
            pltpu.SemaphoreType.DMA((2,)),
        ],
        compiler_params=params(16),
        name="up",
    )(place, spectral, handed, table)
    received = exchanged(message, "gy")
    motion = pl.pallas_call(
        gradient_kernel,
        out_shape=pltpu.HBM(motion_shape, F32),
        in_specs=[SMEM] + [VMEM] * 5 + [HBM],
        out_specs=HBM,
        scratch_shapes=[
            pltpu.VMEM(motion_shape, F32),
            pltpu.VMEM(motion_shape, F32),
            pltpu.VMEM((4 * PIECE, size_x), F32),
            pltpu.VMEM((blocks, ROWS * LAYERS, 128), F32),
            pltpu.VMEM((blocks, LAYERS, 128), F32),
            pltpu.VMEM((blocks, ROWS, 128), F32),
            pltpu.SemaphoreType.DMA((1 + ROWS,)),
        ],
        compiler_params=params(24),
        name="gradient",
    )(place, received, even_h, even_t, odd_h, odd_t, hbm(provisional))
    return motion, thermal_out


def solution(mesh):
    split_y = P(None, "gy", "gz", None)
    split_flat = P("gy", "gz", None)
    return jax.shard_map(
        on_device,
        mesh=mesh,
        in_specs=(split_y, split_flat, split_y, split_flat),
        out_specs=(split_y, split_flat),
        check_vma=False,
    )
```

```python
import functools

import jax
import jax.numpy as jnp
import ml_dtypes
import numpy as np
from jax import lax
from jax.experimental import pallas as pl
from jax.experimental.pallas import tpu as pltpu
from jax.sharding import PartitionSpec as P

F32 = jnp.float32
BF16 = jnp.bfloat16
ROWS = 8
LAYERS = 16
WAVES = 32
QUADS = LAYERS // 4
PIECE = 8 * (QUADS + 1)
VMEM = pl.BlockSpec(memory_space=pltpu.VMEM)
HBM = pl.BlockSpec(memory_space=pltpu.HBM)


def two_parts(table):
    head = table.astype(ml_dtypes.bfloat16)
    return head, (table - head.astype(np.float64)).astype(ml_dtypes.bfloat16)


def cas(phases, length):
    angles = (phases % length) * (2.0 * np.pi / length)
    return np.cos(angles) + np.sin(angles)


@functools.lru_cache(None)
def tables(size_x, size_y):
    half = np.arange(size_x // 2)
    even = two_parts(cas(half[:, None] * half[None, :], size_x // 2))
    odd = two_parts(cas(half[:, None] * (2 * half[None, :] + 1), size_x))
    full = np.arange(size_y)
    span = cas(full[:, None] * full[None, :], size_y)
    waves = np.concatenate([2 * half, 2 * half + 1])
    line_x = 4.0 * np.sin(np.pi * waves / size_x) ** 2
    line_x = np.tile(line_x.reshape(-1, WAVES), (1, 128 // WAVES))
    row = np.arange(size_y // 4)[:, None]
    lane = np.arange(128)[None, :]
    wave_y = 32 * (row // 8) + 8 * (lane // WAVES) + row % 8
    line_y = 4.0 * np.sin(np.pi * wave_y / size_y) ** 2
    halves = [span[:, n * 128:(n + 1) * 128] for n in range(size_y // 128)]
    return even, odd, np.concatenate(halves + [line_y, line_x], 0).astype(np.float32)


def split(values):
    head = values.astype(BF16)
    return head, (values - head.astype(F32)).astype(BF16)


def lane_group(shape):
    return lax.broadcasted_iota(jnp.int32, shape, len(shape) - 1) // WAVES


def swap_groups(a):
    axis = a[0].ndim - 1
    group = lane_group(a[0].shape)
    low = group < 2
    even = group % 2 == 0
    b0 = jnp.where(low, a[0], pltpu.roll(a[2], 64, axis))
    b2 = jnp.where(low, pltpu.roll(a[0], 64, axis), a[2])
    b1 = jnp.where(low, a[1], pltpu.roll(a[3], 64, axis))
    b3 = jnp.where(low, pltpu.roll(a[1], 64, axis), a[3])
    return (
        jnp.where(even, b0, pltpu.roll(b1, 32, axis)),
        jnp.where(even, pltpu.roll(b0, 96, axis), b1),
        jnp.where(even, b2, pltpu.roll(b3, 32, axis)),
        jnp.where(even, pltpu.roll(b2, 96, axis), b3),
    )


def dot(a, b):
    return jnp.dot(a, b, preferred_element_type=F32)


def dot_nt(a, b):
    return lax.dot_general(a, b, (((1,), (1,)), ((), ())), preferred_element_type=F32)


def product(values, head, tail, how):
    a, b = split(values)
    return how(a, head) + (how(b, head) + how(a, tail))


def keep(ref, start, values):
    for b in range(ref.shape[0]):
        ref[b, pl.ds(start, values.shape[0]), :] = values[:, b * 128:(b + 1) * 128]


def kept(ref, start, count):
    return jnp.concatenate([ref[b, pl.ds(start, count), :] for b in range(ref.shape[0])], 1)


def start_copies(pairs, sems):
    copies = [pltpu.make_async_copy(a, b, sems.at[n]) for n, (a, b) in enumerate(pairs)]
    for copy in copies:
        copy.start()
    return copies


def sides_kernel(
    motion_hbm, thermal_hbm, flow_hbm, base_hbm,
    y_first, y_last, z_first, z_last, motion, thermal, flow, base, sems,
):
    pairs = ((base_hbm, base), (thermal_hbm, thermal), (motion_hbm, motion), (flow_hbm, flow))
    fetched = start_copies(pairs, sems)
    fetched[0].wait()
    for y in range(ROWS):
        warm = base[y].astype(F32)
        z_first[4, y:y + 1, :] = warm[:1]
        z_last[4, y:y + 1, :] = warm[LAYERS - 1:]
        if y in (0, ROWS - 1):
            (y_last if y else y_first)[4] = warm
    fetched[1].wait()
    y_first[3] = thermal[0]
    y_last[3] = thermal[ROWS - 1]
    for y in range(ROWS):
        z_first[3, y:y + 1, :] = thermal[y, :1, :]
        z_last[3, y:y + 1, :] = thermal[y, LAYERS - 1:, :]
    fetched[2].wait()
    for c in range(3):
        y_first[c] = motion[c, 0]
        y_last[c] = motion[c, ROWS - 1]
        for y in range(ROWS):
            z_first[c, y:y + 1, :] = motion[c, y, :1, :]
            z_last[c, y:y + 1, :] = motion[c, y, LAYERS - 1:, :]
    fetched[3].wait()


def inner_kernel(motion, thermal, flow, base, moved, row_factors, layer_factors):
    size_x = motion.shape[-1]
    row = lax.broadcasted_iota(jnp.int32, (LAYERS, size_x), 0)
    top = row == LAYERS - 1
    bottom = row == 0

    def field(c, y):
        if c < 3:
            return motion[c, y]
        if c == 3:
            return thermal[y]
        return base[y].astype(F32)

    def neighbours(c, y):
        centre = field(c, y)
        y_plus = field(c, y + 1) if y < ROWS - 1 else None
        y_minus = field(c, y - 1) if y > 0 else None
        z_plus = jnp.where(top, 0.0, pltpu.roll(centre, LAYERS - 1, 0))
        z_minus = jnp.where(bottom, 0.0, pltpu.roll(centre, 1, 0))
        x_plus = pltpu.roll(centre, size_x - 1, 1)
        x_minus = pltpu.roll(centre, 1, 1)
        return centre, x_plus, x_minus, y_plus, y_minus, z_plus, z_minus

    for y in range(ROWS):
        weights = []
        for c in range(3):
            speed = flow[c, y].astype(F32) * 0.1
            weights += [0.02 + speed, 0.02 - speed]
        _, hx, gx, hy, gy, hz, gz = neighbours(4, y)
        slope_y = -gy if hy is None else hy if gy is None else hy - gy
        slopes = (hx - gx, slope_y, hz - gz)
        heat = thermal[y] * 0.1
        if y == 0:
            row_factors[0] = weights[3]
            row_factors[1] = -heat
        if y == ROWS - 1:
            row_factors[2] = weights[2]
            row_factors[3] = heat
        layer_factors[0, y:y + 1, :] = weights[5][:1]
        layer_factors[1, y:y + 1, :] = -heat[:1]
        layer_factors[2, y:y + 1, :] = weights[4][LAYERS - 1:]
        layer_factors[3, y:y + 1, :] = heat[LAYERS - 1:]
        for c in range(4):
            parts = neighbours(c, y)
            value = parts[0] * 0.88
            for weight, part in zip(weights, parts[1:]):
                if part is not None:
                    value = value + weight * part
            moved[c, y] = value + (heat * slopes[c] if c < 3 else 0.2 * motion[2, y])


def source_kernel(
    moved, row_factors, layer_factors, y_low, y_high, z_low, z_high, even_h, even_t, odd_h, odd_t,
    provisional_hbm, thermal_hbm, message,
    provisional, source, lines, row_p, layer_p, sems,
):
    size_x = moved.shape[-1]
    row = lax.broadcasted_iota(jnp.int32, (8, size_x), 0)
    top = lax.broadcasted_iota(jnp.int32, (LAYERS, size_x), 0) == LAYERS - 1
    lows = [layer_factors[0] * z_low[c] for c in range(4)]
    highs = [layer_factors[2] * z_high[c] for c in range(4)]
    lows[2] = lows[2] + layer_factors[1] * z_low[4]
    highs[2] = highs[2] + layer_factors[3] * z_high[4]
    carried = None
    for y in range(ROWS):
        for c in range(4):
            value = moved[c, y]
            if y == 0:
                value = value + row_factors[0] * y_low[c]
                if c == 1:
                    value = value + row_factors[1] * y_low[4]
            if y == ROWS - 1:
                value = value + row_factors[2] * y_high[c]
                if c == 1:
                    value = value + row_factors[3] * y_high[4]
            provisional[c, y, :8] = value[:8] + jnp.where(row == 0, lows[c][y:y + 1], 0.0)
            provisional[c, y, 8:] = value[8:] + jnp.where(row == 7, highs[c][y:y + 1], 0.0)
        p0, p1, p2 = (provisional[c, y] for c in range(3))
        if y == 0:
            keep(row_p, 0, p1)
        else:
            keep(source, (y - 1) * LAYERS, carried + p1)
        keep(layer_p, y, p2[0:1, :])
        above = jnp.where(top, 0.0, pltpu.roll(p2, LAYERS - 1, 0))
        carried = (pltpu.roll(p0, size_x - 1, 1) - p0) - p1 + (above - p2)
    keep(source, (ROWS - 1) * LAYERS, carried)
    stored = start_copies(
        ((provisional.at[pl.ds(0, 3)], provisional_hbm), (provisional.at[3], thermal_hbm)), sems
    )

    for b in range(size_x // 128):
        lanes = pl.ds(b * 128, 128)
        for j in range(4):
            for q in range(QUADS):
                lines[pl.ds(j * PIECE + q * 8, 8), lanes] = source[b, pl.ds(4 * q + j, ROWS, stride=LAYERS), :]
            lines[pl.ds(j * PIECE + 32, 4), lanes] = row_p[b, pl.ds(j, 4, stride=4), :]
            lines[pl.ds(j * PIECE + 36, 2), lanes] = layer_p[b, pl.ds(j, 2, stride=4), :]
            lines[pl.ds(j * PIECE + 38, 2), lanes] = jnp.zeros((2, 128), F32)
    near = lines[:, : size_x // 2]
    far = lines[:, size_x // 2:]
    half = size_x // 256
    for turn in range(2):
        if turn == 0:
            waves = product(near + far, even_h[...], even_t[...], dot)
        else:
            waves = product(near - far, odd_h[...], odd_t[...], dot)
        for block in range(half):
            a = [waves[j * PIECE:(j + 1) * PIECE, block * 128:(block + 1) * 128] for j in range(4)]
            for i, piece in enumerate(swap_groups(a)):
                message[4 * (turn * half + block) + i] = piece
    for copy in stored:
        copy.wait()


def span_product(table, values):
    size_y = values.shape[0]
    wide = jnp.concatenate([table[pl.ds(n * size_y, size_y), :] for n in range(size_y // 128)], 1)
    left = split(wide)
    right = split(values)
    return dot(left[0], right[0]) + (dot(left[0], right[1]) + dot(left[1], right[0]))


def wall_factors(lam, slab, slabs):
    square = lam * lam
    powers = [jnp.ones_like(lam), square]
    for m in range(2, LAYERS + 1):
        powers.append(powers[m // 2] * powers[m - m // 2])
    step = powers[LAYERS]

    def raised(count):
        value = lam
        factor = step
        for bit in range((slabs - 1).bit_length()):
            value = jnp.where((count // (1 << bit)) % 2 == 1, value * factor, value)
            factor = factor * factor
        return value

    low = raised(slab)
    high = raised(slabs - 1 - slab)
    below = low * (1.0 / square)
    floor = [1.0 + jnp.where(slab == 0, lam, below)] + [1.0 + low * powers[l] for l in range(LAYERS)]
    ceiling = [1.0 + high * powers[LAYERS - 1 - l] for l in range(-1, LAYERS)]
    return floor, ceiling, powers


def down_kernel(received, table, spectral, handed):
    sources = received.shape[0]
    size_y = sources * ROWS
    slabs = handed.shape[0]
    size_x = sources * WAVES
    slab = lax.axis_index("gz")
    row = lax.broadcasted_iota(jnp.int32, (sources, 8, 128), 1)
    group = lane_group((sources, 8, 128))
    extra = received[:, 8 * QUADS:, :]
    onward = jnp.concatenate([extra[1:], extra[:1]], 0)
    columns = []
    for q in range(QUADS):
        more = jnp.broadcast_to(onward[:, q:q + 1, :], (sources, 8, 128))
        values = received[:, 8 * q:8 * q + 8, :] + jnp.where(row == ROWS - 1, more, 0.0)
        columns.append(values.reshape(size_y, 128))
    first = jnp.broadcast_to(extra[:, 4:5, :], (sources, 8, 128))
    second = jnp.broadcast_to(extra[:, 5:6, :], (sources, 8, 128))
    layer = jnp.where(row < 4, first, second)
    layer = jnp.where((row % 4 == group) & (slab > 0), layer, 0.0)
    columns.append(layer.reshape(size_y, 128))
    waves = span_product(table, jnp.concatenate(columns, 1))

    last = waves[:, 128 * QUADS:]
    last = last + pltpu.roll(last, 64, 1)
    last = (last + pltpu.roll(last, 32, 1)).reshape(size_y // 32, 4, 8, 128)
    modes = size_y // 4
    mode_group = lane_group((modes, 128))
    pick = [last[:, i].reshape(modes, 128) for i in range(4)]
    layers = [
        jnp.where(
            mode_group < 2,
            jnp.where(mode_group == 0, pick[0], pick[1]),
            jnp.where(mode_group == 2, pick[2], pick[3]),
        )
    ]
    for q in range(QUADS):
        block = waves[:, 128 * q:128 * (q + 1)].reshape(size_y // 32, 4, 8, 128)
        layers += swap_groups([block[:, i].reshape(modes, 128) for i in range(4)])
    modes = size_y // 4
    line_y = table[pl.ds(2 * size_y, modes), :]
    a = table[pl.ds(2 * size_y + modes + lax.axis_index("gy"), 1), :] + line_y
    sinh = jnp.sqrt(a * (1.0 + 0.25 * a))
    lam = 1.0 / (1.0 + 0.5 * a + sinh)
    floor, ceiling, powers = wall_factors(lam, slab, slabs)
    spectral[LAYERS + 1] = lam
    whole = powers[LAYERS]
    for _ in range((slabs - 1).bit_length()):
        whole = whole * whole
    zero = a == 0.0
    weight = (-1.0 / (size_x * size_y)) / jnp.where(zero, 1.0, 2.0 * sinh * (1.0 - whole))
    spectral[LAYERS + 2] = jnp.where(zero, 0.0, weight)
    upward = jnp.zeros_like(lam)
    downward = jnp.zeros_like(lam)
    for l in range(LAYERS + 1):
        spectral[l] = layers[l]
        upward = lam * upward + floor[l] * layers[l]
        m = LAYERS - l
        downward = lam * downward + ceiling[m] * layers[m]
    for d in range(slabs):
        handed[d] = jnp.where(d > slab, upward, downward)


def up_kernel(spectral, handed, table, message):
    sources = message.shape[0]
    size_y = sources * ROWS
    slabs = handed.shape[0]
    size_x = sources * WAVES
    size_z = slabs * LAYERS
    slab = lax.axis_index("gz")
    lam = spectral[LAYERS + 1]
    weight = spectral[LAYERS + 2]
    floor, ceiling, powers = wall_factors(lam, slab, slabs)
    scale = 1.0 / (size_x * size_y)
    reach = powers[LAYERS // 2]
    upward = jnp.zeros_like(lam)
    downward = jnp.zeros_like(lam)
    for d in range(slabs - 1):
        upward = jnp.where(d < slab, reach * upward + handed[d], upward)
        e = slabs - 1 - d
        downward = jnp.where(e > slab, reach * downward + handed[e], downward)
    below = []
    for l in range(LAYERS + 1):
        upward = (lam * upward if l else upward) + floor[l] * spectral[l]
        below.append(upward)
    pressure = [None] * (LAYERS + 1)
    for l in reversed(range(LAYERS + 1)):
        pressure[l] = weight * (ceiling[l] * below[l] + floor[l] * downward)
        if l == LAYERS:
            mean = (0.5 / size_z) * (below[l][:8] + downward[:8])
        downward = lam * (downward + ceiling[l] * spectral[l])
    modes = size_y // 4
    flat = jnp.zeros((8, 128), F32)
    first_zero = weight[:8] == 0.0
    for l in range(LAYERS + 1):
        if l:
            count = (slab * LAYERS + (l - 1)).astype(F32)
            flat = flat + (0.5 * below[l - 1][:8] - count * mean)
        pressure[l] = jnp.concatenate(
            [jnp.where(first_zero, flat * scale, pressure[l][:8]), pressure[l][8:]], 0
        )

    columns = []
    tall = (size_y // 32, 1, 8, 128)
    for q in range(QUADS):
        block = swap_groups(pressure[1 + 4 * q:5 + 4 * q])
        columns.append(jnp.concatenate([b.reshape(tall) for b in block], 1).reshape(size_y, 128))
    mode_group = lane_group((modes, 128))
    spread = []
    for i in range(4):
        part = jnp.where(mode_group == i, pressure[0], 0.0)
        part = part + pltpu.roll(part, 64, 1)
        spread.append((part + pltpu.roll(part, 32, 1)).reshape(tall))
    columns.append(jnp.concatenate(spread, 1).reshape(size_y, 128))
    values = span_product(table, jnp.concatenate(columns, 1))

    row = lax.broadcasted_iota(jnp.int32, (sources, 8, 128), 1)
    group = lane_group((sources, 8, 128))
    extra = jnp.zeros((sources, 8, 128), F32)
    for q in range(QUADS):
        block = values[:, 128 * q:128 * (q + 1)].reshape(sources, 8, 128)
        message[:, 8 * q:8 * q + 8, :] = block
        edge = jnp.concatenate([block[-1:], block[:-1]], 0)[:, ROWS - 1:ROWS, :]
        extra = jnp.where(row == q, jnp.broadcast_to(edge, extra.shape), extra)
    layer = values[:, 128 * QUADS:].reshape(sources, 8, 128)
    layer = jnp.where(row % 4 == group, layer, 0.0)
    layer = layer + pltpu.roll(layer, 7, 1)
    layer = layer + pltpu.roll(layer, 6, 1)
    extra = jnp.where(row == 4, jnp.broadcast_to(layer[:, 0:1, :], extra.shape), extra)
    extra = jnp.where(row == 5, jnp.broadcast_to(layer[:, 4:5, :], extra.shape), extra)
    message[:, 8 * QUADS:, :] = extra


def gradient_kernel(
    received, even_h, even_t, odd_h, odd_t, provisional_hbm, motion_hbm,
    provisional, motion, lines, pressure, row_p, layer_p, sems,
):
    fetched = start_copies(((provisional_hbm, provisional),), sems)
    size_x = provisional.shape[-1]
    for block in range(size_x // 128):
        for j, piece in enumerate(swap_groups([received[4 * block + i] for i in range(4)])):
            lines[j * PIECE:(j + 1) * PIECE, block * 128:(block + 1) * 128] = piece
    evens = product(lines[:, : size_x // 2], even_h[...], even_t[...], dot)
    odds = product(lines[:, size_x // 2:], odd_h[...], odd_t[...], dot_nt)
    lines[:, : size_x // 2] = evens + odds
    lines[:, size_x // 2:] = evens - odds
    for b in range(size_x // 128):
        lanes = pl.ds(b * 128, 128)
        for j in range(4):
            for q in range(QUADS):
                pressure[b, pl.ds(4 * q + j, ROWS, stride=LAYERS), :] = lines[pl.ds(j * PIECE + q * 8, 8), lanes]
            row_p[b, pl.ds(j, 4, stride=4), :] = lines[pl.ds(j * PIECE + 32, 4), lanes]
            layer_p[b, pl.ds(j, 2, stride=4), :] = lines[pl.ds(j * PIECE + 36, 2), lanes]
    fetched[0].wait()
    stored = []
    bottom = lax.broadcasted_iota(jnp.int32, (LAYERS, size_x), 0) == 0
    for y in range(ROWS):
        p = kept(pressure, y * LAYERS, LAYERS)
        before = kept(row_p, 0, LAYERS) if y == 0 else kept(pressure, (y - 1) * LAYERS, LAYERS)
        below = jnp.where(bottom, kept(layer_p, y, 1), pltpu.roll(p, 1, 0))
        slope_z = jnp.where(bottom & (lax.axis_index("gz") == 0), 0.0, p - below)
        motion[0, y] = provisional[0, y] - (p - pltpu.roll(p, 1, 1))
        motion[1, y] = provisional[1, y] - (p - before)
        motion[2, y] = provisional[2, y] - slope_z
        copy = pltpu.make_async_copy(motion.at[:, pl.ds(y, 1)], motion_hbm.at[:, pl.ds(y, 1)], sems.at[1 + y])
        copy.start()
        stored.append(copy)
    for copy in stored:
        copy.wait()


def shifted(value, axis, by, periodic):
    size = lax.axis_size(axis)
    pairs = [(i, (i + by) % size) for i in range(size) if periodic or 0 <= i + by < size]
    return lax.ppermute(value, axis, pairs)


def exchanged(pieces, axis):
    return lax.all_to_all(pieces, axis, split_axis=0, concat_axis=0, tiled=True)


def shape_of(*shape):
    return jax.ShapeDtypeStruct(shape, F32)


def on_device(dual_motion, dual_thermal, flow, base):
    size_x = dual_thermal.shape[-1]
    groups_y = lax.axis_size("gy")
    groups_z = lax.axis_size("gz")
    even, odd, table = tables(size_x, ROWS * groups_y)
    even_h, even_t = map(jnp.asarray, even)
    odd_h, odd_t = map(jnp.asarray, odd)
    modes = ROWS * groups_y // 4
    blocks = size_x // 128

    def hbm(value):
        return pltpu.with_memory_space_constraint(value, pltpu.HBM)

    def params(mib):
        return pltpu.CompilerParams(vmem_limit_bytes=mib << 20)

    table = jnp.asarray(table)
    rows = shape_of(5, LAYERS, size_x)
    layers = shape_of(5, ROWS, size_x)
    motion_shape = (3, ROWS, LAYERS, size_x)
    thermal_shape = motion_shape[1:]
    message_shape = (groups_y, PIECE, 128)
    fields = tuple(jax.ShapeDtypeStruct(a.shape, a.dtype) for a in (dual_motion, dual_thermal, flow, base))
    y_first, y_last, z_first, z_last, *fields = pl.pallas_call(
        sides_kernel,
        out_shape=(rows, rows, layers, layers, *fields),
        in_specs=[HBM] * 4,
        out_specs=(VMEM,) * 8,
        scratch_shapes=[pltpu.SemaphoreType.DMA((4,))],
        compiler_params=params(16),
        name="sides",
    )(*map(hbm, (dual_motion, dual_thermal, flow, base)))
    z_low = shifted(z_last, "gz", 1, False)
    z_high = shifted(z_first, "gz", -1, False)
    y_low = shifted(y_last, "gy", 1, True)
    y_high = shifted(y_first, "gy", -1, True)
    moved, row_factors, layer_factors = pl.pallas_call(
        inner_kernel,
        out_shape=(
            shape_of(4, *thermal_shape),
            shape_of(4, LAYERS, size_x),
            shape_of(4, ROWS, size_x),
        ),
        in_specs=[VMEM] * 4,
        out_specs=(VMEM,) * 3,
        compiler_params=params(16),
        cost_estimate=pl.CostEstimate(
            flops=80 * ROWS * LAYERS * size_x, transcendentals=0, bytes_accessed=10 << 20
        ),
        name="inner",
    )(*fields)
    provisional, thermal_out, message = pl.pallas_call(
        source_kernel,
        out_shape=(
            pltpu.HBM(motion_shape, F32),
            pltpu.HBM(thermal_shape, F32),
            shape_of(*message_shape),
        ),
        in_specs=[VMEM] * 11,
        out_specs=(HBM, HBM, VMEM),
        scratch_shapes=[
            pltpu.VMEM((4, *thermal_shape), F32),
            pltpu.VMEM((blocks, ROWS * LAYERS, 128), F32),
            pltpu.VMEM((4 * PIECE, size_x), F32),
            pltpu.VMEM((blocks, LAYERS, 128), F32),
            pltpu.VMEM((blocks, ROWS, 128), F32),
            pltpu.SemaphoreType.DMA((2,)),
        ],
        compiler_params=params(24),
        name="source",
    )(moved, row_factors, layer_factors, y_low, y_high, z_low, z_high, even_h, even_t, odd_h, odd_t)
    received = exchanged(message, "gy")
    spectral, handed = pl.pallas_call(
        down_kernel,
        out_shape=(shape_of(LAYERS + 3, modes, 128), shape_of(groups_z, modes, 128)),
        in_specs=[VMEM] * 2,
        out_specs=(VMEM,) * 2,
        compiler_params=params(16),
        name="down",
    )(received, table)
    handed = exchanged(handed, "gz")
    message = pl.pallas_call(
        up_kernel,
        out_shape=shape_of(*message_shape),
        in_specs=[VMEM] * 3,
        out_specs=VMEM,
        compiler_params=params(16),
        name="up",
    )(spectral, handed, table)
    received = exchanged(message, "gy")
    motion = pl.pallas_call(
        gradient_kernel,
        out_shape=pltpu.HBM(motion_shape, F32),
        in_specs=[VMEM] * 5 + [HBM],
        out_specs=HBM,
        scratch_shapes=[
            pltpu.VMEM(motion_shape, F32),
            pltpu.VMEM(motion_shape, F32),
            pltpu.VMEM((4 * PIECE, size_x), F32),
            pltpu.VMEM((blocks, ROWS * LAYERS, 128), F32),
            pltpu.VMEM((blocks, LAYERS, 128), F32),
            pltpu.VMEM((blocks, ROWS, 128), F32),
            pltpu.SemaphoreType.DMA((1 + ROWS,)),
        ],
        compiler_params=params(24),
        name="gradient",
    )(received, even_h, even_t, odd_h, odd_t, hbm(provisional))
    return motion, thermal_out


def solution(mesh):
    split_y = P(None, "gy", "gz", None)
    split_flat = P("gy", "gz", None)
    return jax.shard_map(
        on_device,
        mesh=mesh,
        in_specs=(split_y, split_flat, split_y, split_flat),
        out_specs=(split_y, split_flat),
        check_vma=False,
    )
```

```python
import functools

import jax
import jax.numpy as jnp
import ml_dtypes
import numpy as np
from jax import lax
from jax.experimental import pallas as pl
from jax.experimental.pallas import tpu as pltpu
from jax.sharding import PartitionSpec as P

F32 = jnp.float32
BF16 = jnp.bfloat16
ROWS = 8
LAYERS = 16
WAVES = 32
QUADS = LAYERS // 4
PIECE = 8 * (QUADS + 1)
VMEM = pl.BlockSpec(memory_space=pltpu.VMEM)
HBM = pl.BlockSpec(memory_space=pltpu.HBM)


def two_parts(table):
    head = table.astype(ml_dtypes.bfloat16)
    return head, (table - head.astype(np.float64)).astype(ml_dtypes.bfloat16)


def cas(phases, length):
    angles = (phases % length) * (2.0 * np.pi / length)
    return np.cos(angles) + np.sin(angles)


@functools.lru_cache(None)
def tables(size_x, size_y):
    half = np.arange(size_x // 2)
    even = two_parts(cas(half[:, None] * half[None, :], size_x // 2))
    odd = two_parts(cas(half[:, None] * (2 * half[None, :] + 1), size_x))
    full = np.arange(size_y)
    span = cas(full[:, None] * full[None, :], size_y)
    waves = np.concatenate([2 * half, 2 * half + 1])
    line_x = 4.0 * np.sin(np.pi * waves / size_x) ** 2
    line_x = np.tile(line_x.reshape(-1, WAVES), (1, 128 // WAVES))
    row = np.arange(size_y // 4)[:, None]
    lane = np.arange(128)[None, :]
    wave_y = 32 * (row // 8) + 8 * (lane // WAVES) + row % 8
    line_y = 4.0 * np.sin(np.pi * wave_y / size_y) ** 2
    halves = [span[:, n * 128:(n + 1) * 128] for n in range(size_y // 128)]
    return even, odd, np.concatenate(halves + [line_y, line_x], 0).astype(np.float32)


def split(values):
    head = values.astype(BF16)
    return head, (values - head.astype(F32)).astype(BF16)


def lane_group(shape):
    return lax.broadcasted_iota(jnp.int32, shape, len(shape) - 1) // WAVES


def swap_groups(a):
    axis = a[0].ndim - 1
    group = lane_group(a[0].shape)
    low = group < 2
    even = group % 2 == 0
    b0 = jnp.where(low, a[0], pltpu.roll(a[2], 64, axis))
    b2 = jnp.where(low, pltpu.roll(a[0], 64, axis), a[2])
    b1 = jnp.where(low, a[1], pltpu.roll(a[3], 64, axis))
    b3 = jnp.where(low, pltpu.roll(a[1], 64, axis), a[3])
    return (
        jnp.where(even, b0, pltpu.roll(b1, 32, axis)),
        jnp.where(even, pltpu.roll(b0, 96, axis), b1),
        jnp.where(even, b2, pltpu.roll(b3, 32, axis)),
        jnp.where(even, pltpu.roll(b2, 96, axis), b3),
    )


def dot(a, b):
    return jnp.dot(a, b, preferred_element_type=F32)


def dot_nt(a, b):
    return lax.dot_general(a, b, (((1,), (1,)), ((), ())), preferred_element_type=F32)


def product(values, head, tail, how):
    a, b = split(values)
    return how(a, head) + (how(b, head) + how(a, tail))


def keep(ref, start, values):
    for b in range(ref.shape[0]):
        ref[b, pl.ds(start, values.shape[0]), :] = values[:, b * 128:(b + 1) * 128]


def kept(ref, start, count):
    return jnp.concatenate([ref[b, pl.ds(start, count), :] for b in range(ref.shape[0])], 1)


def start_copies(pairs, sems):
    copies = [pltpu.make_async_copy(a, b, sems.at[n]) for n, (a, b) in enumerate(pairs)]
    for copy in copies:
        copy.start()
    return copies


def sides_kernel(
    motion_hbm, thermal_hbm, base_hbm, y_first, y_last, z_first, z_last, motion, thermal, base, sems
):
    pairs = ((base_hbm, base), (thermal_hbm, thermal), (motion_hbm, motion))
    fetched = start_copies(pairs, sems)
    fetched[0].wait()
    for y in range(ROWS):
        warm = base[y].astype(F32)
        z_first[4, y:y + 1, :] = warm[:1]
        z_last[4, y:y + 1, :] = warm[LAYERS - 1:]
        if y in (0, ROWS - 1):
            (y_last if y else y_first)[4] = warm
    fetched[1].wait()
    y_first[3] = thermal[0]
    y_last[3] = thermal[ROWS - 1]
    for y in range(ROWS):
        z_first[3, y:y + 1, :] = thermal[y, :1, :]
        z_last[3, y:y + 1, :] = thermal[y, LAYERS - 1:, :]
    fetched[2].wait()
    for c in range(3):
        y_first[c] = motion[c, 0]
        y_last[c] = motion[c, ROWS - 1]
        for y in range(ROWS):
            z_first[c, y:y + 1, :] = motion[c, y, :1, :]
            z_last[c, y:y + 1, :] = motion[c, y, LAYERS - 1:, :]


def inner_kernel(motion, thermal, flow, base, moved, row_factors, layer_factors):
    size_x = motion.shape[-1]
    row = lax.broadcasted_iota(jnp.int32, (LAYERS, size_x), 0)
    top = row == LAYERS - 1
    bottom = row == 0

    def field(c, y):
        if c < 3:
            return motion[c, y]
        if c == 3:
            return thermal[y]
        return base[y].astype(F32)

    def neighbours(c, y):
        centre = field(c, y)
        y_plus = field(c, y + 1) if y < ROWS - 1 else None
        y_minus = field(c, y - 1) if y > 0 else None
        z_plus = jnp.where(top, 0.0, pltpu.roll(centre, LAYERS - 1, 0))
        z_minus = jnp.where(bottom, 0.0, pltpu.roll(centre, 1, 0))
        x_plus = pltpu.roll(centre, size_x - 1, 1)
        x_minus = pltpu.roll(centre, 1, 1)
        return centre, x_plus, x_minus, y_plus, y_minus, z_plus, z_minus

    for y in range(ROWS):
        weights = []
        for c in range(3):
            speed = flow[c, y].astype(F32) * 0.1
            weights += [0.02 + speed, 0.02 - speed]
        _, hx, gx, hy, gy, hz, gz = neighbours(4, y)
        slope_y = -gy if hy is None else hy if gy is None else hy - gy
        slopes = (hx - gx, slope_y, hz - gz)
        heat = thermal[y] * 0.1
        if y == 0:
            row_factors[0] = weights[3]
            row_factors[1] = -heat
        if y == ROWS - 1:
            row_factors[2] = weights[2]
            row_factors[3] = heat
        layer_factors[0, y:y + 1, :] = weights[5][:1]
        layer_factors[1, y:y + 1, :] = -heat[:1]
        layer_factors[2, y:y + 1, :] = weights[4][LAYERS - 1:]
        layer_factors[3, y:y + 1, :] = heat[LAYERS - 1:]
        for c in range(4):
            parts = neighbours(c, y)
            value = parts[0] * 0.88
            for weight, part in zip(weights, parts[1:]):
                if part is not None:
                    value = value + weight * part
            moved[c, y] = value + (heat * slopes[c] if c < 3 else 0.2 * motion[2, y])


def source_kernel(
    moved, row_factors, layer_factors, y_low, y_high, z_low, z_high, even_h, even_t, odd_h, odd_t,
    provisional, thermal_hbm, message, thermal, source, lines, row_p, layer_p, sems
):
    size_x = moved.shape[-1]
    row = lax.broadcasted_iota(jnp.int32, (8, size_x), 0)
    top = lax.broadcasted_iota(jnp.int32, (LAYERS, size_x), 0) == LAYERS - 1
    lows = [layer_factors[0] * z_low[c] for c in range(4)]
    highs = [layer_factors[2] * z_high[c] for c in range(4)]
    lows[2] = lows[2] + layer_factors[1] * z_low[4]
    highs[2] = highs[2] + layer_factors[3] * z_high[4]
    carried = None
    for y in range(ROWS):
        for c in range(4):
            value = moved[c, y]
            if y == 0:
                value = value + row_factors[0] * y_low[c]
                if c == 1:
                    value = value + row_factors[1] * y_low[4]
            if y == ROWS - 1:
                value = value + row_factors[2] * y_high[c]
                if c == 1:
                    value = value + row_factors[3] * y_high[4]
            out = provisional.at[c, y] if c < 3 else thermal.at[y]
            out[:8] = value[:8] + jnp.where(row == 0, lows[c][y:y + 1], 0.0)
            out[8:] = value[8:] + jnp.where(row == 7, highs[c][y:y + 1], 0.0)
        p0, p1, p2 = (provisional[c, y] for c in range(3))
        if y == 0:
            keep(row_p, 0, p1)
        else:
            keep(source, (y - 1) * LAYERS, carried + p1)
        keep(layer_p, y, p2[0:1, :])
        above = jnp.where(top, 0.0, pltpu.roll(p2, LAYERS - 1, 0))
        carried = (pltpu.roll(p0, size_x - 1, 1) - p0) - p1 + (above - p2)
    keep(source, (ROWS - 1) * LAYERS, carried)
    stored = start_copies(((thermal, thermal_hbm),), sems)

    for b in range(size_x // 128):
        lanes = pl.ds(b * 128, 128)
        for j in range(4):
            for q in range(QUADS):
                lines[pl.ds(j * PIECE + q * 8, 8), lanes] = source[b, pl.ds(4 * q + j, ROWS, stride=LAYERS), :]
            lines[pl.ds(j * PIECE + 32, 4), lanes] = row_p[b, pl.ds(j, 4, stride=4), :]
            lines[pl.ds(j * PIECE + 36, 2), lanes] = layer_p[b, pl.ds(j, 2, stride=4), :]
            lines[pl.ds(j * PIECE + 38, 2), lanes] = jnp.zeros((2, 128), F32)
    near = lines[:, : size_x // 2]
    far = lines[:, size_x // 2:]
    half = size_x // 256
    for turn in range(2):
        if turn == 0:
            waves = product(near + far, even_h[...], even_t[...], dot)
        else:
            waves = product(near - far, odd_h[...], odd_t[...], dot)
        for block in range(half):
            a = [waves[j * PIECE:(j + 1) * PIECE, block * 128:(block + 1) * 128] for j in range(4)]
            for i, piece in enumerate(swap_groups(a)):
                message[4 * (turn * half + block) + i] = piece
    for copy in stored:
        copy.wait()


def span_product(table, values):
    size_y = values.shape[0]
    wide = jnp.concatenate([table[pl.ds(n * size_y, size_y), :] for n in range(size_y // 128)], 1)
    left = split(wide)
    right = split(values)
    return dot(left[0], right[0]) + (dot(left[0], right[1]) + dot(left[1], right[0]))


def wall_factors(lam, slab, slabs):
    square = lam * lam
    powers = [jnp.ones_like(lam), square]
    for m in range(2, LAYERS + 1):
        powers.append(powers[m // 2] * powers[m - m // 2])
    step = powers[LAYERS]

    def raised(count):
        value = lam
        factor = step
        for bit in range((slabs - 1).bit_length()):
            value = jnp.where((count // (1 << bit)) % 2 == 1, value * factor, value)
            factor = factor * factor
        return value

    low = raised(slab)
    high = raised(slabs - 1 - slab)
    below = low * (1.0 / square)
    floor = [1.0 + jnp.where(slab == 0, lam, below)] + [1.0 + low * powers[l] for l in range(LAYERS)]
    ceiling = [1.0 + high * powers[LAYERS - 1 - l] for l in range(-1, LAYERS)]
    return floor, ceiling, powers


def down_kernel(received, table, spectral, handed):
    sources = received.shape[0]
    size_y = sources * ROWS
    slabs = handed.shape[0]
    size_x = sources * WAVES
    slab = lax.axis_index("gz")
    row = lax.broadcasted_iota(jnp.int32, (sources, 8, 128), 1)
    group = lane_group((sources, 8, 128))
    extra = received[:, 8 * QUADS:, :]
    onward = jnp.concatenate([extra[1:], extra[:1]], 0)
    columns = []
    for q in range(QUADS):
        more = jnp.broadcast_to(onward[:, q:q + 1, :], (sources, 8, 128))
        values = received[:, 8 * q:8 * q + 8, :] + jnp.where(row == ROWS - 1, more, 0.0)
        columns.append(values.reshape(size_y, 128))
    first = jnp.broadcast_to(extra[:, 4:5, :], (sources, 8, 128))
    second = jnp.broadcast_to(extra[:, 5:6, :], (sources, 8, 128))
    layer = jnp.where(row < 4, first, second)
    layer = jnp.where((row % 4 == group) & (slab > 0), layer, 0.0)
    columns.append(layer.reshape(size_y, 128))
    waves = span_product(table, jnp.concatenate(columns, 1))

    last = waves[:, 128 * QUADS:]
    last = last + pltpu.roll(last, 64, 1)
    last = (last + pltpu.roll(last, 32, 1)).reshape(size_y // 32, 4, 8, 128)
    modes = size_y // 4
    mode_group = lane_group((modes, 128))
    pick = [last[:, i].reshape(modes, 128) for i in range(4)]
    layers = [
        jnp.where(
            mode_group < 2,
            jnp.where(mode_group == 0, pick[0], pick[1]),
            jnp.where(mode_group == 2, pick[2], pick[3]),
        )
    ]
    for q in range(QUADS):
        block = waves[:, 128 * q:128 * (q + 1)].reshape(size_y // 32, 4, 8, 128)
        layers += swap_groups([block[:, i].reshape(modes, 128) for i in range(4)])
    modes = size_y // 4
    line_y = table[pl.ds(2 * size_y, modes), :]
    a = table[pl.ds(2 * size_y + modes + lax.axis_index("gy"), 1), :] + line_y
    sinh = jnp.sqrt(a * (1.0 + 0.25 * a))
    lam = 1.0 / (1.0 + 0.5 * a + sinh)
    floor, ceiling, powers = wall_factors(lam, slab, slabs)
    spectral[LAYERS + 1] = lam
    whole = powers[LAYERS]
    for _ in range((slabs - 1).bit_length()):
        whole = whole * whole
    zero = a == 0.0
    weight = (-1.0 / (size_x * size_y)) / jnp.where(zero, 1.0, 2.0 * sinh * (1.0 - whole))
    spectral[LAYERS + 2] = jnp.where(zero, 0.0, weight)
    upward = jnp.zeros_like(lam)
    downward = jnp.zeros_like(lam)
    for l in range(LAYERS + 1):
        spectral[l] = layers[l]
        upward = lam * upward + floor[l] * layers[l]
        m = LAYERS - l
        downward = lam * downward + ceiling[m] * layers[m]
    for d in range(slabs):
        handed[d] = jnp.where(d > slab, upward, downward)


def up_kernel(spectral, handed, table, message):
    sources = message.shape[0]
    size_y = sources * ROWS
    slabs = handed.shape[0]
    size_x = sources * WAVES
    size_z = slabs * LAYERS
    slab = lax.axis_index("gz")
    lam = spectral[LAYERS + 1]
    weight = spectral[LAYERS + 2]
    floor, ceiling, powers = wall_factors(lam, slab, slabs)
    scale = 1.0 / (size_x * size_y)
    reach = powers[LAYERS // 2]
    upward = jnp.zeros_like(lam)
    downward = jnp.zeros_like(lam)
    for d in range(slabs - 1):
        upward = jnp.where(d < slab, reach * upward + handed[d], upward)
        e = slabs - 1 - d
        downward = jnp.where(e > slab, reach * downward + handed[e], downward)
    below = []
    for l in range(LAYERS + 1):
        upward = (lam * upward if l else upward) + floor[l] * spectral[l]
        below.append(upward)
    pressure = [None] * (LAYERS + 1)
    for l in reversed(range(LAYERS + 1)):
        pressure[l] = weight * (ceiling[l] * below[l] + floor[l] * downward)
        if l == LAYERS:
            mean = (0.5 / size_z) * (below[l][:8] + downward[:8])
        downward = lam * (downward + ceiling[l] * spectral[l])
    modes = size_y // 4
    flat = jnp.zeros((8, 128), F32)
    first_zero = weight[:8] == 0.0
    for l in range(LAYERS + 1):
        if l:
            count = (slab * LAYERS + (l - 1)).astype(F32)
            flat = flat + (0.5 * below[l - 1][:8] - count * mean)
        pressure[l] = jnp.concatenate(
            [jnp.where(first_zero, flat * scale, pressure[l][:8]), pressure[l][8:]], 0
        )

    columns = []
    tall = (size_y // 32, 1, 8, 128)
    for q in range(QUADS):
        block = swap_groups(pressure[1 + 4 * q:5 + 4 * q])
        columns.append(jnp.concatenate([b.reshape(tall) for b in block], 1).reshape(size_y, 128))
    mode_group = lane_group((modes, 128))
    spread = []
    for i in range(4):
        part = jnp.where(mode_group == i, pressure[0], 0.0)
        part = part + pltpu.roll(part, 64, 1)
        spread.append((part + pltpu.roll(part, 32, 1)).reshape(tall))
    columns.append(jnp.concatenate(spread, 1).reshape(size_y, 128))
    values = span_product(table, jnp.concatenate(columns, 1))

    row = lax.broadcasted_iota(jnp.int32, (sources, 8, 128), 1)
    group = lane_group((sources, 8, 128))
    extra = jnp.zeros((sources, 8, 128), F32)
    for q in range(QUADS):
        block = values[:, 128 * q:128 * (q + 1)].reshape(sources, 8, 128)
        message[:, 8 * q:8 * q + 8, :] = block
        edge = jnp.concatenate([block[-1:], block[:-1]], 0)[:, ROWS - 1:ROWS, :]
        extra = jnp.where(row == q, jnp.broadcast_to(edge, extra.shape), extra)
    layer = values[:, 128 * QUADS:].reshape(sources, 8, 128)
    layer = jnp.where(row % 4 == group, layer, 0.0)
    layer = layer + pltpu.roll(layer, 7, 1)
    layer = layer + pltpu.roll(layer, 6, 1)
    extra = jnp.where(row == 4, jnp.broadcast_to(layer[:, 0:1, :], extra.shape), extra)
    extra = jnp.where(row == 5, jnp.broadcast_to(layer[:, 4:5, :], extra.shape), extra)
    message[:, 8 * QUADS:, :] = extra


def gradient_kernel(
    received, even_h, even_t, odd_h, odd_t, provisional, motion_hbm,
    motion, lines, pressure, row_p, layer_p, sems,
):
    size_x = provisional.shape[-1]
    for block in range(size_x // 128):
        for j, piece in enumerate(swap_groups([received[4 * block + i] for i in range(4)])):
            lines[j * PIECE:(j + 1) * PIECE, block * 128:(block + 1) * 128] = piece
    evens = product(lines[:, : size_x // 2], even_h[...], even_t[...], dot)
    odds = product(lines[:, size_x // 2:], odd_h[...], odd_t[...], dot_nt)
    lines[:, : size_x // 2] = evens + odds
    lines[:, size_x // 2:] = evens - odds
    for b in range(size_x // 128):
        lanes = pl.ds(b * 128, 128)
        for j in range(4):
            for q in range(QUADS):
                pressure[b, pl.ds(4 * q + j, ROWS, stride=LAYERS), :] = lines[pl.ds(j * PIECE + q * 8, 8), lanes]
            row_p[b, pl.ds(j, 4, stride=4), :] = lines[pl.ds(j * PIECE + 32, 4), lanes]
            layer_p[b, pl.ds(j, 2, stride=4), :] = lines[pl.ds(j * PIECE + 36, 2), lanes]
    stored = []
    bottom = lax.broadcasted_iota(jnp.int32, (LAYERS, size_x), 0) == 0
    for y in range(ROWS):
        p = kept(pressure, y * LAYERS, LAYERS)
        before = kept(row_p, 0, LAYERS) if y == 0 else kept(pressure, (y - 1) * LAYERS, LAYERS)
        below = jnp.where(bottom, kept(layer_p, y, 1), pltpu.roll(p, 1, 0))
        slope_z = jnp.where(bottom & (lax.axis_index("gz") == 0), 0.0, p - below)
        motion[0, y] = provisional[0, y] - (p - pltpu.roll(p, 1, 1))
        motion[1, y] = provisional[1, y] - (p - before)
        motion[2, y] = provisional[2, y] - slope_z
        copy = pltpu.make_async_copy(motion.at[:, pl.ds(y, 1)], motion_hbm.at[:, pl.ds(y, 1)], sems.at[y])
        copy.start()
        stored.append(copy)
    for copy in stored:
        copy.wait()


def shifted(value, axis, by, periodic):
    size = lax.axis_size(axis)
    pairs = [(i, (i + by) % size) for i in range(size) if periodic or 0 <= i + by < size]
    return lax.ppermute(value, axis, pairs)


def exchanged(pieces, axis):
    return lax.all_to_all(pieces, axis, split_axis=0, concat_axis=0, tiled=True)


def shape_of(*shape):
    return jax.ShapeDtypeStruct(shape, F32)


def on_device(dual_motion, dual_thermal, flow, base):
    size_x = dual_thermal.shape[-1]
    groups_y = lax.axis_size("gy")
    groups_z = lax.axis_size("gz")
    even, odd, table = tables(size_x, ROWS * groups_y)
    even_h, even_t = map(jnp.asarray, even)
    odd_h, odd_t = map(jnp.asarray, odd)
    modes = ROWS * groups_y // 4
    blocks = size_x // 128

    def hbm(value):
        return pltpu.with_memory_space_constraint(value, pltpu.HBM)

    def params(mib):
        return pltpu.CompilerParams(vmem_limit_bytes=mib << 20)

    table = jnp.asarray(table)
    rows = shape_of(5, LAYERS, size_x)
    layers = shape_of(5, ROWS, size_x)
    motion_shape = (3, ROWS, LAYERS, size_x)
    thermal_shape = motion_shape[1:]
    message_shape = (groups_y, PIECE, 128)
    fields = tuple(jax.ShapeDtypeStruct(a.shape, a.dtype) for a in (dual_motion, dual_thermal, base))
    y_first, y_last, z_first, z_last, motion, thermal, base = pl.pallas_call(
        sides_kernel,
        out_shape=(rows, rows, layers, layers, *fields),
        in_specs=[HBM] * 3,
        out_specs=(VMEM,) * 7,
        scratch_shapes=[pltpu.SemaphoreType.DMA((3,))],
        compiler_params=params(16),
        name="sides",
    )(*map(hbm, (dual_motion, dual_thermal, base)))
    z_low = shifted(z_last, "gz", 1, False)
    z_high = shifted(z_first, "gz", -1, False)
    y_low = shifted(y_last, "gy", 1, True)
    y_high = shifted(y_first, "gy", -1, True)
    moved, row_factors, layer_factors = pl.pallas_call(
        inner_kernel,
        out_shape=(
            shape_of(4, *thermal_shape),
            shape_of(4, LAYERS, size_x),
            shape_of(4, ROWS, size_x),
        ),
        in_specs=[VMEM] * 4,
        out_specs=(VMEM,) * 3,
        compiler_params=params(16),
        cost_estimate=pl.CostEstimate(
            flops=80 * ROWS * LAYERS * size_x, transcendentals=0, bytes_accessed=10 << 20
        ),
        name="inner",
    )(motion, thermal, flow, base)
    provisional, thermal_out, message = pl.pallas_call(
        source_kernel,
        out_shape=(
            shape_of(*motion_shape),
            pltpu.HBM(thermal_shape, F32),
            shape_of(*message_shape),
        ),
        in_specs=[VMEM] * 11,
        out_specs=(VMEM, HBM, VMEM),
        scratch_shapes=[
            pltpu.VMEM(thermal_shape, F32),
            pltpu.VMEM((blocks, ROWS * LAYERS, 128), F32),
            pltpu.VMEM((4 * PIECE, size_x), F32),
            pltpu.VMEM((blocks, LAYERS, 128), F32),
            pltpu.VMEM((blocks, ROWS, 128), F32),
            pltpu.SemaphoreType.DMA((1,)),
        ],
        compiler_params=params(24),
        name="source",
    )(moved, row_factors, layer_factors, y_low, y_high, z_low, z_high, even_h, even_t, odd_h, odd_t)
    received = exchanged(message, "gy")
    spectral, handed = pl.pallas_call(
        down_kernel,
        out_shape=(shape_of(LAYERS + 3, modes, 128), shape_of(groups_z, modes, 128)),
        in_specs=[VMEM] * 2,
        out_specs=(VMEM,) * 2,
        compiler_params=params(16),
        name="down",
    )(received, table)
    handed = exchanged(handed, "gz")
    message = pl.pallas_call(
        up_kernel,
        out_shape=shape_of(*message_shape),
        in_specs=[VMEM] * 3,
        out_specs=VMEM,
        compiler_params=params(16),
        name="up",
    )(spectral, handed, table)
    received = exchanged(message, "gy")
    motion = pl.pallas_call(
        gradient_kernel,
        out_shape=pltpu.HBM(motion_shape, F32),
        in_specs=[VMEM] * 6,
        out_specs=HBM,
        scratch_shapes=[
            pltpu.VMEM(motion_shape, F32),
            pltpu.VMEM((4 * PIECE, size_x), F32),
            pltpu.VMEM((blocks, ROWS * LAYERS, 128), F32),
            pltpu.VMEM((blocks, LAYERS, 128), F32),
            pltpu.VMEM((blocks, ROWS, 128), F32),
            pltpu.SemaphoreType.DMA((ROWS,)),
        ],
        compiler_params=params(24),
        name="gradient",
    )(received, even_h, even_t, odd_h, odd_t, provisional)
    return motion, thermal_out


def solution(mesh):
    split_y = P(None, "gy", "gz", None)
    split_flat = P("gy", "gz", None)
    return jax.shard_map(
        on_device,
        mesh=mesh,
        in_specs=(split_y, split_flat, split_y, split_flat),
        out_specs=(split_y, split_flat),
        check_vma=False,
    )
```

```python
import functools

import jax
import jax.numpy as jnp
import ml_dtypes
import numpy as np
from jax import lax
from jax.experimental import pallas as pl
from jax.experimental.pallas import tpu as pltpu
from jax.sharding import PartitionSpec as P

F32 = jnp.float32
BF16 = jnp.bfloat16
ROWS = 8
LAYERS = 16
WAVES = 32
QUADS = LAYERS // 4
PIECE = 8 * (QUADS + 1)
VMEM = pl.BlockSpec(memory_space=pltpu.VMEM)
HBM = pl.BlockSpec(memory_space=pltpu.HBM)


def two_parts(table):
    head = table.astype(ml_dtypes.bfloat16)
    return head, (table - head.astype(np.float64)).astype(ml_dtypes.bfloat16)


def cas(phases, length):
    angles = (phases % length) * (2.0 * np.pi / length)
    return np.cos(angles) + np.sin(angles)


@functools.lru_cache(None)
def tables(size_x, size_y):
    half = np.arange(size_x // 2)
    even = two_parts(cas(half[:, None] * half[None, :], size_x // 2))
    odd = two_parts(cas(half[:, None] * (2 * half[None, :] + 1), size_x))
    full = np.arange(size_y)
    span = cas(full[:, None] * full[None, :], size_y)
    waves = np.concatenate([2 * half, 2 * half + 1])
    line_x = 4.0 * np.sin(np.pi * waves / size_x) ** 2
    line_x = np.tile(line_x.reshape(-1, WAVES), (1, 128 // WAVES))
    row = np.arange(size_y // 4)[:, None]
    lane = np.arange(128)[None, :]
    wave_y = 32 * (row // 8) + 8 * (lane // WAVES) + row % 8
    line_y = 4.0 * np.sin(np.pi * wave_y / size_y) ** 2
    halves = [span[:, n * 128:(n + 1) * 128] for n in range(size_y // 128)]
    return even, odd, np.concatenate(halves + [line_y, line_x], 0).astype(np.float32)


def split(values):
    head = values.astype(BF16)
    return head, (values - head.astype(F32)).astype(BF16)


def lane_group(shape):
    return lax.broadcasted_iota(jnp.int32, shape, len(shape) - 1) // WAVES


def swap_groups(a):
    axis = a[0].ndim - 1
    group = lane_group(a[0].shape)
    low = group < 2
    even = group % 2 == 0
    b0 = jnp.where(low, a[0], pltpu.roll(a[2], 64, axis))
    b2 = jnp.where(low, pltpu.roll(a[0], 64, axis), a[2])
    b1 = jnp.where(low, a[1], pltpu.roll(a[3], 64, axis))
    b3 = jnp.where(low, pltpu.roll(a[1], 64, axis), a[3])
    return (
        jnp.where(even, b0, pltpu.roll(b1, 32, axis)),
        jnp.where(even, pltpu.roll(b0, 96, axis), b1),
        jnp.where(even, b2, pltpu.roll(b3, 32, axis)),
        jnp.where(even, pltpu.roll(b2, 96, axis), b3),
    )


def dot(a, b):
    return jnp.dot(a, b, preferred_element_type=F32)


def dot_nt(a, b):
    return lax.dot_general(a, b, (((1,), (1,)), ((), ())), preferred_element_type=F32)


def product(values, head, tail, how):
    a, b = split(values)
    return how(a, head) + (how(b, head) + how(a, tail))


def keep(ref, start, values):
    for b in range(ref.shape[0]):
        ref[b, pl.ds(start, values.shape[0]), :] = values[:, b * 128:(b + 1) * 128]


def kept(ref, start, count):
    return jnp.concatenate([ref[b, pl.ds(start, count), :] for b in range(ref.shape[0])], 1)


def start_copies(pairs, sems):
    copies = [pltpu.make_async_copy(a, b, sems.at[n]) for n, (a, b) in enumerate(pairs)]
    for copy in copies:
        copy.start()
    return copies


def odd(axis):
    return lax.axis_index(axis) % 2 == 1


def sides_kernel(
    motion_hbm, thermal_hbm, base_hbm, row_near, row_far, layer_near, layer_far, motion, thermal, base, sems
):
    pairs = ((base_hbm, base), (thermal_hbm, thermal), (motion_hbm, motion))
    fetched = start_copies(pairs, sems)
    is_odd = odd("gz")
    near = jnp.where(odd("gy"), 0, ROWS - 1)
    far = ROWS - 1 - near

    def edges(first, last):
        return jnp.where(is_odd, first, last), jnp.where(is_odd, last, first)

    fetched[0].wait()
    row_near[4] = base[near].astype(F32)
    row_far[4] = base[far].astype(F32)
    for y in range(ROWS):
        warm = base[y].astype(F32)
        layer_near[4, y:y + 1, :], layer_far[4, y:y + 1, :] = edges(warm[:1], warm[LAYERS - 1:])
    fetched[1].wait()
    row_near[3] = thermal[near]
    row_far[3] = thermal[far]
    for y in range(ROWS):
        layer_near[3, y:y + 1, :], layer_far[3, y:y + 1, :] = edges(thermal[y, :1, :], thermal[y, LAYERS - 1:, :])
    fetched[2].wait()
    for c in range(3):
        row_near[c] = motion[c, near]
        row_far[c] = motion[c, far]
        for y in range(ROWS):
            layer_near[c, y:y + 1, :], layer_far[c, y:y + 1, :] = edges(
                motion[c, y, :1, :], motion[c, y, LAYERS - 1:, :]
            )


def inner_kernel(motion, thermal, flow, base, moved, row_factors, layer_factors):
    size_x = motion.shape[-1]
    row = lax.broadcasted_iota(jnp.int32, (LAYERS, size_x), 0)
    top = row == LAYERS - 1
    bottom = row == 0

    def field(c, y):
        if c < 3:
            return motion[c, y]
        if c == 3:
            return thermal[y]
        return base[y].astype(F32)

    def neighbours(c, y):
        centre = field(c, y)
        y_plus = field(c, y + 1) if y < ROWS - 1 else None
        y_minus = field(c, y - 1) if y > 0 else None
        z_plus = jnp.where(top, 0.0, pltpu.roll(centre, LAYERS - 1, 0))
        z_minus = jnp.where(bottom, 0.0, pltpu.roll(centre, 1, 0))
        x_plus = pltpu.roll(centre, size_x - 1, 1)
        x_minus = pltpu.roll(centre, 1, 1)
        return centre, x_plus, x_minus, y_plus, y_minus, z_plus, z_minus

    for y in range(ROWS):
        weights = []
        for c in range(3):
            speed = flow[c, y].astype(F32) * 0.1
            weights += [0.02 + speed, 0.02 - speed]
        _, hx, gx, hy, gy, hz, gz = neighbours(4, y)
        slope_y = -gy if hy is None else hy if gy is None else hy - gy
        slopes = (hx - gx, slope_y, hz - gz)
        heat = thermal[y] * 0.1
        if y == 0:
            row_factors[0] = weights[3]
            row_factors[1] = -heat
        if y == ROWS - 1:
            row_factors[2] = weights[2]
            row_factors[3] = heat
        layer_factors[0, y:y + 1, :] = weights[5][:1]
        layer_factors[1, y:y + 1, :] = -heat[:1]
        layer_factors[2, y:y + 1, :] = weights[4][LAYERS - 1:]
        layer_factors[3, y:y + 1, :] = heat[LAYERS - 1:]
        for c in range(4):
            parts = neighbours(c, y)
            value = parts[0] * 0.88
            for weight, part in zip(weights, parts[1:]):
                if part is not None:
                    value = value + weight * part
            moved[c, y] = value + (heat * slopes[c] if c < 3 else 0.2 * motion[2, y])


def source_kernel(
    moved, row_factors, layer_factors, row_near, row_far, layer_near, layer_far,
    even_h, even_t, odd_h, odd_t,
    provisional, thermal_hbm, message, thermal, source, lines, row_p, layer_p, sems
):
    size_x = moved.shape[-1]
    row = lax.broadcasted_iota(jnp.int32, (8, size_x), 0)
    top = lax.broadcasted_iota(jnp.int32, (LAYERS, size_x), 0) == LAYERS - 1
    odd_y, odd_z = odd("gy"), odd("gz")
    y_low = [jnp.where(odd_y, row_near[c], row_far[c]) for c in range(5)]
    y_high = [jnp.where(odd_y, row_far[c], row_near[c]) for c in range(5)]
    z_low = [jnp.where(odd_z, layer_near[c], layer_far[c]) for c in range(5)]
    z_high = [jnp.where(odd_z, layer_far[c], layer_near[c]) for c in range(5)]
    lows = [layer_factors[0] * z_low[c] for c in range(4)]
    highs = [layer_factors[2] * z_high[c] for c in range(4)]
    lows[2] = lows[2] + layer_factors[1] * z_low[4]
    highs[2] = highs[2] + layer_factors[3] * z_high[4]
    carried = None
    for y in range(ROWS):
        for c in range(4):
            value = moved[c, y]
            if y == 0:
                value = value + row_factors[0] * y_low[c]
                if c == 1:
                    value = value + row_factors[1] * y_low[4]
            if y == ROWS - 1:
                value = value + row_factors[2] * y_high[c]
                if c == 1:
                    value = value + row_factors[3] * y_high[4]
            out = provisional.at[c, y] if c < 3 else thermal.at[y]
            out[:8] = value[:8] + jnp.where(row == 0, lows[c][y:y + 1], 0.0)
            out[8:] = value[8:] + jnp.where(row == 7, highs[c][y:y + 1], 0.0)
        p0, p1, p2 = (provisional[c, y] for c in range(3))
        if y == 0:
            keep(row_p, 0, p1)
        else:
            keep(source, (y - 1) * LAYERS, carried + p1)
        keep(layer_p, y, p2[0:1, :])
        above = jnp.where(top, 0.0, pltpu.roll(p2, LAYERS - 1, 0))
        carried = (pltpu.roll(p0, size_x - 1, 1) - p0) - p1 + (above - p2)
    keep(source, (ROWS - 1) * LAYERS, carried)
    stored = start_copies(((thermal, thermal_hbm),), sems)

    for b in range(size_x // 128):
        lanes = pl.ds(b * 128, 128)
        for j in range(4):
            for q in range(QUADS):
                lines[pl.ds(j * PIECE + q * 8, 8), lanes] = source[b, pl.ds(4 * q + j, ROWS, stride=LAYERS), :]
            lines[pl.ds(j * PIECE + 32, 4), lanes] = row_p[b, pl.ds(j, 4, stride=4), :]
            lines[pl.ds(j * PIECE + 36, 2), lanes] = layer_p[b, pl.ds(j, 2, stride=4), :]
            lines[pl.ds(j * PIECE + 38, 2), lanes] = jnp.zeros((2, 128), F32)
    near = lines[:, : size_x // 2]
    far = lines[:, size_x // 2:]
    half = size_x // 256
    for turn in range(2):
        if turn == 0:
            waves = product(near + far, even_h[...], even_t[...], dot)
        else:
            waves = product(near - far, odd_h[...], odd_t[...], dot)
        for block in range(half):
            a = [waves[j * PIECE:(j + 1) * PIECE, block * 128:(block + 1) * 128] for j in range(4)]
            for i, piece in enumerate(swap_groups(a)):
                message[4 * (turn * half + block) + i] = piece
    for copy in stored:
        copy.wait()


def span_product(table, values):
    size_y = values.shape[0]
    wide = jnp.concatenate([table[pl.ds(n * size_y, size_y), :] for n in range(size_y // 128)], 1)
    left = split(wide)
    right = split(values)
    return dot(left[0], right[0]) + (dot(left[0], right[1]) + dot(left[1], right[0]))


def wall_factors(lam, slab, slabs):
    square = lam * lam
    powers = [jnp.ones_like(lam), square]
    for m in range(2, LAYERS + 1):
        powers.append(powers[m // 2] * powers[m - m // 2])
    step = powers[LAYERS]

    def raised(count):
        value = lam
        factor = step
        for bit in range((slabs - 1).bit_length()):
            value = jnp.where((count // (1 << bit)) % 2 == 1, value * factor, value)
            factor = factor * factor
        return value

    low = raised(slab)
    high = raised(slabs - 1 - slab)
    below = low * (1.0 / square)
    floor = [1.0 + jnp.where(slab == 0, lam, below)] + [1.0 + low * powers[l] for l in range(LAYERS)]
    ceiling = [1.0 + high * powers[LAYERS - 1 - l] for l in range(-1, LAYERS)]
    return floor, ceiling, powers


def down_kernel(received, table, spectral, handed):
    sources = received.shape[0]
    size_y = sources * ROWS
    slabs = handed.shape[0]
    size_x = sources * WAVES
    slab = lax.axis_index("gz")
    row = lax.broadcasted_iota(jnp.int32, (sources, 8, 128), 1)
    group = lane_group((sources, 8, 128))
    extra = received[:, 8 * QUADS:, :]
    onward = jnp.concatenate([extra[1:], extra[:1]], 0)
    columns = []
    for q in range(QUADS):
        more = jnp.broadcast_to(onward[:, q:q + 1, :], (sources, 8, 128))
        values = received[:, 8 * q:8 * q + 8, :] + jnp.where(row == ROWS - 1, more, 0.0)
        columns.append(values.reshape(size_y, 128))
    first = jnp.broadcast_to(extra[:, 4:5, :], (sources, 8, 128))
    second = jnp.broadcast_to(extra[:, 5:6, :], (sources, 8, 128))
    layer = jnp.where(row < 4, first, second)
    layer = jnp.where((row % 4 == group) & (slab > 0), layer, 0.0)
    columns.append(layer.reshape(size_y, 128))
    waves = span_product(table, jnp.concatenate(columns, 1))

    last = waves[:, 128 * QUADS:]
    last = last + pltpu.roll(last, 64, 1)
    last = (last + pltpu.roll(last, 32, 1)).reshape(size_y // 32, 4, 8, 128)
    modes = size_y // 4
    mode_group = lane_group((modes, 128))
    pick = [last[:, i].reshape(modes, 128) for i in range(4)]
    layers = [
        jnp.where(
            mode_group < 2,
            jnp.where(mode_group == 0, pick[0], pick[1]),
            jnp.where(mode_group == 2, pick[2], pick[3]),
        )
    ]
    for q in range(QUADS):
        block = waves[:, 128 * q:128 * (q + 1)].reshape(size_y // 32, 4, 8, 128)
        layers += swap_groups([block[:, i].reshape(modes, 128) for i in range(4)])
    modes = size_y // 4
    line_y = table[pl.ds(2 * size_y, modes), :]
    a = table[pl.ds(2 * size_y + modes + lax.axis_index("gy"), 1), :] + line_y
    sinh = jnp.sqrt(a * (1.0 + 0.25 * a))
    lam = 1.0 / (1.0 + 0.5 * a + sinh)
    floor, ceiling, powers = wall_factors(lam, slab, slabs)
    spectral[LAYERS + 1] = lam
    whole = powers[LAYERS]
    for _ in range((slabs - 1).bit_length()):
        whole = whole * whole
    zero = a == 0.0
    weight = (-1.0 / (size_x * size_y)) / jnp.where(zero, 1.0, 2.0 * sinh * (1.0 - whole))
    spectral[LAYERS + 2] = jnp.where(zero, 0.0, weight)
    upward = jnp.zeros_like(lam)
    downward = jnp.zeros_like(lam)
    for l in range(LAYERS + 1):
        spectral[l] = layers[l]
        upward = lam * upward + floor[l] * layers[l]
        m = LAYERS - l
        downward = lam * downward + ceiling[m] * layers[m]
    for d in range(slabs):
        handed[d] = jnp.where(d > slab, upward, downward)


def up_kernel(spectral, handed, table, message):
    sources = message.shape[0]
    size_y = sources * ROWS
    slabs = handed.shape[0]
    size_x = sources * WAVES
    size_z = slabs * LAYERS
    slab = lax.axis_index("gz")
    lam = spectral[LAYERS + 1]
    weight = spectral[LAYERS + 2]
    floor, ceiling, powers = wall_factors(lam, slab, slabs)
    scale = 1.0 / (size_x * size_y)
    reach = powers[LAYERS // 2]
    upward = jnp.zeros_like(lam)
    downward = jnp.zeros_like(lam)
    for d in range(slabs - 1):
        upward = jnp.where(d < slab, reach * upward + handed[d], upward)
        e = slabs - 1 - d
        downward = jnp.where(e > slab, reach * downward + handed[e], downward)
    below = []
    for l in range(LAYERS + 1):
        upward = (lam * upward if l else upward) + floor[l] * spectral[l]
        below.append(upward)
    pressure = [None] * (LAYERS + 1)
    for l in reversed(range(LAYERS + 1)):
        pressure[l] = weight * (ceiling[l] * below[l] + floor[l] * downward)
        if l == LAYERS:
            mean = (0.5 / size_z) * (below[l][:8] + downward[:8])
        downward = lam * (downward + ceiling[l] * spectral[l])
    modes = size_y // 4
    flat = jnp.zeros((8, 128), F32)
    first_zero = weight[:8] == 0.0
    for l in range(LAYERS + 1):
        if l:
            count = (slab * LAYERS + (l - 1)).astype(F32)
            flat = flat + (0.5 * below[l - 1][:8] - count * mean)
        pressure[l] = jnp.concatenate(
            [jnp.where(first_zero, flat * scale, pressure[l][:8]), pressure[l][8:]], 0
        )

    columns = []
    tall = (size_y // 32, 1, 8, 128)
    for q in range(QUADS):
        block = swap_groups(pressure[1 + 4 * q:5 + 4 * q])
        columns.append(jnp.concatenate([b.reshape(tall) for b in block], 1).reshape(size_y, 128))
    mode_group = lane_group((modes, 128))
    spread = []
    for i in range(4):
        part = jnp.where(mode_group == i, pressure[0], 0.0)
        part = part + pltpu.roll(part, 64, 1)
        spread.append((part + pltpu.roll(part, 32, 1)).reshape(tall))
    columns.append(jnp.concatenate(spread, 1).reshape(size_y, 128))
    values = span_product(table, jnp.concatenate(columns, 1))

    row = lax.broadcasted_iota(jnp.int32, (sources, 8, 128), 1)
    group = lane_group((sources, 8, 128))
    extra = jnp.zeros((sources, 8, 128), F32)
    for q in range(QUADS):
        block = values[:, 128 * q:128 * (q + 1)].reshape(sources, 8, 128)
        message[:, 8 * q:8 * q + 8, :] = block
        edge = jnp.concatenate([block[-1:], block[:-1]], 0)[:, ROWS - 1:ROWS, :]
        extra = jnp.where(row == q, jnp.broadcast_to(edge, extra.shape), extra)
    layer = values[:, 128 * QUADS:].reshape(sources, 8, 128)
    layer = jnp.where(row % 4 == group, layer, 0.0)
    layer = layer + pltpu.roll(layer, 7, 1)
    layer = layer + pltpu.roll(layer, 6, 1)
    extra = jnp.where(row == 4, jnp.broadcast_to(layer[:, 0:1, :], extra.shape), extra)
    extra = jnp.where(row == 5, jnp.broadcast_to(layer[:, 4:5, :], extra.shape), extra)
    message[:, 8 * QUADS:, :] = extra


def gradient_kernel(
    received, even_h, even_t, odd_h, odd_t, provisional, motion_hbm,
    motion, lines, pressure, row_p, layer_p, sems,
):
    size_x = provisional.shape[-1]
    for block in range(size_x // 128):
        for j, piece in enumerate(swap_groups([received[4 * block + i] for i in range(4)])):
            lines[j * PIECE:(j + 1) * PIECE, block * 128:(block + 1) * 128] = piece
    evens = product(lines[:, : size_x // 2], even_h[...], even_t[...], dot)
    odds = product(lines[:, size_x // 2:], odd_h[...], odd_t[...], dot_nt)
    lines[:, : size_x // 2] = evens + odds
    lines[:, size_x // 2:] = evens - odds
    for b in range(size_x // 128):
        lanes = pl.ds(b * 128, 128)
        for j in range(4):
            for q in range(QUADS):
                pressure[b, pl.ds(4 * q + j, ROWS, stride=LAYERS), :] = lines[pl.ds(j * PIECE + q * 8, 8), lanes]
            row_p[b, pl.ds(j, 4, stride=4), :] = lines[pl.ds(j * PIECE + 32, 4), lanes]
            layer_p[b, pl.ds(j, 2, stride=4), :] = lines[pl.ds(j * PIECE + 36, 2), lanes]
    stored = []
    bottom = lax.broadcasted_iota(jnp.int32, (LAYERS, size_x), 0) == 0
    for y in range(ROWS):
        p = kept(pressure, y * LAYERS, LAYERS)
        before = kept(row_p, 0, LAYERS) if y == 0 else kept(pressure, (y - 1) * LAYERS, LAYERS)
        below = jnp.where(bottom, kept(layer_p, y, 1), pltpu.roll(p, 1, 0))
        slope_z = jnp.where(bottom & (lax.axis_index("gz") == 0), 0.0, p - below)
        motion[0, y] = provisional[0, y] - (p - pltpu.roll(p, 1, 1))
        motion[1, y] = provisional[1, y] - (p - before)
        motion[2, y] = provisional[2, y] - slope_z
        copy = pltpu.make_async_copy(motion.at[:, pl.ds(y, 1)], motion_hbm.at[:, pl.ds(y, 1)], sems.at[y])
        copy.start()
        stored.append(copy)
    for copy in stored:
        copy.wait()


def swapped(value, axis, first, periodic):
    size = lax.axis_size(axis)
    pairs = []
    for i in range(first, size, 2):
        if periodic or i + 1 < size:
            pairs += [(i, (i + 1) % size), ((i + 1) % size, i)]
    return lax.ppermute(value, axis, pairs)


def exchanged(pieces, axis):
    return lax.all_to_all(pieces, axis, split_axis=0, concat_axis=0, tiled=True)


def shape_of(*shape):
    return jax.ShapeDtypeStruct(shape, F32)


def on_device(dual_motion, dual_thermal, flow, base):
    size_x = dual_thermal.shape[-1]
    groups_y = lax.axis_size("gy")
    groups_z = lax.axis_size("gz")
    evens, odds, table = tables(size_x, ROWS * groups_y)
    even_h, even_t = map(jnp.asarray, evens)
    odd_h, odd_t = map(jnp.asarray, odds)
    modes = ROWS * groups_y // 4
    blocks = size_x // 128

    def hbm(value):
        return pltpu.with_memory_space_constraint(value, pltpu.HBM)

    def params(mib):
        return pltpu.CompilerParams(vmem_limit_bytes=mib << 20)

    table = jnp.asarray(table)
    rows = shape_of(5, LAYERS, size_x)
    layers = shape_of(5, ROWS, size_x)
    motion_shape = (3, ROWS, LAYERS, size_x)
    thermal_shape = motion_shape[1:]
    message_shape = (groups_y, PIECE, 128)
    fields = tuple(jax.ShapeDtypeStruct(a.shape, a.dtype) for a in (dual_motion, dual_thermal, base))
    row_near, row_far, layer_near, layer_far, motion, thermal, base = pl.pallas_call(
        sides_kernel,
        out_shape=(rows, rows, layers, layers, *fields),
        in_specs=[HBM] * 3,
        out_specs=(VMEM,) * 7,
        scratch_shapes=[pltpu.SemaphoreType.DMA((3,))],
        compiler_params=params(16),
        name="sides",
    )(*map(hbm, (dual_motion, dual_thermal, base)))
    row_near = swapped(row_near, "gy", 0, True)
    row_far = swapped(row_far, "gy", 1, True)
    layer_near = swapped(layer_near, "gz", 0, False)
    layer_far = swapped(layer_far, "gz", 1, False)
    moved, row_factors, layer_factors = pl.pallas_call(
        inner_kernel,
        out_shape=(
            shape_of(4, *thermal_shape),
            shape_of(4, LAYERS, size_x),
            shape_of(4, ROWS, size_x),
        ),
        in_specs=[VMEM] * 4,
        out_specs=(VMEM,) * 3,
        compiler_params=params(16),
        cost_estimate=pl.CostEstimate(
            flops=80 * ROWS * LAYERS * size_x, transcendentals=0, bytes_accessed=10 << 20
        ),
        name="inner",
    )(motion, thermal, flow, base)
    provisional, thermal_out, message = pl.pallas_call(
        source_kernel,
        out_shape=(
            shape_of(*motion_shape),
            pltpu.HBM(thermal_shape, F32),
            shape_of(*message_shape),
        ),
        in_specs=[VMEM] * 11,
        out_specs=(VMEM, HBM, VMEM),
        scratch_shapes=[
            pltpu.VMEM(thermal_shape, F32),
            pltpu.VMEM((blocks, ROWS * LAYERS, 128), F32),
            pltpu.VMEM((4 * PIECE, size_x), F32),
            pltpu.VMEM((blocks, LAYERS, 128), F32),
            pltpu.VMEM((blocks, ROWS, 128), F32),
            pltpu.SemaphoreType.DMA((1,)),
        ],
        compiler_params=params(24),
        name="source",
    )(
        moved, row_factors, layer_factors, row_near, row_far, layer_near, layer_far,
        even_h, even_t, odd_h, odd_t,
    )
    received = exchanged(message, "gy")
    spectral, handed = pl.pallas_call(
        down_kernel,
        out_shape=(shape_of(LAYERS + 3, modes, 128), shape_of(groups_z, modes, 128)),
        in_specs=[VMEM] * 2,
        out_specs=(VMEM,) * 2,
        compiler_params=params(16),
        name="down",
    )(received, table)
    handed = exchanged(handed, "gz")
    message = pl.pallas_call(
        up_kernel,
        out_shape=shape_of(*message_shape),
        in_specs=[VMEM] * 3,
        out_specs=VMEM,
        compiler_params=params(16),
        name="up",
    )(spectral, handed, table)
    received = exchanged(message, "gy")
    motion = pl.pallas_call(
        gradient_kernel,
        out_shape=pltpu.HBM(motion_shape, F32),
        in_specs=[VMEM] * 6,
        out_specs=HBM,
        scratch_shapes=[
            pltpu.VMEM(motion_shape, F32),
            pltpu.VMEM((4 * PIECE, size_x), F32),
            pltpu.VMEM((blocks, ROWS * LAYERS, 128), F32),
            pltpu.VMEM((blocks, LAYERS, 128), F32),
            pltpu.VMEM((blocks, ROWS, 128), F32),
            pltpu.SemaphoreType.DMA((ROWS,)),
        ],
        compiler_params=params(24),
        name="gradient",
    )(received, even_h, even_t, odd_h, odd_t, provisional)
    return motion, thermal_out


def solution(mesh):
    split_y = P(None, "gy", "gz", None)
    split_flat = P("gy", "gz", None)
    return jax.shard_map(
        on_device,
        mesh=mesh,
        in_specs=(split_y, split_flat, split_y, split_flat),
        out_specs=(split_y, split_flat),
        check_vma=False,
    )
```

```python
import functools

import jax
import jax.numpy as jnp
import ml_dtypes
import numpy as np
from jax import lax
from jax.experimental import pallas as pl
from jax.experimental.pallas import tpu as pltpu
from jax.sharding import PartitionSpec as P

F32 = jnp.float32
BF16 = jnp.bfloat16
ROWS = 8
LAYERS = 16
WAVES = 32
QUADS = LAYERS // 4
PIECE = 8 * (QUADS + 1)
VMEM = pl.BlockSpec(memory_space=pltpu.VMEM)
HBM = pl.BlockSpec(memory_space=pltpu.HBM)


def two_parts(table):
    head = table.astype(ml_dtypes.bfloat16)
    return head, (table - head.astype(np.float64)).astype(ml_dtypes.bfloat16)


def cas(phases, length):
    angles = (phases % length) * (2.0 * np.pi / length)
    return np.cos(angles) + np.sin(angles)


@functools.lru_cache(None)
def tables(size_x, size_y):
    half = np.arange(size_x // 2)
    even = two_parts(cas(half[:, None] * half[None, :], size_x // 2))
    odd = two_parts(cas(half[:, None] * (2 * half[None, :] + 1), size_x))
    full = np.arange(size_y)
    span = cas(full[:, None] * full[None, :], size_y)
    waves = np.concatenate([2 * half, 2 * half + 1])
    line_x = 4.0 * np.sin(np.pi * waves / size_x) ** 2
    line_x = np.tile(line_x.reshape(-1, WAVES), (1, 128 // WAVES))
    row = np.arange(size_y // 4)[:, None]
    lane = np.arange(128)[None, :]
    wave_y = 32 * (row // 8) + 8 * (lane // WAVES) + row % 8
    line_y = 4.0 * np.sin(np.pi * wave_y / size_y) ** 2
    halves = [span[:, n * 128:(n + 1) * 128] for n in range(size_y // 128)]
    return even, odd, np.concatenate(halves + [line_y, line_x], 0).astype(np.float32)


def split(values):
    head = values.astype(BF16)
    return head, (values - head.astype(F32)).astype(BF16)


def lane_group(shape):
    return lax.broadcasted_iota(jnp.int32, shape, len(shape) - 1) // WAVES


def swap_groups(a):
    axis = a[0].ndim - 1
    group = lane_group(a[0].shape)
    low = group < 2
    even = group % 2 == 0
    b0 = jnp.where(low, a[0], pltpu.roll(a[2], 64, axis))
    b2 = jnp.where(low, pltpu.roll(a[0], 64, axis), a[2])
    b1 = jnp.where(low, a[1], pltpu.roll(a[3], 64, axis))
    b3 = jnp.where(low, pltpu.roll(a[1], 64, axis), a[3])
    return (
        jnp.where(even, b0, pltpu.roll(b1, 32, axis)),
        jnp.where(even, pltpu.roll(b0, 96, axis), b1),
        jnp.where(even, b2, pltpu.roll(b3, 32, axis)),
        jnp.where(even, pltpu.roll(b2, 96, axis), b3),
    )


def dot(a, b):
    return jnp.dot(a, b, preferred_element_type=F32)


def dot_nt(a, b):
    return lax.dot_general(a, b, (((1,), (1,)), ((), ())), preferred_element_type=F32)


def product(values, head, tail, how):
    a, b = split(values)
    both = how(jnp.concatenate([a, b], 0), head)
    count = values.shape[0]
    return both[:count] + (both[count:] + how(a, tail))


def keep(ref, start, values):
    for b in range(ref.shape[0]):
        ref[b, pl.ds(start, values.shape[0]), :] = values[:, b * 128:(b + 1) * 128]


def kept(ref, start, count):
    return jnp.concatenate([ref[b, pl.ds(start, count), :] for b in range(ref.shape[0])], 1)


def start_copies(pairs, sems):
    copies = [pltpu.make_async_copy(a, b, sems.at[n]) for n, (a, b) in enumerate(pairs)]
    for copy in copies:
        copy.start()
    return copies


def odd(axis):
    return lax.axis_index(axis) % 2 == 1


def sides_kernel(
    motion_hbm, thermal_hbm, base_hbm, row_near, row_far, layer_near, layer_far, motion, thermal, base, sems
):
    pairs = ((base_hbm, base), (thermal_hbm, thermal), (motion_hbm, motion))
    fetched = start_copies(pairs, sems)
    is_odd = odd("gz")
    near = jnp.where(odd("gy"), 0, ROWS - 1)
    far = ROWS - 1 - near

    def edges(first, last):
        return jnp.where(is_odd, first, last), jnp.where(is_odd, last, first)

    fetched[0].wait()
    row_near[4] = base[near].astype(F32)
    row_far[4] = base[far].astype(F32)
    for y in range(ROWS):
        warm = base[y].astype(F32)
        layer_near[4, y:y + 1, :], layer_far[4, y:y + 1, :] = edges(warm[:1], warm[LAYERS - 1:])
    fetched[1].wait()
    row_near[3] = thermal[near]
    row_far[3] = thermal[far]
    for y in range(ROWS):
        layer_near[3, y:y + 1, :], layer_far[3, y:y + 1, :] = edges(thermal[y, :1, :], thermal[y, LAYERS - 1:, :])
    fetched[2].wait()
    for c in range(3):
        row_near[c] = motion[c, near]
        row_far[c] = motion[c, far]
        for y in range(ROWS):
            layer_near[c, y:y + 1, :], layer_far[c, y:y + 1, :] = edges(
                motion[c, y, :1, :], motion[c, y, LAYERS - 1:, :]
            )


def inner_kernel(motion, thermal, flow, base, moved, row_factors, layer_factors):
    size_x = motion.shape[-1]
    row = lax.broadcasted_iota(jnp.int32, (LAYERS, size_x), 0)
    top = row == LAYERS - 1
    bottom = row == 0

    def field(c, y):
        if c < 3:
            return motion[c, y]
        if c == 3:
            return thermal[y]
        return base[y].astype(F32)

    def neighbours(c, y):
        centre = field(c, y)
        y_plus = field(c, y + 1) if y < ROWS - 1 else None
        y_minus = field(c, y - 1) if y > 0 else None
        z_plus = jnp.where(top, 0.0, pltpu.roll(centre, LAYERS - 1, 0))
        z_minus = jnp.where(bottom, 0.0, pltpu.roll(centre, 1, 0))
        x_plus = pltpu.roll(centre, size_x - 1, 1)
        x_minus = pltpu.roll(centre, 1, 1)
        return centre, x_plus, x_minus, y_plus, y_minus, z_plus, z_minus

    for y in range(ROWS):
        weights = []
        for c in range(3):
            speed = flow[c, y].astype(F32) * 0.1
            weights += [0.02 + speed, 0.02 - speed]
        _, hx, gx, hy, gy, hz, gz = neighbours(4, y)
        slope_y = -gy if hy is None else hy if gy is None else hy - gy
        slopes = (hx - gx, slope_y, hz - gz)
        heat = thermal[y] * 0.1
        if y == 0:
            row_factors[0] = weights[3]
            row_factors[1] = -heat
        if y == ROWS - 1:
            row_factors[2] = weights[2]
            row_factors[3] = heat
        layer_factors[0, y:y + 1, :] = weights[5][:1]
        layer_factors[1, y:y + 1, :] = -heat[:1]
        layer_factors[2, y:y + 1, :] = weights[4][LAYERS - 1:]
        layer_factors[3, y:y + 1, :] = heat[LAYERS - 1:]
        for c in range(4):
            parts = neighbours(c, y)
            value = parts[0] * 0.88
            for weight, part in zip(weights, parts[1:]):
                if part is not None:
                    value = value + weight * part
            moved[c, y] = value + (heat * slopes[c] if c < 3 else 0.2 * motion[2, y])


def source_kernel(
    moved, row_factors, layer_factors, layer_far, layer_near, row_far, row_near,
    even_h, even_t, odd_h, odd_t,
    provisional, thermal_hbm, message, thermal, source, lines, row_p, layer_p, sems
):
    size_x = moved.shape[-1]
    row = lax.broadcasted_iota(jnp.int32, (8, size_x), 0)
    top = lax.broadcasted_iota(jnp.int32, (LAYERS, size_x), 0) == LAYERS - 1
    odd_y, odd_z = odd("gy"), odd("gz")
    y_low = [jnp.where(odd_y, row_near[c], row_far[c]) for c in range(5)]
    y_high = [jnp.where(odd_y, row_far[c], row_near[c]) for c in range(5)]
    z_low = [jnp.where(odd_z, layer_near[c], layer_far[c]) for c in range(5)]
    z_high = [jnp.where(odd_z, layer_far[c], layer_near[c]) for c in range(5)]
    lows = [layer_factors[0] * z_low[c] for c in range(4)]
    highs = [layer_factors[2] * z_high[c] for c in range(4)]
    lows[2] = lows[2] + layer_factors[1] * z_low[4]
    highs[2] = highs[2] + layer_factors[3] * z_high[4]
    carried = None
    for y in range(ROWS):
        for c in range(4):
            value = moved[c, y]
            if y == 0:
                value = value + row_factors[0] * y_low[c]
                if c == 1:
                    value = value + row_factors[1] * y_low[4]
            if y == ROWS - 1:
                value = value + row_factors[2] * y_high[c]
                if c == 1:
                    value = value + row_factors[3] * y_high[4]
            out = provisional.at[c, y] if c < 3 else thermal.at[y]
            out[:8] = value[:8] + jnp.where(row == 0, lows[c][y:y + 1], 0.0)
            out[8:] = value[8:] + jnp.where(row == 7, highs[c][y:y + 1], 0.0)
        p0, p1, p2 = (provisional[c, y] for c in range(3))
        if y == 0:
            keep(row_p, 0, p1)
        else:
            keep(source, (y - 1) * LAYERS, carried + p1)
        keep(layer_p, y, p2[0:1, :])
        above = jnp.where(top, 0.0, pltpu.roll(p2, LAYERS - 1, 0))
        carried = (pltpu.roll(p0, size_x - 1, 1) - p0) - p1 + (above - p2)
    keep(source, (ROWS - 1) * LAYERS, carried)
    stored = start_copies(((thermal, thermal_hbm),), sems)

    for b in range(size_x // 128):
        lanes = pl.ds(b * 128, 128)
        for j in range(4):
            for q in range(QUADS):
                lines[pl.ds(j * PIECE + q * 8, 8), lanes] = source[b, pl.ds(4 * q + j, ROWS, stride=LAYERS), :]
            lines[pl.ds(j * PIECE + 32, 4), lanes] = row_p[b, pl.ds(j, 4, stride=4), :]
            lines[pl.ds(j * PIECE + 36, 2), lanes] = layer_p[b, pl.ds(j, 2, stride=4), :]
            lines[pl.ds(j * PIECE + 38, 2), lanes] = jnp.zeros((2, 128), F32)
    near = lines[:, : size_x // 2]
    far = lines[:, size_x // 2:]
    half = size_x // 256
    for turn in range(2):
        if turn == 0:
            waves = product(near + far, even_h[...], even_t[...], dot)
        else:
            waves = product(near - far, odd_h[...], odd_t[...], dot)
        for block in range(half):
            a = [waves[j * PIECE:(j + 1) * PIECE, block * 128:(block + 1) * 128] for j in range(4)]
            for i, piece in enumerate(swap_groups(a)):
                message[4 * (turn * half + block) + i] = piece
    for copy in stored:
        copy.wait()


def span_product(table, values):
    size_y = values.shape[0]
    wide = jnp.concatenate([table[pl.ds(n * size_y, size_y), :] for n in range(size_y // 128)], 1)
    left = split(wide)
    right = split(values)
    both = dot(jnp.concatenate(left, 0), right[0])
    return both[:size_y] + (both[size_y:] + dot(left[0], right[1]))


def wall_factors(lam, slab, slabs):
    square = lam * lam
    powers = [jnp.ones_like(lam), square]
    for m in range(2, LAYERS + 1):
        powers.append(powers[m // 2] * powers[m - m // 2])
    step = powers[LAYERS]

    def raised(count):
        value = lam
        factor = step
        for bit in range((slabs - 1).bit_length()):
            value = jnp.where((count // (1 << bit)) % 2 == 1, value * factor, value)
            factor = factor * factor
        return value

    low = raised(slab)
    high = raised(slabs - 1 - slab)
    below = low * (1.0 / square)
    floor = [1.0 + jnp.where(slab == 0, lam, below)] + [1.0 + low * powers[l] for l in range(LAYERS)]
    ceiling = [1.0 + high * powers[LAYERS - 1 - l] for l in range(-1, LAYERS)]
    return floor, ceiling, powers


def down_kernel(received, table, spectral, handed):
    sources = received.shape[0]
    size_y = sources * ROWS
    slabs = handed.shape[0]
    size_x = sources * WAVES
    slab = lax.axis_index("gz")
    row = lax.broadcasted_iota(jnp.int32, (sources, 8, 128), 1)
    group = lane_group((sources, 8, 128))
    extra = received[:, 8 * QUADS:, :]
    onward = jnp.concatenate([extra[1:], extra[:1]], 0)
    columns = []
    for q in range(QUADS):
        more = jnp.broadcast_to(onward[:, q:q + 1, :], (sources, 8, 128))
        values = received[:, 8 * q:8 * q + 8, :] + jnp.where(row == ROWS - 1, more, 0.0)
        columns.append(values.reshape(size_y, 128))
    first = jnp.broadcast_to(extra[:, 4:5, :], (sources, 8, 128))
    second = jnp.broadcast_to(extra[:, 5:6, :], (sources, 8, 128))
    layer = jnp.where(row < 4, first, second)
    layer = jnp.where((row % 4 == group) & (slab > 0), layer, 0.0)
    columns.append(layer.reshape(size_y, 128))
    waves = span_product(table, jnp.concatenate(columns, 1))

    last = waves[:, 128 * QUADS:]
    last = last + pltpu.roll(last, 64, 1)
    last = (last + pltpu.roll(last, 32, 1)).reshape(size_y // 32, 4, 8, 128)
    modes = size_y // 4
    mode_group = lane_group((modes, 128))
    pick = [last[:, i].reshape(modes, 128) for i in range(4)]
    layers = [
        jnp.where(
            mode_group < 2,
            jnp.where(mode_group == 0, pick[0], pick[1]),
            jnp.where(mode_group == 2, pick[2], pick[3]),
        )
    ]
    for q in range(QUADS):
        block = waves[:, 128 * q:128 * (q + 1)].reshape(size_y // 32, 4, 8, 128)
        layers += swap_groups([block[:, i].reshape(modes, 128) for i in range(4)])
    modes = size_y // 4
    line_y = table[pl.ds(2 * size_y, modes), :]
    a = table[pl.ds(2 * size_y + modes + lax.axis_index("gy"), 1), :] + line_y
    sinh = jnp.sqrt(a * (1.0 + 0.25 * a))
    lam = 1.0 / (1.0 + 0.5 * a + sinh)
    floor, ceiling, powers = wall_factors(lam, slab, slabs)
    spectral[LAYERS + 1] = lam
    whole = powers[LAYERS]
    for _ in range((slabs - 1).bit_length()):
        whole = whole * whole
    zero = a == 0.0
    weight = (-1.0 / (size_x * size_y)) / jnp.where(zero, 1.0, 2.0 * sinh * (1.0 - whole))
    spectral[LAYERS + 2] = jnp.where(zero, 0.0, weight)
    upward = jnp.zeros_like(lam)
    downward = jnp.zeros_like(lam)
    for l in range(LAYERS + 1):
        spectral[l] = layers[l]
        upward = lam * upward + floor[l] * layers[l]
        m = LAYERS - l
        downward = lam * downward + ceiling[m] * layers[m]
    for d in range(slabs):
        handed[d] = jnp.where(d > slab, upward, downward)


def up_kernel(spectral, handed, table, message):
    sources = message.shape[0]
    size_y = sources * ROWS
    slabs = handed.shape[0]
    size_x = sources * WAVES
    size_z = slabs * LAYERS
    slab = lax.axis_index("gz")
    lam = spectral[LAYERS + 1]
    weight = spectral[LAYERS + 2]
    floor, ceiling, powers = wall_factors(lam, slab, slabs)
    scale = 1.0 / (size_x * size_y)
    reach = powers[LAYERS // 2]
    upward = jnp.zeros_like(lam)
    downward = jnp.zeros_like(lam)
    for d in range(slabs - 1):
        upward = jnp.where(d < slab, reach * upward + handed[d], upward)
        e = slabs - 1 - d
        downward = jnp.where(e > slab, reach * downward + handed[e], downward)
    below = []
    for l in range(LAYERS + 1):
        upward = (lam * upward if l else upward) + floor[l] * spectral[l]
        below.append(upward)
    pressure = [None] * (LAYERS + 1)
    for l in reversed(range(LAYERS + 1)):
        pressure[l] = weight * (ceiling[l] * below[l] + floor[l] * downward)
        if l == LAYERS:
            mean = (0.5 / size_z) * (below[l][:8] + downward[:8])
        downward = lam * (downward + ceiling[l] * spectral[l])
    modes = size_y // 4
    flat = jnp.zeros((8, 128), F32)
    first_zero = weight[:8] == 0.0
    for l in range(LAYERS + 1):
        if l:
            count = (slab * LAYERS + (l - 1)).astype(F32)
            flat = flat + (0.5 * below[l - 1][:8] - count * mean)
        pressure[l] = jnp.concatenate(
            [jnp.where(first_zero, flat * scale, pressure[l][:8]), pressure[l][8:]], 0
        )

    columns = []
    tall = (size_y // 32, 1, 8, 128)
    for q in range(QUADS):
        block = swap_groups(pressure[1 + 4 * q:5 + 4 * q])
        columns.append(jnp.concatenate([b.reshape(tall) for b in block], 1).reshape(size_y, 128))
    mode_group = lane_group((modes, 128))
    spread = []
    for i in range(4):
        part = jnp.where(mode_group == i, pressure[0], 0.0)
        part = part + pltpu.roll(part, 64, 1)
        spread.append((part + pltpu.roll(part, 32, 1)).reshape(tall))
    columns.append(jnp.concatenate(spread, 1).reshape(size_y, 128))
    values = span_product(table, jnp.concatenate(columns, 1))

    row = lax.broadcasted_iota(jnp.int32, (sources, 8, 128), 1)
    group = lane_group((sources, 8, 128))
    extra = jnp.zeros((sources, 8, 128), F32)
    for q in range(QUADS):
        block = values[:, 128 * q:128 * (q + 1)].reshape(sources, 8, 128)
        message[:, 8 * q:8 * q + 8, :] = block
        edge = jnp.concatenate([block[-1:], block[:-1]], 0)[:, ROWS - 1:ROWS, :]
        extra = jnp.where(row == q, jnp.broadcast_to(edge, extra.shape), extra)
    layer = values[:, 128 * QUADS:].reshape(sources, 8, 128)
    layer = jnp.where(row % 4 == group, layer, 0.0)
    layer = layer + pltpu.roll(layer, 7, 1)
    layer = layer + pltpu.roll(layer, 6, 1)
    extra = jnp.where(row == 4, jnp.broadcast_to(layer[:, 0:1, :], extra.shape), extra)
    extra = jnp.where(row == 5, jnp.broadcast_to(layer[:, 4:5, :], extra.shape), extra)
    message[:, 8 * QUADS:, :] = extra


def gradient_kernel(
    received, even_h, even_t, odd_h, odd_t, provisional, motion_hbm,
    motion, lines, pressure, row_p, layer_p, sems,
):
    size_x = provisional.shape[-1]
    for block in range(size_x // 128):
        for j, piece in enumerate(swap_groups([received[4 * block + i] for i in range(4)])):
            lines[j * PIECE:(j + 1) * PIECE, block * 128:(block + 1) * 128] = piece
    evens = product(lines[:, : size_x // 2], even_h[...], even_t[...], dot)
    odds = product(lines[:, size_x // 2:], odd_h[...], odd_t[...], dot_nt)
    lines[:, : size_x // 2] = evens + odds
    lines[:, size_x // 2:] = evens - odds
    for b in range(size_x // 128):
        lanes = pl.ds(b * 128, 128)
        for j in range(4):
            for q in range(QUADS):
                pressure[b, pl.ds(4 * q + j, ROWS, stride=LAYERS), :] = lines[pl.ds(j * PIECE + q * 8, 8), lanes]
            row_p[b, pl.ds(j, 4, stride=4), :] = lines[pl.ds(j * PIECE + 32, 4), lanes]
            layer_p[b, pl.ds(j, 2, stride=4), :] = lines[pl.ds(j * PIECE + 36, 2), lanes]
    stored = []
    bottom = lax.broadcasted_iota(jnp.int32, (LAYERS, size_x), 0) == 0
    for y in range(ROWS):
        p = kept(pressure, y * LAYERS, LAYERS)
        before = kept(row_p, 0, LAYERS) if y == 0 else kept(pressure, (y - 1) * LAYERS, LAYERS)
        below = jnp.where(bottom, kept(layer_p, y, 1), pltpu.roll(p, 1, 0))
        slope_z = jnp.where(bottom & (lax.axis_index("gz") == 0), 0.0, p - below)
        motion[0, y] = provisional[0, y] - (p - pltpu.roll(p, 1, 1))
        motion[1, y] = provisional[1, y] - (p - before)
        motion[2, y] = provisional[2, y] - slope_z
        copy = pltpu.make_async_copy(motion.at[:, pl.ds(y, 1)], motion_hbm.at[:, pl.ds(y, 1)], sems.at[y])
        copy.start()
        stored.append(copy)
    for copy in stored:
        copy.wait()


def swapped(value, axis, first, periodic):
    size = lax.axis_size(axis)
    pairs = []
    for i in range(first, size, 2):
        if periodic or i + 1 < size:
            pairs += [(i, (i + 1) % size), ((i + 1) % size, i)]
    return lax.ppermute(value, axis, pairs)


def exchanged(pieces, axis):
    return lax.all_to_all(pieces, axis, split_axis=0, concat_axis=0, tiled=True)


def shape_of(*shape):
    return jax.ShapeDtypeStruct(shape, F32)


def on_device(dual_motion, dual_thermal, flow, base):
    size_x = dual_thermal.shape[-1]
    groups_y = lax.axis_size("gy")
    groups_z = lax.axis_size("gz")
    evens, odds, table = tables(size_x, ROWS * groups_y)
    even_h, even_t = map(jnp.asarray, evens)
    odd_h, odd_t = map(jnp.asarray, odds)
    modes = ROWS * groups_y // 4
    blocks = size_x // 128

    def hbm(value):
        return pltpu.with_memory_space_constraint(value, pltpu.HBM)

    def params(mib):
        return pltpu.CompilerParams(vmem_limit_bytes=mib << 20)

    table = jnp.asarray(table)
    rows = shape_of(5, LAYERS, size_x)
    layers = shape_of(5, ROWS, size_x)
    motion_shape = (3, ROWS, LAYERS, size_x)
    thermal_shape = motion_shape[1:]
    message_shape = (groups_y, PIECE, 128)
    fields = tuple(jax.ShapeDtypeStruct(a.shape, a.dtype) for a in (dual_motion, dual_thermal, base))
    row_near, row_far, layer_near, layer_far, motion, thermal, base = pl.pallas_call(
        sides_kernel,
        out_shape=(rows, rows, layers, layers, *fields),
        in_specs=[HBM] * 3,
        out_specs=(VMEM,) * 7,
        scratch_shapes=[pltpu.SemaphoreType.DMA((3,))],
        compiler_params=params(16),
        name="sides",
    )(*map(hbm, (dual_motion, dual_thermal, base)))
    row_near = swapped(row_near, "gy", 0, True)
    row_far = swapped(row_far, "gy", 1, True)
    layer_near = swapped(layer_near, "gz", 0, False)
    layer_far = swapped(layer_far, "gz", 1, False)
    moved, row_factors, layer_factors = pl.pallas_call(
        inner_kernel,
        out_shape=(
            shape_of(4, *thermal_shape),
            shape_of(4, LAYERS, size_x),
            shape_of(4, ROWS, size_x),
        ),
        in_specs=[VMEM] * 4,
        out_specs=(VMEM,) * 3,
        compiler_params=params(16),
        cost_estimate=pl.CostEstimate(
            flops=80 * ROWS * LAYERS * size_x, transcendentals=0, bytes_accessed=10 << 20
        ),
        name="inner",
    )(motion, thermal, flow, base)
    provisional, thermal_out, message = pl.pallas_call(
        source_kernel,
        out_shape=(
            shape_of(*motion_shape),
            pltpu.HBM(thermal_shape, F32),
            shape_of(*message_shape),
        ),
        in_specs=[VMEM] * 11,
        out_specs=(VMEM, HBM, VMEM),
        scratch_shapes=[
            pltpu.VMEM(thermal_shape, F32),
            pltpu.VMEM((blocks, ROWS * LAYERS, 128), F32),
            pltpu.VMEM((4 * PIECE, size_x), F32),
            pltpu.VMEM((blocks, LAYERS, 128), F32),
            pltpu.VMEM((blocks, ROWS, 128), F32),
            pltpu.SemaphoreType.DMA((1,)),
        ],
        compiler_params=params(24),
        name="source",
    )(
        moved, row_factors, layer_factors, layer_far, layer_near, row_far, row_near,
        even_h, even_t, odd_h, odd_t,
    )
    received = exchanged(message, "gy")
    spectral, handed = pl.pallas_call(
        down_kernel,
        out_shape=(shape_of(LAYERS + 3, modes, 128), shape_of(groups_z, modes, 128)),
        in_specs=[VMEM] * 2,
        out_specs=(VMEM,) * 2,
        compiler_params=params(16),
        name="down",
    )(received, table)
    handed = exchanged(handed, "gz")
    message = pl.pallas_call(
        up_kernel,
        out_shape=shape_of(*message_shape),
        in_specs=[VMEM] * 3,
        out_specs=VMEM,
        compiler_params=params(16),
        name="up",
    )(spectral, handed, table)
    received = exchanged(message, "gy")
    motion = pl.pallas_call(
        gradient_kernel,
        out_shape=pltpu.HBM(motion_shape, F32),
        in_specs=[VMEM] * 6,
        out_specs=HBM,
        scratch_shapes=[
            pltpu.VMEM(motion_shape, F32),
            pltpu.VMEM((4 * PIECE, size_x), F32),
            pltpu.VMEM((blocks, ROWS * LAYERS, 128), F32),
            pltpu.VMEM((blocks, LAYERS, 128), F32),
            pltpu.VMEM((blocks, ROWS, 128), F32),
            pltpu.SemaphoreType.DMA((ROWS,)),
        ],
        compiler_params=params(24),
        name="gradient",
    )(received, even_h, even_t, odd_h, odd_t, provisional)
    return motion, thermal_out


def solution(mesh):
    split_y = P(None, "gy", "gz", None)
    split_flat = P("gy", "gz", None)
    return jax.shard_map(
        on_device,
        mesh=mesh,
        in_specs=(split_y, split_flat, split_y, split_flat),
        out_specs=(split_y, split_flat),
        check_vma=False,
    )
```

```python
import functools

import jax
import jax.numpy as jnp
import ml_dtypes
import numpy as np
from jax import lax
from jax.experimental import pallas as pl
from jax.experimental.pallas import tpu as pltpu
from jax.sharding import PartitionSpec as P

F32 = jnp.float32
BF16 = jnp.bfloat16
ROWS = 8
LAYERS = 16
WAVES = 32
QUADS = LAYERS // 4
PIECE = 8 * (QUADS + 1)
VMEM = pl.BlockSpec(memory_space=pltpu.VMEM)
HBM = pl.BlockSpec(memory_space=pltpu.HBM)


def two_parts(table):
    head = table.astype(ml_dtypes.bfloat16)
    return head, (table - head.astype(np.float64)).astype(ml_dtypes.bfloat16)


def cas(phases, length):
    angles = (phases % length) * (2.0 * np.pi / length)
    return np.cos(angles) + np.sin(angles)


@functools.lru_cache(None)
def tables(size_x, size_y):
    half = np.arange(size_x // 2)
    quarter = np.arange(size_x // 4)
    fourth = two_parts(cas(quarter[:, None] * quarter[None, :], size_x // 4))
    even = two_parts(cas(quarter[:, None] * (2 * quarter[None, :] + 1), size_x // 2))
    odd = two_parts(cas(half[:, None] * (2 * half[None, :] + 1), size_x))
    full = np.arange(size_y)
    span = cas(full[:, None] * full[None, :], size_y)
    waves = np.concatenate([4 * quarter, 4 * quarter + 2, 2 * half + 1])
    line_x = 4.0 * np.sin(np.pi * waves / size_x) ** 2
    line_x = np.tile(line_x.reshape(-1, WAVES), (1, 128 // WAVES))
    row = np.arange(size_y // 4)[:, None]
    lane = np.arange(128)[None, :]
    wave_y = 32 * (row // 8) + 8 * (lane // WAVES) + row % 8
    line_y = 4.0 * np.sin(np.pi * wave_y / size_y) ** 2
    halves = [span[:, n * 128:(n + 1) * 128] for n in range(size_y // 128)]
    return fourth + even + odd, np.concatenate(halves + [line_y, line_x], 0).astype(np.float32)


def split(values):
    head = values.astype(BF16)
    return head, (values - head.astype(F32)).astype(BF16)


def lane_group(shape):
    return lax.broadcasted_iota(jnp.int32, shape, len(shape) - 1) // WAVES


def swap_groups(a):
    axis = a[0].ndim - 1
    group = lane_group(a[0].shape)
    low = group < 2
    even = group % 2 == 0
    b0 = jnp.where(low, a[0], pltpu.roll(a[2], 64, axis))
    b2 = jnp.where(low, pltpu.roll(a[0], 64, axis), a[2])
    b1 = jnp.where(low, a[1], pltpu.roll(a[3], 64, axis))
    b3 = jnp.where(low, pltpu.roll(a[1], 64, axis), a[3])
    return (
        jnp.where(even, b0, pltpu.roll(b1, 32, axis)),
        jnp.where(even, pltpu.roll(b0, 96, axis), b1),
        jnp.where(even, b2, pltpu.roll(b3, 32, axis)),
        jnp.where(even, pltpu.roll(b2, 96, axis), b3),
    )


def dot(a, b):
    return jnp.dot(a, b, preferred_element_type=F32)


def dot_nt(a, b):
    return lax.dot_general(a, b, (((1,), (1,)), ((), ())), preferred_element_type=F32)


def product(values, head, tail, how):
    a, b = split(values)
    both = how(jnp.concatenate([a, b], 0), head)
    count = values.shape[0]
    return both[:count] + (both[count:] + how(a, tail))


def keep(ref, start, values):
    for b in range(ref.shape[0]):
        ref[b, pl.ds(start, values.shape[0]), :] = values[:, b * 128:(b + 1) * 128]


def kept(ref, start, count):
    return jnp.concatenate([ref[b, pl.ds(start, count), :] for b in range(ref.shape[0])], 1)


def start_copies(pairs, sems):
    copies = [pltpu.make_async_copy(a, b, sems.at[n]) for n, (a, b) in enumerate(pairs)]
    for copy in copies:
        copy.start()
    return copies


def odd(axis):
    return lax.axis_index(axis) % 2 == 1


def sides_kernel(
    motion_hbm, thermal_hbm, base_hbm, row_near, row_far, layer_near, layer_far, motion, thermal, base, sems
):
    pairs = ((base_hbm, base), (thermal_hbm, thermal), (motion_hbm, motion))
    fetched = start_copies(pairs, sems)
    is_odd = odd("gz")
    near = jnp.where(odd("gy"), 0, ROWS - 1)
    far = ROWS - 1 - near

    def edges(first, last):
        return jnp.where(is_odd, first, last), jnp.where(is_odd, last, first)

    fetched[0].wait()
    row_near[4] = base[near].astype(F32)
    row_far[4] = base[far].astype(F32)
    for y in range(ROWS):
        warm = base[y].astype(F32)
        layer_near[4, y:y + 1, :], layer_far[4, y:y + 1, :] = edges(warm[:1], warm[LAYERS - 1:])
    fetched[1].wait()
    row_near[3] = thermal[near]
    row_far[3] = thermal[far]
    for y in range(ROWS):
        layer_near[3, y:y + 1, :], layer_far[3, y:y + 1, :] = edges(thermal[y, :1, :], thermal[y, LAYERS - 1:, :])
    fetched[2].wait()
    for c in range(3):
        row_near[c] = motion[c, near]
        row_far[c] = motion[c, far]
        for y in range(ROWS):
            layer_near[c, y:y + 1, :], layer_far[c, y:y + 1, :] = edges(
                motion[c, y, :1, :], motion[c, y, LAYERS - 1:, :]
            )


def inner_kernel(motion, thermal, flow, base, moved, row_factors, layer_factors):
    size_x = motion.shape[-1]
    row = lax.broadcasted_iota(jnp.int32, (LAYERS, size_x), 0)
    top = row == LAYERS - 1
    bottom = row == 0

    def field(c, y):
        if c < 3:
            return motion[c, y]
        if c == 3:
            return thermal[y]
        return base[y].astype(F32)

    def neighbours(c, y):
        centre = field(c, y)
        y_plus = field(c, y + 1) if y < ROWS - 1 else None
        y_minus = field(c, y - 1) if y > 0 else None
        z_plus = jnp.where(top, 0.0, pltpu.roll(centre, LAYERS - 1, 0))
        z_minus = jnp.where(bottom, 0.0, pltpu.roll(centre, 1, 0))
        x_plus = pltpu.roll(centre, size_x - 1, 1)
        x_minus = pltpu.roll(centre, 1, 1)
        return centre, x_plus, x_minus, y_plus, y_minus, z_plus, z_minus

    for y in range(ROWS):
        weights = []
        for c in range(3):
            speed = flow[c, y].astype(F32) * 0.1
            weights += [0.02 + speed, 0.02 - speed]
        _, hx, gx, hy, gy, hz, gz = neighbours(4, y)
        slope_y = -gy if hy is None else hy if gy is None else hy - gy
        slopes = (hx - gx, slope_y, hz - gz)
        heat = thermal[y] * 0.1
        if y == 0:
            row_factors[0] = weights[3]
            row_factors[1] = -heat
        if y == ROWS - 1:
            row_factors[2] = weights[2]
            row_factors[3] = heat
        layer_factors[0, y:y + 1, :] = weights[5][:1]
        layer_factors[1, y:y + 1, :] = -heat[:1]
        layer_factors[2, y:y + 1, :] = weights[4][LAYERS - 1:]
        layer_factors[3, y:y + 1, :] = heat[LAYERS - 1:]
        for c in range(4):
            parts = neighbours(c, y)
            value = parts[0] * 0.88
            for weight, part in zip(weights, parts[1:]):
                if part is not None:
                    value = value + weight * part
            moved[c, y] = value + (heat * slopes[c] if c < 3 else 0.2 * motion[2, y])


def source_kernel(
    moved, row_factors, layer_factors, layer_far, layer_near, row_far, row_near,
    fourth_h, fourth_t, even_h, even_t, odd_h, odd_t,
    provisional, thermal_hbm, message, thermal, source, lines, row_p, layer_p, sems
):
    size_x = moved.shape[-1]
    row = lax.broadcasted_iota(jnp.int32, (8, size_x), 0)
    top = lax.broadcasted_iota(jnp.int32, (LAYERS, size_x), 0) == LAYERS - 1
    odd_y, odd_z = odd("gy"), odd("gz")
    y_low = [jnp.where(odd_y, row_near[c], row_far[c]) for c in range(5)]
    y_high = [jnp.where(odd_y, row_far[c], row_near[c]) for c in range(5)]
    z_low = [jnp.where(odd_z, layer_near[c], layer_far[c]) for c in range(5)]
    z_high = [jnp.where(odd_z, layer_far[c], layer_near[c]) for c in range(5)]
    lows = [layer_factors[0] * z_low[c] for c in range(4)]
    highs = [layer_factors[2] * z_high[c] for c in range(4)]
    lows[2] = lows[2] + layer_factors[1] * z_low[4]
    highs[2] = highs[2] + layer_factors[3] * z_high[4]
    carried = None
    for y in range(ROWS):
        for c in range(4):
            value = moved[c, y]
            if y == 0:
                value = value + row_factors[0] * y_low[c]
                if c == 1:
                    value = value + row_factors[1] * y_low[4]
            if y == ROWS - 1:
                value = value + row_factors[2] * y_high[c]
                if c == 1:
                    value = value + row_factors[3] * y_high[4]
            out = provisional.at[c, y] if c < 3 else thermal.at[y]
            out[:8] = value[:8] + jnp.where(row == 0, lows[c][y:y + 1], 0.0)
            out[8:] = value[8:] + jnp.where(row == 7, highs[c][y:y + 1], 0.0)
        p0, p1, p2 = (provisional[c, y] for c in range(3))
        if y == 0:
            keep(row_p, 0, p1)
        else:
            keep(source, (y - 1) * LAYERS, carried + p1)
        keep(layer_p, y, p2[0:1, :])
        above = jnp.where(top, 0.0, pltpu.roll(p2, LAYERS - 1, 0))
        carried = (pltpu.roll(p0, size_x - 1, 1) - p0) - p1 + (above - p2)
    keep(source, (ROWS - 1) * LAYERS, carried)
    stored = start_copies(((thermal, thermal_hbm),), sems)

    for b in range(size_x // 128):
        lanes = pl.ds(b * 128, 128)
        for j in range(4):
            for q in range(QUADS):
                lines[pl.ds(j * PIECE + q * 8, 8), lanes] = source[b, pl.ds(4 * q + j, ROWS, stride=LAYERS), :]
            lines[pl.ds(j * PIECE + 32, 4), lanes] = row_p[b, pl.ds(j, 4, stride=4), :]
            lines[pl.ds(j * PIECE + 36, 2), lanes] = layer_p[b, pl.ds(j, 2, stride=4), :]
            lines[pl.ds(j * PIECE + 38, 2), lanes] = jnp.zeros((2, 128), F32)
    near = lines[:, : size_x // 2]
    far = lines[:, size_x // 2:]
    both = near + far
    left, right = both[:, : size_x // 4], both[:, size_x // 4:]
    turns = (
        (left + right, fourth_h, fourth_t),
        (left - right, even_h, even_t),
        (near - far, odd_h, odd_t),
    )
    at = 0
    for values, head, tail in turns:
        waves = product(values, head[...], tail[...], dot)
        for block in range(waves.shape[1] // 128):
            a = [waves[j * PIECE:(j + 1) * PIECE, block * 128:(block + 1) * 128] for j in range(4)]
            for i, piece in enumerate(swap_groups(a)):
                message[at + i] = piece
            at += 4
    for copy in stored:
        copy.wait()


def span_product(table, values):
    size_y = values.shape[0]
    wide = jnp.concatenate([table[pl.ds(n * size_y, size_y), :] for n in range(size_y // 128)], 1)
    left = split(wide)
    right = split(values)
    both = dot(jnp.concatenate(left, 0), right[0])
    return both[:size_y] + (both[size_y:] + dot(left[0], right[1]))


def wall_factors(lam, slab, slabs):
    square = lam * lam
    powers = [jnp.ones_like(lam), square]
    for m in range(2, LAYERS + 1):
        powers.append(powers[m // 2] * powers[m - m // 2])
    step = powers[LAYERS]

    def raised(count):
        value = lam
        factor = step
        for bit in range((slabs - 1).bit_length()):
            value = jnp.where((count // (1 << bit)) % 2 == 1, value * factor, value)
            factor = factor * factor
        return value

    low = raised(slab)
    high = raised(slabs - 1 - slab)
    below = low * (1.0 / square)
    floor = [1.0 + jnp.where(slab == 0, lam, below)] + [1.0 + low * powers[l] for l in range(LAYERS)]
    ceiling = [1.0 + high * powers[LAYERS - 1 - l] for l in range(-1, LAYERS)]
    return floor, ceiling, powers


def down_kernel(received, table, spectral, handed):
    sources = received.shape[0]
    size_y = sources * ROWS
    slabs = handed.shape[0]
    size_x = sources * WAVES
    slab = lax.axis_index("gz")
    row = lax.broadcasted_iota(jnp.int32, (sources, 8, 128), 1)
    group = lane_group((sources, 8, 128))
    extra = received[:, 8 * QUADS:, :]
    onward = jnp.concatenate([extra[1:], extra[:1]], 0)
    columns = []
    for q in range(QUADS):
        more = jnp.broadcast_to(onward[:, q:q + 1, :], (sources, 8, 128))
        values = received[:, 8 * q:8 * q + 8, :] + jnp.where(row == ROWS - 1, more, 0.0)
        columns.append(values.reshape(size_y, 128))
    first = jnp.broadcast_to(extra[:, 4:5, :], (sources, 8, 128))
    second = jnp.broadcast_to(extra[:, 5:6, :], (sources, 8, 128))
    layer = jnp.where(row < 4, first, second)
    layer = jnp.where((row % 4 == group) & (slab > 0), layer, 0.0)
    columns.append(layer.reshape(size_y, 128))
    waves = span_product(table, jnp.concatenate(columns, 1))

    last = waves[:, 128 * QUADS:]
    last = last + pltpu.roll(last, 64, 1)
    last = (last + pltpu.roll(last, 32, 1)).reshape(size_y // 32, 4, 8, 128)
    modes = size_y // 4
    mode_group = lane_group((modes, 128))
    pick = [last[:, i].reshape(modes, 128) for i in range(4)]
    layers = [
        jnp.where(
            mode_group < 2,
            jnp.where(mode_group == 0, pick[0], pick[1]),
            jnp.where(mode_group == 2, pick[2], pick[3]),
        )
    ]
    for q in range(QUADS):
        block = waves[:, 128 * q:128 * (q + 1)].reshape(size_y // 32, 4, 8, 128)
        layers += swap_groups([block[:, i].reshape(modes, 128) for i in range(4)])
    modes = size_y // 4
    line_y = table[pl.ds(2 * size_y, modes), :]
    a = table[pl.ds(2 * size_y + modes + lax.axis_index("gy"), 1), :] + line_y
    sinh = jnp.sqrt(a * (1.0 + 0.25 * a))
    lam = 1.0 / (1.0 + 0.5 * a + sinh)
    floor, ceiling, powers = wall_factors(lam, slab, slabs)
    spectral[LAYERS + 1] = lam
    whole = powers[LAYERS]
    for _ in range((slabs - 1).bit_length()):
        whole = whole * whole
    zero = a == 0.0
    weight = (-1.0 / (size_x * size_y)) / jnp.where(zero, 1.0, 2.0 * sinh * (1.0 - whole))
    spectral[LAYERS + 2] = jnp.where(zero, 0.0, weight)
    upward = jnp.zeros_like(lam)
    downward = jnp.zeros_like(lam)
    for l in range(LAYERS + 1):
        spectral[l] = layers[l]
        upward = lam * upward + floor[l] * layers[l]
        m = LAYERS - l
        downward = lam * downward + ceiling[m] * layers[m]
    for d in range(slabs):
        handed[d] = jnp.where(d > slab, upward, downward)


def up_kernel(spectral, handed, table, message):
    sources = message.shape[0]
    size_y = sources * ROWS
    slabs = handed.shape[0]
    size_x = sources * WAVES
    size_z = slabs * LAYERS
    slab = lax.axis_index("gz")
    lam = spectral[LAYERS + 1]
    weight = spectral[LAYERS + 2]
    floor, ceiling, powers = wall_factors(lam, slab, slabs)
    scale = 1.0 / (size_x * size_y)
    reach = powers[LAYERS // 2]
    upward = jnp.zeros_like(lam)
    downward = jnp.zeros_like(lam)
    for d in range(slabs - 1):
        upward = jnp.where(d < slab, reach * upward + handed[d], upward)
        e = slabs - 1 - d
        downward = jnp.where(e > slab, reach * downward + handed[e], downward)
    below = []
    for l in range(LAYERS + 1):
        upward = (lam * upward if l else upward) + floor[l] * spectral[l]
        below.append(upward)
    pressure = [None] * (LAYERS + 1)
    for l in reversed(range(LAYERS + 1)):
        pressure[l] = weight * (ceiling[l] * below[l] + floor[l] * downward)
        if l == LAYERS:
            mean = (0.5 / size_z) * (below[l][:8] + downward[:8])
        downward = lam * (downward + ceiling[l] * spectral[l])
    modes = size_y // 4
    flat = jnp.zeros((8, 128), F32)
    first_zero = weight[:8] == 0.0
    for l in range(LAYERS + 1):
        if l:
            count = (slab * LAYERS + (l - 1)).astype(F32)
            flat = flat + (0.5 * below[l - 1][:8] - count * mean)
        pressure[l] = jnp.concatenate(
            [jnp.where(first_zero, flat * scale, pressure[l][:8]), pressure[l][8:]], 0
        )

    columns = []
    tall = (size_y // 32, 1, 8, 128)
    for q in range(QUADS):
        block = swap_groups(pressure[1 + 4 * q:5 + 4 * q])
        columns.append(jnp.concatenate([b.reshape(tall) for b in block], 1).reshape(size_y, 128))
    mode_group = lane_group((modes, 128))
    spread = []
    for i in range(4):
        part = jnp.where(mode_group == i, pressure[0], 0.0)
        part = part + pltpu.roll(part, 64, 1)
        spread.append((part + pltpu.roll(part, 32, 1)).reshape(tall))
    columns.append(jnp.concatenate(spread, 1).reshape(size_y, 128))
    values = span_product(table, jnp.concatenate(columns, 1))

    row = lax.broadcasted_iota(jnp.int32, (sources, 8, 128), 1)
    group = lane_group((sources, 8, 128))
    extra = jnp.zeros((sources, 8, 128), F32)
    for q in range(QUADS):
        block = values[:, 128 * q:128 * (q + 1)].reshape(sources, 8, 128)
        message[:, 8 * q:8 * q + 8, :] = block
        edge = jnp.concatenate([block[-1:], block[:-1]], 0)[:, ROWS - 1:ROWS, :]
        extra = jnp.where(row == q, jnp.broadcast_to(edge, extra.shape), extra)
    layer = values[:, 128 * QUADS:].reshape(sources, 8, 128)
    layer = jnp.where(row % 4 == group, layer, 0.0)
    layer = layer + pltpu.roll(layer, 7, 1)
    layer = layer + pltpu.roll(layer, 6, 1)
    extra = jnp.where(row == 4, jnp.broadcast_to(layer[:, 0:1, :], extra.shape), extra)
    extra = jnp.where(row == 5, jnp.broadcast_to(layer[:, 4:5, :], extra.shape), extra)
    message[:, 8 * QUADS:, :] = extra


def gradient_kernel(
    received, fourth_h, fourth_t, even_h, even_t, odd_h, odd_t, provisional, motion_hbm,
    motion, lines, pressure, row_p, layer_p, sems,
):
    size_x = provisional.shape[-1]
    for block in range(size_x // 128):
        for j, piece in enumerate(swap_groups([received[4 * block + i] for i in range(4)])):
            lines[j * PIECE:(j + 1) * PIECE, block * 128:(block + 1) * 128] = piece
    fourths = product(lines[:, : size_x // 4], fourth_h[...], fourth_t[...], dot)
    others = product(lines[:, size_x // 4: size_x // 2], even_h[...], even_t[...], dot_nt)
    evens = jnp.concatenate([fourths + others, fourths - others], 1)
    odds = product(lines[:, size_x // 2:], odd_h[...], odd_t[...], dot_nt)
    lines[:, : size_x // 2] = evens + odds
    lines[:, size_x // 2:] = evens - odds
    for b in range(size_x // 128):
        lanes = pl.ds(b * 128, 128)
        for j in range(4):
            for q in range(QUADS):
                pressure[b, pl.ds(4 * q + j, ROWS, stride=LAYERS), :] = lines[pl.ds(j * PIECE + q * 8, 8), lanes]
            row_p[b, pl.ds(j, 4, stride=4), :] = lines[pl.ds(j * PIECE + 32, 4), lanes]
            layer_p[b, pl.ds(j, 2, stride=4), :] = lines[pl.ds(j * PIECE + 36, 2), lanes]
    stored = []
    bottom = lax.broadcasted_iota(jnp.int32, (LAYERS, size_x), 0) == 0
    for y in range(ROWS):
        p = kept(pressure, y * LAYERS, LAYERS)
        before = kept(row_p, 0, LAYERS) if y == 0 else kept(pressure, (y - 1) * LAYERS, LAYERS)
        below = jnp.where(bottom, kept(layer_p, y, 1), pltpu.roll(p, 1, 0))
        slope_z = jnp.where(bottom & (lax.axis_index("gz") == 0), 0.0, p - below)
        motion[0, y] = provisional[0, y] - (p - pltpu.roll(p, 1, 1))
        motion[1, y] = provisional[1, y] - (p - before)
        motion[2, y] = provisional[2, y] - slope_z
        copy = pltpu.make_async_copy(motion.at[:, pl.ds(y, 1)], motion_hbm.at[:, pl.ds(y, 1)], sems.at[y])
        copy.start()
        stored.append(copy)
    for copy in stored:
        copy.wait()


def swapped(value, axis, first, periodic):
    size = lax.axis_size(axis)
    pairs = []
    for i in range(first, size, 2):
        if periodic or i + 1 < size:
            pairs += [(i, (i + 1) % size), ((i + 1) % size, i)]
    return lax.ppermute(value, axis, pairs)


def exchanged(pieces, axis):
    return lax.all_to_all(pieces, axis, split_axis=0, concat_axis=0, tiled=True)


def shape_of(*shape):
    return jax.ShapeDtypeStruct(shape, F32)


def on_device(dual_motion, dual_thermal, flow, base):
    size_x = dual_thermal.shape[-1]
    groups_y = lax.axis_size("gy")
    groups_z = lax.axis_size("gz")
    waves, table = tables(size_x, ROWS * groups_y)
    waves = tuple(map(jnp.asarray, waves))
    modes = ROWS * groups_y // 4
    blocks = size_x // 128

    def hbm(value):
        return pltpu.with_memory_space_constraint(value, pltpu.HBM)

    def params(mib):
        return pltpu.CompilerParams(vmem_limit_bytes=mib << 20)

    table = jnp.asarray(table)
    rows = shape_of(5, LAYERS, size_x)
    layers = shape_of(5, ROWS, size_x)
    motion_shape = (3, ROWS, LAYERS, size_x)
    thermal_shape = motion_shape[1:]
    message_shape = (groups_y, PIECE, 128)
    fields = tuple(jax.ShapeDtypeStruct(a.shape, a.dtype) for a in (dual_motion, dual_thermal, base))
    row_near, row_far, layer_near, layer_far, motion, thermal, base = pl.pallas_call(
        sides_kernel,
        out_shape=(rows, rows, layers, layers, *fields),
        in_specs=[HBM] * 3,
        out_specs=(VMEM,) * 7,
        scratch_shapes=[pltpu.SemaphoreType.DMA((3,))],
        compiler_params=params(16),
        name="sides",
    )(*map(hbm, (dual_motion, dual_thermal, base)))
    row_near = swapped(row_near, "gy", 0, True)
    row_far = swapped(row_far, "gy", 1, True)
    layer_near = swapped(layer_near, "gz", 0, False)
    layer_far = swapped(layer_far, "gz", 1, False)
    moved, row_factors, layer_factors = pl.pallas_call(
        inner_kernel,
        out_shape=(
            shape_of(4, *thermal_shape),
            shape_of(4, LAYERS, size_x),
            shape_of(4, ROWS, size_x),
        ),
        in_specs=[VMEM] * 4,
        out_specs=(VMEM,) * 3,
        compiler_params=params(16),
        cost_estimate=pl.CostEstimate(
            flops=80 * ROWS * LAYERS * size_x, transcendentals=0, bytes_accessed=10 << 20
        ),
        name="inner",
    )(motion, thermal, flow, base)
    provisional, thermal_out, message = pl.pallas_call(
        source_kernel,
        out_shape=(
            shape_of(*motion_shape),
            pltpu.HBM(thermal_shape, F32),
            shape_of(*message_shape),
        ),
        in_specs=[VMEM] * 13,
        out_specs=(VMEM, HBM, VMEM),
        scratch_shapes=[
            pltpu.VMEM(thermal_shape, F32),
            pltpu.VMEM((blocks, ROWS * LAYERS, 128), F32),
            pltpu.VMEM((4 * PIECE, size_x), F32),
            pltpu.VMEM((blocks, LAYERS, 128), F32),
            pltpu.VMEM((blocks, ROWS, 128), F32),
            pltpu.SemaphoreType.DMA((1,)),
        ],
        compiler_params=params(24),
        name="source",
    )(
        moved, row_factors, layer_factors, layer_far, layer_near, row_far, row_near,
        *waves,
    )
    received = exchanged(message, "gy")
    spectral, handed = pl.pallas_call(
        down_kernel,
        out_shape=(shape_of(LAYERS + 3, modes, 128), shape_of(groups_z, modes, 128)),
        in_specs=[VMEM] * 2,
        out_specs=(VMEM,) * 2,
        compiler_params=params(16),
        name="down",
    )(received, table)
    handed = exchanged(handed, "gz")
    message = pl.pallas_call(
        up_kernel,
        out_shape=shape_of(*message_shape),
        in_specs=[VMEM] * 3,
        out_specs=VMEM,
        compiler_params=params(16),
        name="up",
    )(spectral, handed, table)
    received = exchanged(message, "gy")
    motion = pl.pallas_call(
        gradient_kernel,
        out_shape=pltpu.HBM(motion_shape, F32),
        in_specs=[VMEM] * 8,
        out_specs=HBM,
        scratch_shapes=[
            pltpu.VMEM(motion_shape, F32),
            pltpu.VMEM((4 * PIECE, size_x), F32),
            pltpu.VMEM((blocks, ROWS * LAYERS, 128), F32),
            pltpu.VMEM((blocks, LAYERS, 128), F32),
            pltpu.VMEM((blocks, ROWS, 128), F32),
            pltpu.SemaphoreType.DMA((ROWS,)),
        ],
        compiler_params=params(24),
        name="gradient",
    )(received, *waves, provisional)
    return motion, thermal_out


def solution(mesh):
    split_y = P(None, "gy", "gz", None)
    split_flat = P("gy", "gz", None)
    return jax.shard_map(
        on_device,
        mesh=mesh,
        in_specs=(split_y, split_flat, split_y, split_flat),
        out_specs=(split_y, split_flat),
        check_vma=False,
    )
```

```python
import functools

import jax
import jax.numpy as jnp
import ml_dtypes
import numpy as np
from jax import lax
from jax.experimental import pallas as pl
from jax.experimental.pallas import tpu as pltpu
from jax.sharding import PartitionSpec as P

F32 = jnp.float32
BF16 = jnp.bfloat16
ROWS = 8
LAYERS = 16
WAVES = 32
QUADS = LAYERS // 4
PIECE = 8 * (QUADS + 1)
VMEM = pl.BlockSpec(memory_space=pltpu.VMEM)
HBM = pl.BlockSpec(memory_space=pltpu.HBM)


def two_parts(table):
    head = table.astype(ml_dtypes.bfloat16)
    return head, (table - head.astype(np.float64)).astype(ml_dtypes.bfloat16)


def cas(phases, length):
    angles = (phases % length) * (2.0 * np.pi / length)
    return np.cos(angles) + np.sin(angles)


@functools.lru_cache(None)
def tables(size_x, size_y):
    half = np.arange(size_x // 2)
    quarter = np.arange(size_x // 4)
    fourth = two_parts(cas(quarter[:, None] * quarter[None, :], size_x // 4))
    even = two_parts(cas(quarter[:, None] * (2 * quarter[None, :] + 1), size_x // 2))
    odd = two_parts(cas(half[:, None] * (2 * half[None, :] + 1), size_x))
    full = np.arange(size_y)
    span = cas(full[:, None] * full[None, :], size_y)
    waves = np.concatenate([4 * quarter, 4 * quarter + 2, 2 * half + 1])
    line_x = 4.0 * np.sin(np.pi * waves / size_x) ** 2
    line_x = np.tile(line_x.reshape(-1, WAVES), (1, 128 // WAVES))
    row = np.arange(size_y // 4)[:, None]
    lane = np.arange(128)[None, :]
    wave_y = 32 * (row // 8) + 8 * (lane // WAVES) + row % 8
    line_y = 4.0 * np.sin(np.pi * wave_y / size_y) ** 2
    halves = [span[:, n * 128:(n + 1) * 128] for n in range(size_y // 128)]
    return fourth + even + odd, np.concatenate(halves + [line_y, line_x], 0).astype(np.float32)


def split(values):
    head = values.astype(BF16)
    return head, (values - head.astype(F32)).astype(BF16)


def lane_group(shape):
    return lax.broadcasted_iota(jnp.int32, shape, len(shape) - 1) // WAVES


def swap_groups(a):
    axis = a[0].ndim - 1
    group = lane_group(a[0].shape)
    low = group < 2
    even = group % 2 == 0
    b0 = jnp.where(low, a[0], pltpu.roll(a[2], 64, axis))
    b2 = jnp.where(low, pltpu.roll(a[0], 64, axis), a[2])
    b1 = jnp.where(low, a[1], pltpu.roll(a[3], 64, axis))
    b3 = jnp.where(low, pltpu.roll(a[1], 64, axis), a[3])
    return (
        jnp.where(even, b0, pltpu.roll(b1, 32, axis)),
        jnp.where(even, pltpu.roll(b0, 96, axis), b1),
        jnp.where(even, b2, pltpu.roll(b3, 32, axis)),
        jnp.where(even, pltpu.roll(b2, 96, axis), b3),
    )


def dot(a, b):
    return jnp.dot(a, b, preferred_element_type=F32)


def dot_nt(a, b):
    return lax.dot_general(a, b, (((1,), (1,)), ((), ())), preferred_element_type=F32)


def product(values, head, tail, how):
    a, b = split(values)
    both = how(jnp.concatenate([a, b], 0), head)
    count = values.shape[0]
    return both[:count] + (both[count:] + how(a, tail))


def keep(ref, start, values):
    for b in range(ref.shape[0]):
        ref[b, pl.ds(start, values.shape[0]), :] = values[:, b * 128:(b + 1) * 128]


def kept(ref, start, count):
    return jnp.concatenate([ref[b, pl.ds(start, count), :] for b in range(ref.shape[0])], 1)


def start_copies(pairs, sems):
    copies = [pltpu.make_async_copy(a, b, sems.at[n]) for n, (a, b) in enumerate(pairs)]
    for copy in copies:
        copy.start()
    return copies


def odd(axis):
    return lax.axis_index(axis) % 2 == 1


def rows_kernel(motion_hbm, thermal_hbm, base_hbm, row_near, row_far, base, sems):
    near = jnp.where(odd("gy"), 0, ROWS - 1)
    pairs = []
    for n, (out, y) in enumerate(((row_near, near), (row_far, ROWS - 1 - near))):
        pairs += [
            (base_hbm.at[y], base.at[n]),
            (motion_hbm.at[:, y], out.at[pl.ds(0, 3)]),
            (thermal_hbm.at[y], out.at[3]),
        ]
    fetched = start_copies(pairs, sems)
    fetched[0].wait()
    row_near[4] = base[0].astype(F32)
    fetched[3].wait()
    row_far[4] = base[1].astype(F32)
    for n in (1, 2, 4, 5):
        fetched[n].wait()


def layers_kernel(motion, thermal, base, layer_near, layer_far):
    is_odd = odd("gz")
    for y in range(ROWS):
        for c in range(5):
            value = base[y].astype(F32) if c == 4 else thermal[y] if c == 3 else motion[c, y]
            first, last = value[:1], value[LAYERS - 1:]
            layer_near[c, y:y + 1, :] = jnp.where(is_odd, first, last)
            layer_far[c, y:y + 1, :] = jnp.where(is_odd, last, first)


def inner_kernel(motion, thermal, flow, base, moved, row_factors, layer_factors):
    size_x = motion.shape[-1]
    row = lax.broadcasted_iota(jnp.int32, (LAYERS, size_x), 0)
    top = row == LAYERS - 1
    bottom = row == 0

    def field(c, y):
        if c < 3:
            return motion[c, y]
        if c == 3:
            return thermal[y]
        return base[y].astype(F32)

    def neighbours(c, y):
        centre = field(c, y)
        y_plus = field(c, y + 1) if y < ROWS - 1 else None
        y_minus = field(c, y - 1) if y > 0 else None
        z_plus = jnp.where(top, 0.0, pltpu.roll(centre, LAYERS - 1, 0))
        z_minus = jnp.where(bottom, 0.0, pltpu.roll(centre, 1, 0))
        x_plus = pltpu.roll(centre, size_x - 1, 1)
        x_minus = pltpu.roll(centre, 1, 1)
        return centre, x_plus, x_minus, y_plus, y_minus, z_plus, z_minus

    for y in range(ROWS):
        weights = []
        for c in range(3):
            speed = flow[c, y].astype(F32) * 0.1
            weights += [0.02 + speed, 0.02 - speed]
        _, hx, gx, hy, gy, hz, gz = neighbours(4, y)
        slope_y = -gy if hy is None else hy if gy is None else hy - gy
        slopes = (hx - gx, slope_y, hz - gz)
        heat = thermal[y] * 0.1
        if y == 0:
            row_factors[0] = weights[3]
            row_factors[1] = -heat
        if y == ROWS - 1:
            row_factors[2] = weights[2]
            row_factors[3] = heat
        layer_factors[0, y:y + 1, :] = weights[5][:1]
        layer_factors[1, y:y + 1, :] = -heat[:1]
        layer_factors[2, y:y + 1, :] = weights[4][LAYERS - 1:]
        layer_factors[3, y:y + 1, :] = heat[LAYERS - 1:]
        for c in range(4):
            parts = neighbours(c, y)
            value = parts[0] * 0.88
            for weight, part in zip(weights, parts[1:]):
                if part is not None:
                    value = value + weight * part
            moved[c, y] = value + (heat * slopes[c] if c < 3 else 0.2 * motion[2, y])


def source_kernel(
    moved, row_factors, layer_factors, layer_far, layer_near, row_far, row_near,
    fourth_h, fourth_t, even_h, even_t, odd_h, odd_t,
    provisional, thermal_hbm, message, thermal, source, lines, row_p, layer_p, sems
):
    size_x = moved.shape[-1]
    row = lax.broadcasted_iota(jnp.int32, (8, size_x), 0)
    top = lax.broadcasted_iota(jnp.int32, (LAYERS, size_x), 0) == LAYERS - 1
    odd_y, odd_z = odd("gy"), odd("gz")
    y_low = [jnp.where(odd_y, row_near[c], row_far[c]) for c in range(5)]
    y_high = [jnp.where(odd_y, row_far[c], row_near[c]) for c in range(5)]
    z_low = [jnp.where(odd_z, layer_near[c], layer_far[c]) for c in range(5)]
    z_high = [jnp.where(odd_z, layer_far[c], layer_near[c]) for c in range(5)]
    lows = [layer_factors[0] * z_low[c] for c in range(4)]
    highs = [layer_factors[2] * z_high[c] for c in range(4)]
    lows[2] = lows[2] + layer_factors[1] * z_low[4]
    highs[2] = highs[2] + layer_factors[3] * z_high[4]
    carried = None
    for y in range(ROWS):
        for c in range(4):
            value = moved[c, y]
            if y == 0:
                value = value + row_factors[0] * y_low[c]
                if c == 1:
                    value = value + row_factors[1] * y_low[4]
            if y == ROWS - 1:
                value = value + row_factors[2] * y_high[c]
                if c == 1:
                    value = value + row_factors[3] * y_high[4]
            out = provisional.at[c, y] if c < 3 else thermal.at[y]
            out[:8] = value[:8] + jnp.where(row == 0, lows[c][y:y + 1], 0.0)
            out[8:] = value[8:] + jnp.where(row == 7, highs[c][y:y + 1], 0.0)
        p0, p1, p2 = (provisional[c, y] for c in range(3))
        if y == 0:
            keep(row_p, 0, p1)
        else:
            keep(source, (y - 1) * LAYERS, carried + p1)
        keep(layer_p, y, p2[0:1, :])
        above = jnp.where(top, 0.0, pltpu.roll(p2, LAYERS - 1, 0))
        carried = (pltpu.roll(p0, size_x - 1, 1) - p0) - p1 + (above - p2)
    keep(source, (ROWS - 1) * LAYERS, carried)
    stored = start_copies(((thermal, thermal_hbm),), sems)

    for b in range(size_x // 128):
        lanes = pl.ds(b * 128, 128)
        for j in range(4):
            for q in range(QUADS):
                lines[pl.ds(j * PIECE + q * 8, 8), lanes] = source[b, pl.ds(4 * q + j, ROWS, stride=LAYERS), :]
            lines[pl.ds(j * PIECE + 32, 4), lanes] = row_p[b, pl.ds(j, 4, stride=4), :]
            lines[pl.ds(j * PIECE + 36, 2), lanes] = layer_p[b, pl.ds(j, 2, stride=4), :]
            lines[pl.ds(j * PIECE + 38, 2), lanes] = jnp.zeros((2, 128), F32)
    near = lines[:, : size_x // 2]
    far = lines[:, size_x // 2:]
    both = near + far
    left, right = both[:, : size_x // 4], both[:, size_x // 4:]
    turns = (
        (left + right, fourth_h, fourth_t),
        (left - right, even_h, even_t),
        (near - far, odd_h, odd_t),
    )
    at = 0
    for values, head, tail in turns:
        waves = product(values, head[...], tail[...], dot)
        for block in range(waves.shape[1] // 128):
            a = [waves[j * PIECE:(j + 1) * PIECE, block * 128:(block + 1) * 128] for j in range(4)]
            for i, piece in enumerate(swap_groups(a)):
                message[at + i] = piece
            at += 4
    for copy in stored:
        copy.wait()


def span_product(table, values):
    size_y = values.shape[0]
    wide = jnp.concatenate([table[pl.ds(n * size_y, size_y), :] for n in range(size_y // 128)], 1)
    left = split(wide)
    right = split(values)
    both = dot(jnp.concatenate(left, 0), right[0])
    return both[:size_y] + (both[size_y:] + dot(left[0], right[1]))


def wall_factors(lam, slab, slabs):
    square = lam * lam
    powers = [jnp.ones_like(lam), square]
    for m in range(2, LAYERS + 1):
        powers.append(powers[m // 2] * powers[m - m // 2])
    step = powers[LAYERS]

    def raised(count):
        value = lam
        factor = step
        for bit in range((slabs - 1).bit_length()):
            value = jnp.where((count // (1 << bit)) % 2 == 1, value * factor, value)
            factor = factor * factor
        return value

    low = raised(slab)
    high = raised(slabs - 1 - slab)
    below = low * (1.0 / square)
    floor = [1.0 + jnp.where(slab == 0, lam, below)] + [1.0 + low * powers[l] for l in range(LAYERS)]
    ceiling = [1.0 + high * powers[LAYERS - 1 - l] for l in range(-1, LAYERS)]
    return floor, ceiling, powers


def down_kernel(received, table, spectral, handed):
    sources = received.shape[0]
    size_y = sources * ROWS
    slabs = handed.shape[0]
    size_x = sources * WAVES
    slab = lax.axis_index("gz")
    row = lax.broadcasted_iota(jnp.int32, (sources, 8, 128), 1)
    group = lane_group((sources, 8, 128))
    extra = received[:, 8 * QUADS:, :]
    onward = jnp.concatenate([extra[1:], extra[:1]], 0)
    columns = []
    for q in range(QUADS):
        more = jnp.broadcast_to(onward[:, q:q + 1, :], (sources, 8, 128))
        values = received[:, 8 * q:8 * q + 8, :] + jnp.where(row == ROWS - 1, more, 0.0)
        columns.append(values.reshape(size_y, 128))
    first = jnp.broadcast_to(extra[:, 4:5, :], (sources, 8, 128))
    second = jnp.broadcast_to(extra[:, 5:6, :], (sources, 8, 128))
    layer = jnp.where(row < 4, first, second)
    layer = jnp.where((row % 4 == group) & (slab > 0), layer, 0.0)
    columns.append(layer.reshape(size_y, 128))
    waves = span_product(table, jnp.concatenate(columns, 1))

    last = waves[:, 128 * QUADS:]
    last = last + pltpu.roll(last, 64, 1)
    last = (last + pltpu.roll(last, 32, 1)).reshape(size_y // 32, 4, 8, 128)
    modes = size_y // 4
    mode_group = lane_group((modes, 128))
    pick = [last[:, i].reshape(modes, 128) for i in range(4)]
    layers = [
        jnp.where(
            mode_group < 2,
            jnp.where(mode_group == 0, pick[0], pick[1]),
            jnp.where(mode_group == 2, pick[2], pick[3]),
        )
    ]
    for q in range(QUADS):
        block = waves[:, 128 * q:128 * (q + 1)].reshape(size_y // 32, 4, 8, 128)
        layers += swap_groups([block[:, i].reshape(modes, 128) for i in range(4)])
    modes = size_y // 4
    line_y = table[pl.ds(2 * size_y, modes), :]
    a = table[pl.ds(2 * size_y + modes + lax.axis_index("gy"), 1), :] + line_y
    sinh = jnp.sqrt(a * (1.0 + 0.25 * a))
    lam = 1.0 / (1.0 + 0.5 * a + sinh)
    floor, ceiling, powers = wall_factors(lam, slab, slabs)
    spectral[LAYERS + 1] = lam
    whole = powers[LAYERS]
    for _ in range((slabs - 1).bit_length()):
        whole = whole * whole
    zero = a == 0.0
    weight = (-1.0 / (size_x * size_y)) / jnp.where(zero, 1.0, 2.0 * sinh * (1.0 - whole))
    spectral[LAYERS + 2] = jnp.where(zero, 0.0, weight)
    upward = jnp.zeros_like(lam)
    downward = jnp.zeros_like(lam)
    for l in range(LAYERS + 1):
        spectral[l] = layers[l]
        upward = lam * upward + floor[l] * layers[l]
        m = LAYERS - l
        downward = lam * downward + ceiling[m] * layers[m]
    for d in range(slabs):
        handed[d] = jnp.where(d > slab, upward, downward)


def up_kernel(spectral, handed, table, message):
    sources = message.shape[0]
    size_y = sources * ROWS
    slabs = handed.shape[0]
    size_x = sources * WAVES
    size_z = slabs * LAYERS
    slab = lax.axis_index("gz")
    lam = spectral[LAYERS + 1]
    weight = spectral[LAYERS + 2]
    floor, ceiling, powers = wall_factors(lam, slab, slabs)
    scale = 1.0 / (size_x * size_y)
    reach = powers[LAYERS // 2]
    upward = jnp.zeros_like(lam)
    downward = jnp.zeros_like(lam)
    for d in range(slabs - 1):
        upward = jnp.where(d < slab, reach * upward + handed[d], upward)
        e = slabs - 1 - d
        downward = jnp.where(e > slab, reach * downward + handed[e], downward)
    below = []
    for l in range(LAYERS + 1):
        upward = (lam * upward if l else upward) + floor[l] * spectral[l]
        below.append(upward)
    pressure = [None] * (LAYERS + 1)
    for l in reversed(range(LAYERS + 1)):
        pressure[l] = weight * (ceiling[l] * below[l] + floor[l] * downward)
        if l == LAYERS:
            mean = (0.5 / size_z) * (below[l][:8] + downward[:8])
        downward = lam * (downward + ceiling[l] * spectral[l])
    modes = size_y // 4
    flat = jnp.zeros((8, 128), F32)
    first_zero = weight[:8] == 0.0
    for l in range(LAYERS + 1):
        if l:
            count = (slab * LAYERS + (l - 1)).astype(F32)
            flat = flat + (0.5 * below[l - 1][:8] - count * mean)
        pressure[l] = jnp.concatenate(
            [jnp.where(first_zero, flat * scale, pressure[l][:8]), pressure[l][8:]], 0
        )

    columns = []
    tall = (size_y // 32, 1, 8, 128)
    for q in range(QUADS):
        block = swap_groups(pressure[1 + 4 * q:5 + 4 * q])
        columns.append(jnp.concatenate([b.reshape(tall) for b in block], 1).reshape(size_y, 128))
    mode_group = lane_group((modes, 128))
    spread = []
    for i in range(4):
        part = jnp.where(mode_group == i, pressure[0], 0.0)
        part = part + pltpu.roll(part, 64, 1)
        spread.append((part + pltpu.roll(part, 32, 1)).reshape(tall))
    columns.append(jnp.concatenate(spread, 1).reshape(size_y, 128))
    values = span_product(table, jnp.concatenate(columns, 1))

    row = lax.broadcasted_iota(jnp.int32, (sources, 8, 128), 1)
    group = lane_group((sources, 8, 128))
    extra = jnp.zeros((sources, 8, 128), F32)
    for q in range(QUADS):
        block = values[:, 128 * q:128 * (q + 1)].reshape(sources, 8, 128)
        message[:, 8 * q:8 * q + 8, :] = block
        edge = jnp.concatenate([block[-1:], block[:-1]], 0)[:, ROWS - 1:ROWS, :]
        extra = jnp.where(row == q, jnp.broadcast_to(edge, extra.shape), extra)
    layer = values[:, 128 * QUADS:].reshape(sources, 8, 128)
    layer = jnp.where(row % 4 == group, layer, 0.0)
    layer = layer + pltpu.roll(layer, 7, 1)
    layer = layer + pltpu.roll(layer, 6, 1)
    extra = jnp.where(row == 4, jnp.broadcast_to(layer[:, 0:1, :], extra.shape), extra)
    extra = jnp.where(row == 5, jnp.broadcast_to(layer[:, 4:5, :], extra.shape), extra)
    message[:, 8 * QUADS:, :] = extra


def gradient_kernel(
    received, fourth_h, fourth_t, even_h, even_t, odd_h, odd_t, provisional, motion_hbm,
    motion, lines, pressure, row_p, layer_p, sems,
):
    size_x = provisional.shape[-1]
    for block in range(size_x // 128):
        for j, piece in enumerate(swap_groups([received[4 * block + i] for i in range(4)])):
            lines[j * PIECE:(j + 1) * PIECE, block * 128:(block + 1) * 128] = piece
    fourths = product(lines[:, : size_x // 4], fourth_h[...], fourth_t[...], dot)
    others = product(lines[:, size_x // 4: size_x // 2], even_h[...], even_t[...], dot_nt)
    evens = jnp.concatenate([fourths + others, fourths - others], 1)
    odds = product(lines[:, size_x // 2:], odd_h[...], odd_t[...], dot_nt)
    lines[:, : size_x // 2] = evens + odds
    lines[:, size_x // 2:] = evens - odds
    for b in range(size_x // 128):
        lanes = pl.ds(b * 128, 128)
        for j in range(4):
            for q in range(QUADS):
                pressure[b, pl.ds(4 * q + j, ROWS, stride=LAYERS), :] = lines[pl.ds(j * PIECE + q * 8, 8), lanes]
            row_p[b, pl.ds(j, 4, stride=4), :] = lines[pl.ds(j * PIECE + 32, 4), lanes]
            layer_p[b, pl.ds(j, 2, stride=4), :] = lines[pl.ds(j * PIECE + 36, 2), lanes]
    stored = []
    bottom = lax.broadcasted_iota(jnp.int32, (LAYERS, size_x), 0) == 0
    for y in range(ROWS):
        p = kept(pressure, y * LAYERS, LAYERS)
        before = kept(row_p, 0, LAYERS) if y == 0 else kept(pressure, (y - 1) * LAYERS, LAYERS)
        below = jnp.where(bottom, kept(layer_p, y, 1), pltpu.roll(p, 1, 0))
        slope_z = jnp.where(bottom & (lax.axis_index("gz") == 0), 0.0, p - below)
        motion[0, y] = provisional[0, y] - (p - pltpu.roll(p, 1, 1))
        motion[1, y] = provisional[1, y] - (p - before)
        motion[2, y] = provisional[2, y] - slope_z
        copy = pltpu.make_async_copy(motion.at[:, pl.ds(y, 1)], motion_hbm.at[:, pl.ds(y, 1)], sems.at[y])
        copy.start()
        stored.append(copy)
    for copy in stored:
        copy.wait()


def swapped(value, axis, first, periodic):
    size = lax.axis_size(axis)
    pairs = []
    for i in range(first, size, 2):
        if periodic or i + 1 < size:
            pairs += [(i, (i + 1) % size), ((i + 1) % size, i)]
    return lax.ppermute(value, axis, pairs)


def exchanged(pieces, axis):
    return lax.all_to_all(pieces, axis, split_axis=0, concat_axis=0, tiled=True)


def shape_of(*shape):
    return jax.ShapeDtypeStruct(shape, F32)


def on_device(dual_motion, dual_thermal, flow, base):
    size_x = dual_thermal.shape[-1]
    groups_y = lax.axis_size("gy")
    groups_z = lax.axis_size("gz")
    waves, table = tables(size_x, ROWS * groups_y)
    waves = tuple(map(jnp.asarray, waves))
    modes = ROWS * groups_y // 4
    blocks = size_x // 128

    def hbm(value):
        return pltpu.with_memory_space_constraint(value, pltpu.HBM)

    def params(mib):
        return pltpu.CompilerParams(vmem_limit_bytes=mib << 20)

    table = jnp.asarray(table)
    rows = shape_of(5, LAYERS, size_x)
    layers = shape_of(5, ROWS, size_x)
    motion_shape = (3, ROWS, LAYERS, size_x)
    thermal_shape = motion_shape[1:]
    message_shape = (groups_y, PIECE, 128)
    row_near, row_far = pl.pallas_call(
        rows_kernel,
        out_shape=(rows, rows),
        in_specs=[HBM] * 3,
        out_specs=(VMEM,) * 2,
        scratch_shapes=[pltpu.VMEM((2, LAYERS, size_x), BF16), pltpu.SemaphoreType.DMA((6,))],
        compiler_params=params(16),
        name="rows",
    )(*map(hbm, (dual_motion, dual_thermal, base)))
    layer_near, layer_far = pl.pallas_call(
        layers_kernel,
        out_shape=(layers, layers),
        in_specs=[VMEM] * 3,
        out_specs=(VMEM,) * 2,
        compiler_params=params(16),
        name="layers",
    )(dual_motion, dual_thermal, base)
    row_near = swapped(row_near, "gy", 0, True)
    row_far = swapped(row_far, "gy", 1, True)
    layer_near = swapped(layer_near, "gz", 0, False)
    layer_far = swapped(layer_far, "gz", 1, False)
    moved, row_factors, layer_factors = pl.pallas_call(
        inner_kernel,
        out_shape=(
            shape_of(4, *thermal_shape),
            shape_of(4, LAYERS, size_x),
            shape_of(4, ROWS, size_x),
        ),
        in_specs=[VMEM] * 4,
        out_specs=(VMEM,) * 3,
        compiler_params=params(16),
        cost_estimate=pl.CostEstimate(
            flops=80 * ROWS * LAYERS * size_x, transcendentals=0, bytes_accessed=10 << 20
        ),
        name="inner",
    )(dual_motion, dual_thermal, flow, base)
    provisional, thermal_out, message = pl.pallas_call(
        source_kernel,
        out_shape=(
            shape_of(*motion_shape),
            pltpu.HBM(thermal_shape, F32),
            shape_of(*message_shape),
        ),
        in_specs=[VMEM] * 13,
        out_specs=(VMEM, HBM, VMEM),
        scratch_shapes=[
            pltpu.VMEM(thermal_shape, F32),
            pltpu.VMEM((blocks, ROWS * LAYERS, 128), F32),
            pltpu.VMEM((4 * PIECE, size_x), F32),
            pltpu.VMEM((blocks, LAYERS, 128), F32),
            pltpu.VMEM((blocks, ROWS, 128), F32),
            pltpu.SemaphoreType.DMA((1,)),
        ],
        compiler_params=params(24),
        name="source",
    )(
        moved, row_factors, layer_factors, layer_far, layer_near, row_far, row_near,
        *waves,
    )
    received = exchanged(message, "gy")
    spectral, handed = pl.pallas_call(
        down_kernel,
        out_shape=(shape_of(LAYERS + 3, modes, 128), shape_of(groups_z, modes, 128)),
        in_specs=[VMEM] * 2,
        out_specs=(VMEM,) * 2,
        compiler_params=params(16),
        name="down",
    )(received, table)
    handed = exchanged(handed, "gz")
    message = pl.pallas_call(
        up_kernel,
        out_shape=shape_of(*message_shape),
        in_specs=[VMEM] * 3,
        out_specs=VMEM,
        compiler_params=params(16),
        name="up",
    )(spectral, handed, table)
    received = exchanged(message, "gy")
    motion = pl.pallas_call(
        gradient_kernel,
        out_shape=pltpu.HBM(motion_shape, F32),
        in_specs=[VMEM] * 8,
        out_specs=HBM,
        scratch_shapes=[
            pltpu.VMEM(motion_shape, F32),
            pltpu.VMEM((4 * PIECE, size_x), F32),
            pltpu.VMEM((blocks, ROWS * LAYERS, 128), F32),
            pltpu.VMEM((blocks, LAYERS, 128), F32),
            pltpu.VMEM((blocks, ROWS, 128), F32),
            pltpu.SemaphoreType.DMA((ROWS,)),
        ],
        compiler_params=params(24),
        name="gradient",
    )(received, *waves, provisional)
    return motion, thermal_out


def solution(mesh):
    split_y = P(None, "gy", "gz", None)
    split_flat = P("gy", "gz", None)
    return jax.shard_map(
        on_device,
        mesh=mesh,
        in_specs=(split_y, split_flat, split_y, split_flat),
        out_specs=(split_y, split_flat),
        check_vma=False,
    )
```

```python
import functools

import jax
import jax.numpy as jnp
import ml_dtypes
import numpy as np
from jax import lax
from jax.experimental import pallas as pl
from jax.experimental.pallas import tpu as pltpu
from jax.sharding import PartitionSpec as P

F32 = jnp.float32
BF16 = jnp.bfloat16
ROWS = 8
LAYERS = 16
WAVES = 32
QUADS = LAYERS // 4
PIECE = 8 * (QUADS + 1)
VMEM = pl.BlockSpec(memory_space=pltpu.VMEM)
HBM = pl.BlockSpec(memory_space=pltpu.HBM)


def two_parts(table):
    head = table.astype(ml_dtypes.bfloat16)
    return head, (table - head.astype(np.float64)).astype(ml_dtypes.bfloat16)


def cas(phases, length):
    angles = (phases % length) * (2.0 * np.pi / length)
    return np.cos(angles) + np.sin(angles)


@functools.lru_cache(None)
def tables(size_x, size_y):
    half = np.arange(size_x // 2)
    quarter = np.arange(size_x // 4)
    fourth = two_parts(cas(quarter[:, None] * quarter[None, :], size_x // 4))
    even = two_parts(cas(quarter[:, None] * (2 * quarter[None, :] + 1), size_x // 2))
    odd = two_parts(cas(half[:, None] * (2 * half[None, :] + 1), size_x))
    full = np.arange(size_y)
    span = cas(full[:, None] * full[None, :], size_y)
    waves = np.concatenate([4 * quarter, 4 * quarter + 2, 2 * half + 1])
    line_x = 4.0 * np.sin(np.pi * waves / size_x) ** 2
    line_x = np.tile(line_x.reshape(-1, WAVES), (1, 128 // WAVES))
    row = np.arange(size_y // 4)[:, None]
    lane = np.arange(128)[None, :]
    wave_y = 32 * (row // 8) + 8 * (lane // WAVES) + row % 8
    line_y = 4.0 * np.sin(np.pi * wave_y / size_y) ** 2
    halves = [span[:, n * 128:(n + 1) * 128] for n in range(size_y // 128)]
    return fourth + even + odd, np.concatenate(halves + [line_y, line_x], 0).astype(np.float32)


def split(values):
    head = values.astype(BF16)
    return head, (values - head.astype(F32)).astype(BF16)


def lane_group(shape):
    return lax.broadcasted_iota(jnp.int32, shape, len(shape) - 1) // WAVES


def swap_groups(a):
    axis = a[0].ndim - 1
    group = lane_group(a[0].shape)
    low = group < 2
    even = group % 2 == 0
    b0 = jnp.where(low, a[0], pltpu.roll(a[2], 64, axis))
    b2 = jnp.where(low, pltpu.roll(a[0], 64, axis), a[2])
    b1 = jnp.where(low, a[1], pltpu.roll(a[3], 64, axis))
    b3 = jnp.where(low, pltpu.roll(a[1], 64, axis), a[3])
    return (
        jnp.where(even, b0, pltpu.roll(b1, 32, axis)),
        jnp.where(even, pltpu.roll(b0, 96, axis), b1),
        jnp.where(even, b2, pltpu.roll(b3, 32, axis)),
        jnp.where(even, pltpu.roll(b2, 96, axis), b3),
    )


def dot(a, b):
    return jnp.dot(a, b, preferred_element_type=F32)


def dot_nt(a, b):
    return lax.dot_general(a, b, (((1,), (1,)), ((), ())), preferred_element_type=F32)


def product(values, head, tail, how):
    a, b = split(values)
    both = how(jnp.concatenate([a, b], 0), head)
    count = values.shape[0]
    return both[:count] + (both[count:] + how(a, tail))


def keep(ref, start, values):
    for b in range(ref.shape[0]):
        ref[b, pl.ds(start, values.shape[0]), :] = values[:, b * 128:(b + 1) * 128]


def kept(ref, start, count):
    return jnp.concatenate([ref[b, pl.ds(start, count), :] for b in range(ref.shape[0])], 1)


def start_copies(pairs, sems):
    copies = [pltpu.make_async_copy(a, b, sems.at[n]) for n, (a, b) in enumerate(pairs)]
    for copy in copies:
        copy.start()
    return copies


def odd(axis):
    return lax.axis_index(axis) % 2 == 1


def rows_kernel(motion_hbm, thermal_hbm, base_hbm, row_near, row_far, base, sems):
    near = jnp.where(odd("gy"), 0, ROWS - 1)
    pairs = []
    for n, (out, y) in enumerate(((row_near, near), (row_far, ROWS - 1 - near))):
        pairs += [
            (base_hbm.at[y], base.at[n]),
            (motion_hbm.at[:, y], out.at[pl.ds(0, 3)]),
            (thermal_hbm.at[y], out.at[3]),
        ]
    fetched = start_copies(pairs, sems)
    fetched[0].wait()
    row_near[4] = base[0].astype(F32)
    fetched[3].wait()
    row_far[4] = base[1].astype(F32)
    for n in (1, 2, 4, 5):
        fetched[n].wait()


def layers_kernel(motion, thermal, base, layer_near, layer_far):
    is_odd = odd("gz")
    for y in range(ROWS):
        for c in range(5):
            value = base[y].astype(F32) if c == 4 else thermal[y] if c == 3 else motion[c, y]
            first, last = value[:1], value[LAYERS - 1:]
            layer_near[c, y:y + 1, :] = jnp.where(is_odd, first, last)
            layer_far[c, y:y + 1, :] = jnp.where(is_odd, last, first)


def inner_kernel(motion, thermal, flow, base, moved, row_factors, layer_factors):
    size_x = motion.shape[-1]
    row = lax.broadcasted_iota(jnp.int32, (LAYERS, size_x), 0)
    top = row == LAYERS - 1
    bottom = row == 0

    def field(c, y):
        if c < 3:
            return motion[c, y]
        if c == 3:
            return thermal[y]
        return base[y].astype(F32)

    def neighbours(c, y):
        centre = field(c, y)
        y_plus = field(c, y + 1) if y < ROWS - 1 else None
        y_minus = field(c, y - 1) if y > 0 else None
        z_plus = jnp.where(top, 0.0, pltpu.roll(centre, LAYERS - 1, 0))
        z_minus = jnp.where(bottom, 0.0, pltpu.roll(centre, 1, 0))
        x_plus = pltpu.roll(centre, size_x - 1, 1)
        x_minus = pltpu.roll(centre, 1, 1)
        return centre, x_plus, x_minus, y_plus, y_minus, z_plus, z_minus

    for y in range(ROWS):
        weights = []
        for c in range(3):
            speed = flow[c, y].astype(F32) * 0.1
            weights += [0.02 + speed, 0.02 - speed]
        _, hx, gx, hy, gy, hz, gz = neighbours(4, y)
        slope_y = -gy if hy is None else hy if gy is None else hy - gy
        slopes = (hx - gx, slope_y, hz - gz)
        heat = thermal[y] * 0.1
        if y == 0:
            row_factors[0] = weights[3]
            row_factors[1] = -heat
        if y == ROWS - 1:
            row_factors[2] = weights[2]
            row_factors[3] = heat
        layer_factors[0, y:y + 1, :] = weights[5][:1]
        layer_factors[1, y:y + 1, :] = -heat[:1]
        layer_factors[2, y:y + 1, :] = weights[4][LAYERS - 1:]
        layer_factors[3, y:y + 1, :] = heat[LAYERS - 1:]
        for c in range(4):
            parts = neighbours(c, y)
            value = parts[0] * 0.88
            for weight, part in zip(weights, parts[1:]):
                if part is not None:
                    value = value + weight * part
            moved[c, y] = value + (heat * slopes[c] if c < 3 else 0.2 * motion[2, y])


def source_kernel(
    moved, row_factors, layer_factors, layer_far, layer_near, row_far, row_near,
    fourth_h, fourth_t, even_h, even_t, odd_h, odd_t,
    provisional, thermal_hbm, message, thermal, source, lines, row_p, layer_p, sems
):
    size_x = moved.shape[-1]
    row = lax.broadcasted_iota(jnp.int32, (8, size_x), 0)
    top = lax.broadcasted_iota(jnp.int32, (LAYERS, size_x), 0) == LAYERS - 1
    odd_y, odd_z = odd("gy"), odd("gz")
    y_low = [jnp.where(odd_y, row_near[c], row_far[c]) for c in range(5)]
    y_high = [jnp.where(odd_y, row_far[c], row_near[c]) for c in range(5)]
    z_low = [jnp.where(odd_z, layer_near[c], layer_far[c]) for c in range(5)]
    z_high = [jnp.where(odd_z, layer_far[c], layer_near[c]) for c in range(5)]
    lows = [layer_factors[0] * z_low[c] for c in range(4)]
    highs = [layer_factors[2] * z_high[c] for c in range(4)]
    lows[2] = lows[2] + layer_factors[1] * z_low[4]
    highs[2] = highs[2] + layer_factors[3] * z_high[4]
    carried = None
    for y in range(ROWS):
        for c in range(4):
            value = moved[c, y]
            if y == 0:
                value = value + row_factors[0] * y_low[c]
                if c == 1:
                    value = value + row_factors[1] * y_low[4]
            if y == ROWS - 1:
                value = value + row_factors[2] * y_high[c]
                if c == 1:
                    value = value + row_factors[3] * y_high[4]
            out = provisional.at[c, y] if c < 3 else thermal.at[y]
            out[:8] = value[:8] + jnp.where(row == 0, lows[c][y:y + 1], 0.0)
            out[8:] = value[8:] + jnp.where(row == 7, highs[c][y:y + 1], 0.0)
        p0, p1, p2 = (provisional[c, y] for c in range(3))
        if y == 0:
            keep(row_p, 0, p1)
        else:
            keep(source, (y - 1) * LAYERS, carried + p1)
        keep(layer_p, y, p2[0:1, :])
        above = jnp.where(top, 0.0, pltpu.roll(p2, LAYERS - 1, 0))
        carried = (pltpu.roll(p0, size_x - 1, 1) - p0) - p1 + (above - p2)
    keep(source, (ROWS - 1) * LAYERS, carried)
    stored = start_copies(((thermal, thermal_hbm),), sems)

    for b in range(size_x // 128):
        lanes = pl.ds(b * 128, 128)
        for j in range(4):
            for q in range(QUADS):
                lines[pl.ds(j * PIECE + q * 8, 8), lanes] = source[b, pl.ds(4 * q + j, ROWS, stride=LAYERS), :]
            lines[pl.ds(j * PIECE + 32, 4), lanes] = row_p[b, pl.ds(j, 4, stride=4), :]
            lines[pl.ds(j * PIECE + 36, 2), lanes] = layer_p[b, pl.ds(j, 2, stride=4), :]
            lines[pl.ds(j * PIECE + 38, 2), lanes] = jnp.zeros((2, 128), F32)
    near = lines[:, : size_x // 2]
    far = lines[:, size_x // 2:]
    both = near + far
    left, right = both[:, : size_x // 4], both[:, size_x // 4:]
    turns = (
        (left + right, fourth_h, fourth_t),
        (left - right, even_h, even_t),
        (near - far, odd_h, odd_t),
    )
    at = 0
    for values, head, tail in turns:
        waves = product(values, head[...], tail[...], dot)
        for block in range(waves.shape[1] // 128):
            a = [waves[j * PIECE:(j + 1) * PIECE, block * 128:(block + 1) * 128] for j in range(4)]
            for i, piece in enumerate(swap_groups(a)):
                message[at + i] = piece
            at += 4
    for copy in stored:
        copy.wait()


def span_product(table, values):
    size_y = values.shape[0]
    wide = jnp.concatenate([table[pl.ds(n * size_y, size_y), :] for n in range(size_y // 128)], 1)
    left = split(wide)
    right = split(values)
    both = dot(jnp.concatenate(left, 0), right[0])
    return both[:size_y] + (both[size_y:] + dot(left[0], right[1]))


def wall_factors(lam, slab, slabs):
    square = lam * lam
    powers = [jnp.ones_like(lam), square]
    for m in range(2, LAYERS + 1):
        powers.append(powers[m // 2] * powers[m - m // 2])
    step = powers[LAYERS]

    def raised(count):
        value = lam
        factor = step
        for bit in range((slabs - 1).bit_length()):
            value = jnp.where((count // (1 << bit)) % 2 == 1, value * factor, value)
            factor = factor * factor
        return value

    low = raised(slab)
    high = raised(slabs - 1 - slab)
    below = low * (1.0 / square)
    floor = [1.0 + jnp.where(slab == 0, lam, below)] + [1.0 + low * powers[l] for l in range(LAYERS)]
    ceiling = [1.0 + high * powers[LAYERS - 1 - l] for l in range(-1, LAYERS)]
    return floor, ceiling, powers


def down_kernel(received, table, spectral, handed):
    sources = received.shape[0]
    size_y = sources * ROWS
    slabs = handed.shape[0]
    size_x = sources * WAVES
    slab = lax.axis_index("gz")
    row = lax.broadcasted_iota(jnp.int32, (sources, 8, 128), 1)
    group = lane_group((sources, 8, 128))
    extra = received[:, 8 * QUADS:, :]
    onward = jnp.concatenate([extra[1:], extra[:1]], 0)
    columns = []
    for q in range(QUADS):
        more = jnp.broadcast_to(onward[:, q:q + 1, :], (sources, 8, 128))
        values = received[:, 8 * q:8 * q + 8, :] + jnp.where(row == ROWS - 1, more, 0.0)
        columns.append(values.reshape(size_y, 128))
    first = jnp.broadcast_to(extra[:, 4:5, :], (sources, 8, 128))
    second = jnp.broadcast_to(extra[:, 5:6, :], (sources, 8, 128))
    layer = jnp.where(row < 4, first, second)
    layer = jnp.where((row % 4 == group) & (slab > 0), layer, 0.0)
    columns.append(layer.reshape(size_y, 128))
    waves = span_product(table, jnp.concatenate(columns, 1))

    last = waves[:, 128 * QUADS:]
    last = last + pltpu.roll(last, 64, 1)
    last = (last + pltpu.roll(last, 32, 1)).reshape(size_y // 32, 4, 8, 128)
    modes = size_y // 4
    mode_group = lane_group((modes, 128))
    pick = [last[:, i].reshape(modes, 128) for i in range(4)]
    layers = [
        jnp.where(
            mode_group < 2,
            jnp.where(mode_group == 0, pick[0], pick[1]),
            jnp.where(mode_group == 2, pick[2], pick[3]),
        )
    ]
    for q in range(QUADS):
        block = waves[:, 128 * q:128 * (q + 1)].reshape(size_y // 32, 4, 8, 128)
        layers += swap_groups([block[:, i].reshape(modes, 128) for i in range(4)])
    modes = size_y // 4
    line_y = table[pl.ds(2 * size_y, modes), :]
    a = table[pl.ds(2 * size_y + modes + lax.axis_index("gy"), 1), :] + line_y
    sinh = jnp.sqrt(a * (1.0 + 0.25 * a))
    lam = 1.0 / (1.0 + 0.5 * a + sinh)
    floor, ceiling, powers = wall_factors(lam, slab, slabs)
    spectral[LAYERS + 1] = lam
    whole = powers[LAYERS]
    for _ in range((slabs - 1).bit_length()):
        whole = whole * whole
    zero = a == 0.0
    weight = (-1.0 / (size_x * size_y)) / jnp.where(zero, 1.0, 2.0 * sinh * (1.0 - whole))
    spectral[LAYERS + 2] = jnp.where(zero, 0.0, weight)
    upward = jnp.zeros_like(lam)
    downward = jnp.zeros_like(lam)
    for l in range(LAYERS + 1):
        spectral[l] = layers[l]
        upward = lam * upward + floor[l] * layers[l]
        m = LAYERS - l
        downward = lam * downward + ceiling[m] * layers[m]
    for d in range(slabs):
        handed[d] = jnp.where(d > slab, upward, downward)


def up_kernel(spectral, handed, table, message):
    sources = message.shape[0]
    size_y = sources * ROWS
    slabs = handed.shape[0]
    size_x = sources * WAVES
    size_z = slabs * LAYERS
    slab = lax.axis_index("gz")
    lam = spectral[LAYERS + 1]
    weight = spectral[LAYERS + 2]
    floor, ceiling, powers = wall_factors(lam, slab, slabs)
    scale = 1.0 / (size_x * size_y)
    reach = powers[LAYERS // 2]
    upward = jnp.zeros_like(lam)
    downward = jnp.zeros_like(lam)
    for d in range(slabs - 1):
        upward = jnp.where(d < slab, reach * upward + handed[d], upward)
        e = slabs - 1 - d
        downward = jnp.where(e > slab, reach * downward + handed[e], downward)
    below = []
    for l in range(LAYERS + 1):
        upward = (lam * upward if l else upward) + floor[l] * spectral[l]
        below.append(upward)
    pressure = [None] * (LAYERS + 1)
    for l in reversed(range(LAYERS + 1)):
        pressure[l] = weight * (ceiling[l] * below[l] + floor[l] * downward)
        if l == LAYERS:
            mean = (0.5 / size_z) * (below[l][:8] + downward[:8])
        downward = lam * (downward + ceiling[l] * spectral[l])
    modes = size_y // 4
    flat = jnp.zeros((8, 128), F32)
    first_zero = weight[:8] == 0.0
    for l in range(LAYERS + 1):
        if l:
            count = (slab * LAYERS + (l - 1)).astype(F32)
            flat = flat + (0.5 * below[l - 1][:8] - count * mean)
        pressure[l] = jnp.concatenate(
            [jnp.where(first_zero, flat * scale, pressure[l][:8]), pressure[l][8:]], 0
        )

    columns = []
    tall = (size_y // 32, 1, 8, 128)
    for q in range(QUADS):
        block = swap_groups(pressure[1 + 4 * q:5 + 4 * q])
        columns.append(jnp.concatenate([b.reshape(tall) for b in block], 1).reshape(size_y, 128))
    mode_group = lane_group((modes, 128))
    spread = []
    for i in range(4):
        part = jnp.where(mode_group == i, pressure[0], 0.0)
        part = part + pltpu.roll(part, 64, 1)
        spread.append((part + pltpu.roll(part, 32, 1)).reshape(tall))
    columns.append(jnp.concatenate(spread, 1).reshape(size_y, 128))
    values = span_product(table, jnp.concatenate(columns, 1))

    row = lax.broadcasted_iota(jnp.int32, (sources, 8, 128), 1)
    group = lane_group((sources, 8, 128))
    extra = jnp.zeros((sources, 8, 128), F32)
    for q in range(QUADS):
        block = values[:, 128 * q:128 * (q + 1)].reshape(sources, 8, 128)
        message[:, 8 * q:8 * q + 8, :] = block
        edge = jnp.concatenate([block[-1:], block[:-1]], 0)[:, ROWS - 1:ROWS, :]
        extra = jnp.where(row == q, jnp.broadcast_to(edge, extra.shape), extra)
    layer = values[:, 128 * QUADS:].reshape(sources, 8, 128)
    layer = jnp.where(row % 4 == group, layer, 0.0)
    layer = layer + pltpu.roll(layer, 7, 1)
    layer = layer + pltpu.roll(layer, 6, 1)
    extra = jnp.where(row == 4, jnp.broadcast_to(layer[:, 0:1, :], extra.shape), extra)
    extra = jnp.where(row == 5, jnp.broadcast_to(layer[:, 4:5, :], extra.shape), extra)
    message[:, 8 * QUADS:, :] = extra


def gradient_kernel(
    received, fourth_h, fourth_t, even_h, even_t, odd_h, odd_t, provisional, motion_hbm,
    motion, lines, pressure, row_p, layer_p, sems,
):
    size_x = provisional.shape[-1]
    for block in range(size_x // 128):
        for j, piece in enumerate(swap_groups([received[4 * block + i] for i in range(4)])):
            lines[j * PIECE:(j + 1) * PIECE, block * 128:(block + 1) * 128] = piece
    fourths = product(lines[:, : size_x // 4], fourth_h[...], fourth_t[...], dot)
    others = product(lines[:, size_x // 4: size_x // 2], even_h[...], even_t[...], dot_nt)
    evens = jnp.concatenate([fourths + others, fourths - others], 1)
    odds = product(lines[:, size_x // 2:], odd_h[...], odd_t[...], dot_nt)
    half = size_x // 256
    for b in range(2 * half):
        lanes = slice(b % half * 128, (b % half + 1) * 128)
        values = evens[:, lanes] + odds[:, lanes] if b < half else evens[:, lanes] - odds[:, lanes]
        for j in range(4):
            for q in range(QUADS):
                at = j * PIECE + q * 8
                pressure[b, pl.ds(4 * q + j, ROWS, stride=LAYERS), :] = values[at:at + 8]
            at = j * PIECE + 8 * QUADS
            row_p[b, pl.ds(j, 4, stride=4), :] = values[at:at + 4]
            layer_p[b, pl.ds(j, 2, stride=4), :] = values[at + 4:at + 6]
    stored = []
    bottom = lax.broadcasted_iota(jnp.int32, (LAYERS, size_x), 0) == 0
    for y in range(ROWS):
        p = kept(pressure, y * LAYERS, LAYERS)
        before = kept(row_p, 0, LAYERS) if y == 0 else kept(pressure, (y - 1) * LAYERS, LAYERS)
        below = jnp.where(bottom, kept(layer_p, y, 1), pltpu.roll(p, 1, 0))
        slope_z = jnp.where(bottom & (lax.axis_index("gz") == 0), 0.0, p - below)
        motion[0, y] = provisional[0, y] - (p - pltpu.roll(p, 1, 1))
        motion[1, y] = provisional[1, y] - (p - before)
        motion[2, y] = provisional[2, y] - slope_z
        copy = pltpu.make_async_copy(motion.at[:, pl.ds(y, 1)], motion_hbm.at[:, pl.ds(y, 1)], sems.at[y])
        copy.start()
        stored.append(copy)
    for copy in stored:
        copy.wait()


def swapped(value, axis, first, periodic):
    size = lax.axis_size(axis)
    pairs = []
    for i in range(first, size, 2):
        if periodic or i + 1 < size:
            pairs += [(i, (i + 1) % size), ((i + 1) % size, i)]
    return lax.ppermute(value, axis, pairs)


def exchanged(pieces, axis):
    return lax.all_to_all(pieces, axis, split_axis=0, concat_axis=0, tiled=True)


def shape_of(*shape):
    return jax.ShapeDtypeStruct(shape, F32)


def on_device(dual_motion, dual_thermal, flow, base):
    size_x = dual_thermal.shape[-1]
    groups_y = lax.axis_size("gy")
    groups_z = lax.axis_size("gz")
    waves, table = tables(size_x, ROWS * groups_y)
    waves = tuple(map(jnp.asarray, waves))
    modes = ROWS * groups_y // 4
    blocks = size_x // 128

    def hbm(value):
        return pltpu.with_memory_space_constraint(value, pltpu.HBM)

    def params(mib):
        return pltpu.CompilerParams(vmem_limit_bytes=mib << 20)

    table = jnp.asarray(table)
    rows = shape_of(5, LAYERS, size_x)
    layers = shape_of(5, ROWS, size_x)
    motion_shape = (3, ROWS, LAYERS, size_x)
    thermal_shape = motion_shape[1:]
    message_shape = (groups_y, PIECE, 128)
    row_near, row_far = pl.pallas_call(
        rows_kernel,
        out_shape=(rows, rows),
        in_specs=[HBM] * 3,
        out_specs=(VMEM,) * 2,
        scratch_shapes=[pltpu.VMEM((2, LAYERS, size_x), BF16), pltpu.SemaphoreType.DMA((6,))],
        compiler_params=params(16),
        name="rows",
    )(*map(hbm, (dual_motion, dual_thermal, base)))
    layer_near, layer_far = pl.pallas_call(
        layers_kernel,
        out_shape=(layers, layers),
        in_specs=[VMEM] * 3,
        out_specs=(VMEM,) * 2,
        compiler_params=params(16),
        name="layers",
    )(dual_motion, dual_thermal, base)
    row_near = swapped(row_near, "gy", 0, True)
    row_far = swapped(row_far, "gy", 1, True)
    layer_near = swapped(layer_near, "gz", 0, False)
    layer_far = swapped(layer_far, "gz", 1, False)
    moved, row_factors, layer_factors = pl.pallas_call(
        inner_kernel,
        out_shape=(
            shape_of(4, *thermal_shape),
            shape_of(4, LAYERS, size_x),
            shape_of(4, ROWS, size_x),
        ),
        in_specs=[VMEM] * 4,
        out_specs=(VMEM,) * 3,
        compiler_params=params(16),
        cost_estimate=pl.CostEstimate(
            flops=80 * ROWS * LAYERS * size_x, transcendentals=0, bytes_accessed=10 << 20
        ),
        name="inner",
    )(dual_motion, dual_thermal, flow, base)
    provisional, thermal_out, message = pl.pallas_call(
        source_kernel,
        out_shape=(
            shape_of(*motion_shape),
            pltpu.HBM(thermal_shape, F32),
            shape_of(*message_shape),
        ),
        in_specs=[VMEM] * 13,
        out_specs=(VMEM, HBM, VMEM),
        scratch_shapes=[
            pltpu.VMEM(thermal_shape, F32),
            pltpu.VMEM((blocks, ROWS * LAYERS, 128), F32),
            pltpu.VMEM((4 * PIECE, size_x), F32),
            pltpu.VMEM((blocks, LAYERS, 128), F32),
            pltpu.VMEM((blocks, ROWS, 128), F32),
            pltpu.SemaphoreType.DMA((1,)),
        ],
        compiler_params=params(24),
        name="source",
    )(
        moved, row_factors, layer_factors, layer_far, layer_near, row_far, row_near,
        *waves,
    )
    received = exchanged(message, "gy")
    spectral, handed = pl.pallas_call(
        down_kernel,
        out_shape=(shape_of(LAYERS + 3, modes, 128), shape_of(groups_z, modes, 128)),
        in_specs=[VMEM] * 2,
        out_specs=(VMEM,) * 2,
        compiler_params=params(16),
        name="down",
    )(received, table)
    handed = exchanged(handed, "gz")
    message = pl.pallas_call(
        up_kernel,
        out_shape=shape_of(*message_shape),
        in_specs=[VMEM] * 3,
        out_specs=VMEM,
        compiler_params=params(16),
        name="up",
    )(spectral, handed, table)
    received = exchanged(message, "gy")
    motion = pl.pallas_call(
        gradient_kernel,
        out_shape=pltpu.HBM(motion_shape, F32),
        in_specs=[VMEM] * 8,
        out_specs=HBM,
        scratch_shapes=[
            pltpu.VMEM(motion_shape, F32),
            pltpu.VMEM((4 * PIECE, size_x), F32),
            pltpu.VMEM((blocks, ROWS * LAYERS, 128), F32),
            pltpu.VMEM((blocks, LAYERS, 128), F32),
            pltpu.VMEM((blocks, ROWS, 128), F32),
            pltpu.SemaphoreType.DMA((ROWS,)),
        ],
        compiler_params=params(24),
        name="gradient",
    )(received, *waves, provisional)
    return motion, thermal_out


def solution(mesh):
    split_y = P(None, "gy", "gz", None)
    split_flat = P("gy", "gz", None)
    return jax.shard_map(
        on_device,
        mesh=mesh,
        in_specs=(split_y, split_flat, split_y, split_flat),
        out_specs=(split_y, split_flat),
        check_vma=False,
    )
```
